256 devices in a mesh: tm: 8 (over z), gx: 8 (over y, core), gy: 4 (over x).
Axes of the slice: x: 4, y: 4, z: 8, core: 2. Of those that a mesh axis runs over, the one named last changes fastest.
Arguments:
- segment_opening_values: float32 [8, 4, 96, 64, 128], P('tm', None, 'gx', 'gy'), may hold values from -6 to 6
- cell_material_label: int32 [96, 64, 128], P('gx', 'gy'), may hold values from 0 to 5
- material_rigidity: float32 [6], replicated, may hold values from 0.3 to 3
- dilation_mismatch: float32 [6], replicated, may hold values from -1 to 1
- heat_swings_array: float32 [8, 2], P('tm'), may hold values from 0.5 to 4
- prony_coefficients: float32 [3], replicated, may hold values from 0.2 to 2
- prony_decay_times: float32 [3], replicated, may hold values from 0.7 to 48
Outputs:
- end_state: float32 [8, 4, 96, 64, 128], P('tm', None, 'gx', 'gy')
The draws below stay inside these ranges and needn't reach their ends.
All inputs are finite; a program needn't handle non-finite values.
Results may differ from the reference program's by a relative error of at most 0.0001.
Values sent between devices are 32-bit elements; how exact they have to be, the bound alone decides.
No kernel may reach another device: no remote copies, remote signals or barrier semaphores. Data moves between devices by JAX's collectives and lax.ppermute only.
A program may use at most 64 MiB of HBM per device.

```python
import math
import jax
import jax.numpy as jnp

PRONY = 3
REGIONS = 6
PARTITION_PACES = 2
SHARP_SOLVER_ITER = 3
LOOSE_SOLVER_ITER = 2
STATE = 4
NX = 96
NY = 64
NZ = 128
N_TM = 8


def with_ends(drawn, rng, least, top_value):
    shape = drawn.shape
    place = [jax.random.randint(jax.random.fold_in(rng, axis), (), 0, shape[axis]) for axis in range(len(shape))]
    drawn = drawn.at[tuple(place)].set(least)
    longest = shape.index(max(shape))
    place[longest] = (place[longest] + 1) % shape[longest]
    return drawn.at[tuple(place)].set(top_value)


def level_of(stream_key, extent, pieces, low, high):
    factor_of, own = 1.0, jax.random.fold_in(stream_key, 6)
    for dim, blocks in pieces:
        steps = jnp.exp(jax.random.uniform(jax.random.fold_in(own, dim), (blocks,), jnp.float32, low / len(pieces), high / len(pieces)))
        factor_of = factor_of * jnp.repeat(steps, extent[dim] // blocks).reshape([-1 if axis == dim else 1 for axis in range(len(extent))])
    return factor_of


def normal_values(stream_key, extent, scale, bound, shards=(), held_as=jnp.bfloat16):
    drawn = scale * jax.random.normal(stream_key, extent, jnp.float32)
    if shards:
        drawn = drawn * level_of(stream_key, extent, shards, -0.22, 0.18)
    return jnp.clip(drawn, -bound, bound).astype(held_as)


def setup_inputs(seed: int = 0) -> dict:
    streams_of = jax.random.split(jax.random.key(seed), 8)
    return {
        "segment_opening_values": normal_values(streams_of[0], (N_TM, STATE, NX, NY, NZ), 1.0, 6.0, ((0, 8), (2, 8), (3, 4)), jnp.float32),
        "cell_material_label": with_ends(jax.random.randint(streams_of[1], (NX, NY, NZ), 0, REGIONS), jax.random.fold_in(streams_of[1], 1), 0, REGIONS - 1).astype(jnp.int32),
        "material_rigidity": jnp.clip(jnp.exp(jax.random.uniform(streams_of[2], (REGIONS,), jnp.float32, math.log(0.3), math.log(3.0))), 0.3, 3.0),
        "dilation_mismatch": jnp.clip(jax.random.uniform(streams_of[3], (REGIONS,), jnp.float32, -1.0, 1.0), -1.0, 1.0),
        "heat_swings_array": jnp.clip(0.5 + 3.5 * jax.random.uniform(streams_of[4], (N_TM, PARTITION_PACES), jnp.float32) ** level_of(streams_of[4], (N_TM, PARTITION_PACES), ((0, 8),), -0.2, 0.2), 0.5, 4.0),
        "prony_coefficients": jnp.clip(jnp.exp(jax.random.uniform(streams_of[5], (PRONY,), jnp.float32, math.log(0.2), math.log(2.0))), 0.2, 2.0),
        "prony_decay_times": jnp.clip(jnp.exp(jax.random.uniform(streams_of[6], (PRONY,), jnp.float32, math.log(0.7), math.log(48.0))), 0.7, 48.0),
    }


corners = [(near_one, near_two, near_three) for near_one in (0, 1) for near_two in (0, 1) for near_three in (0, 1)]
diagonal_weights = [1.0 / 3.0] * 8
thermal_weights = [0.25 * (2 * near_three - 1) for near_one, near_two, near_three in corners]


def region_lookup(cell_material_label, region_table):
    looked_up = jnp.zeros(cell_material_label.shape, region_table.dtype)
    for region in range(region_table.shape[0]):
        looked_up = looked_up + jnp.where(cell_material_label == region, region_table[region], jnp.zeros((), region_table.dtype))
    return looked_up


def stencil_apply(padded, cell_rigidity):
    extent_one, extent_two, extent_three = cell_rigidity.shape
    values = [padded[near_one:near_one + extent_one, near_two:near_two + extent_two, near_three:near_three + extent_three] for near_one, near_two, near_three in corners]
    corner_total = values[0]
    for corner_value in values[1:]:
        corner_total = corner_total + corner_value
    result = None
    for corner_index, (near_one, near_two, near_three) in enumerate(corners):
        face_sum = values[corner_index ^ 4] + values[corner_index ^ 2] + values[corner_index ^ 1]
        element_part = cell_rigidity * ((5.0 / 12.0) * values[corner_index] + (face_sum - corner_total) / 12.0)
        node_part = element_part[1 - near_one:extent_one - near_one, 1 - near_two:extent_two - near_two, 1 - near_three:extent_three - near_three]
        result = node_part if result is None else result + node_part
    return result


def nodal_sum(element_field, weights):
    extent_one, extent_two, extent_three = element_field.shape
    result = None
    for corner_index, (near_one, near_two, near_three) in enumerate(corners):
        node_part = weights[corner_index] * element_field[1 - near_one:extent_one - near_one, 1 - near_two:extent_two - near_two, 1 - near_three:extent_three - near_three]
        result = node_part if result is None else result + node_part
    return result


def apply_operator(field, shift_value, cell_rigidity):
    return shift_value * field + stencil_apply(jnp.pad(field, 1), cell_rigidity)


def conjugate_solve(rhs_field, initial, shift_value, diagonal, cell_rigidity, iterations):
    solution = initial
    remainder = rhs_field - apply_operator(solution, shift_value, cell_rigidity)
    scaled = remainder / diagonal
    search = scaled
    gamma_now = jnp.sum(remainder * scaled)
    for iteration in range(iterations):
        image = apply_operator(search, shift_value, cell_rigidity)
        step_size = gamma_now / jnp.sum(search * image)
        solution = solution + step_size * search
        if iteration + 1 < iterations:
            remainder = remainder - step_size * image
            scaled = remainder / diagonal
            gamma_next = jnp.sum(remainder * scaled)
            search = scaled + (gamma_next / gamma_now) * search
            gamma_now = gamma_next
    return solution


def moment_forward(present_displacements, heat_level, step_length, iterations, dilation_deformation, rigidity_main_terms, cell_rigidity, prony_coefficients, prony_decay_times):
    decay_rate = jnp.exp(-step_length / prony_decay_times)
    factors = prony_coefficients * decay_rate
    shift_value = 1.0 / step_length + jnp.sum(factors)
    history = present_displacements[1:]
    rhs_field = present_displacements[0] / step_length + heat_level * dilation_deformation + jnp.sum(factors[:, None, None, None] * history, axis=0)
    displaced = conjugate_solve(rhs_field, present_displacements[0], shift_value, shift_value + rigidity_main_terms, cell_rigidity, iterations)
    history = decay_rate[:, None, None, None] * history + (1.0 - decay_rate)[:, None, None, None] * displaced[None]
    return jnp.concatenate([displaced[None], history], axis=0)


def reference(segment_opening_values, cell_material_label, material_rigidity, dilation_mismatch, heat_swings_array, prony_coefficients, prony_decay_times):
    coefficient = region_lookup(cell_material_label, material_rigidity)
    loaded = coefficient * region_lookup(cell_material_label, dilation_mismatch)
    cell_rigidity = jnp.pad(coefficient, ((1, 0), (1, 0), (1, 0)))
    element_load = jnp.pad(loaded, ((1, 0), (1, 0), (1, 0)))
    dilation_deformation = nodal_sum(element_load, thermal_weights)
    rigidity_main_terms = nodal_sum(cell_rigidity, diagonal_weights)
    loose_interval_span = 1.0 * PARTITION_PACES
    corrections = []
    first_coarse = None
    for segment_number in range(N_TM):
        present_displacements = segment_opening_values[segment_number]
        for sharp_interval_span in range(PARTITION_PACES):
            present_displacements = moment_forward(present_displacements, heat_swings_array[segment_number, sharp_interval_span], 1.0, SHARP_SOLVER_ITER, dilation_deformation, rigidity_main_terms, cell_rigidity, prony_coefficients, prony_decay_times)
        crude_advance_operator = moment_forward(segment_opening_values[segment_number], heat_swings_array[segment_number, PARTITION_PACES - 1], loose_interval_span, LOOSE_SOLVER_ITER, dilation_deformation, rigidity_main_terms, cell_rigidity, prony_coefficients, prony_decay_times)
        corrections.append(present_displacements - crude_advance_operator)
        if segment_number == 0:
            first_coarse = crude_advance_operator
    segment_closing_values = []
    for segment_number in range(N_TM):
        if segment_number == 0:
            crude_prediction = first_coarse
        else:
            crude_prediction = moment_forward(segment_closing_values[-1], heat_swings_array[segment_number, PARTITION_PACES - 1], loose_interval_span, LOOSE_SOLVER_ITER, dilation_deformation, rigidity_main_terms, cell_rigidity, prony_coefficients, prony_decay_times)
        segment_closing_values.append(crude_prediction + corrections[segment_number])
    return jnp.stack(segment_closing_values)
```

```python
import functools

import jax
import jax.numpy as jnp
from jax import lax
from jax.experimental import pallas as pl
from jax.experimental.pallas import tpu as pltpu
from jax.sharding import PartitionSpec as P

PACES = 2
SHARP = 3
LOOSE = 2
PRONY = 3
L = 3
LINE = ("gx", "gy")
LIMIT = 48 << 20


def masks(ny, nz):
    row = lax.broadcasted_iota(jnp.int32, (ny, nz), 0)
    lane = lax.broadcasted_iota(jnp.int32, (ny, nz), 1)
    return row == 0, row == ny - 1, lane == 0, lane == nz - 1


class Shifts:
    def __init__(self, ny, nz):
        self.ny, self.nz = ny, nz
        self.row_first, self.row_last, self.lane_first, self.lane_last = masks(ny, nz)

    def zup(self, v):
        return jnp.where(self.lane_last, 0.0, pltpu.roll(v, self.nz - 1, 1))

    def zdn(self, v):
        return jnp.where(self.lane_first, 0.0, pltpu.roll(v, 1, 1))

    def yup(self, v):
        return jnp.where(self.row_last, 0.0, pltpu.roll(v, self.ny - 1, 0))

    def ydn(self, v):
        return jnp.where(self.row_first, 0.0, pltpu.roll(v, 1, 0))


def off_diagonal(sh, v, k, low, high, put):
    def spread(plane):
        up = sh.zup(plane)
        side, side_up = sh.yup(plane), sh.yup(up)
        return plane, up, side, side_up, plane + up, side + side_up

    near = spread(v(low - 1))
    carry = None
    for e in range(low - 1, high + 1):
        far = spread(v(e + 1))
        a, a_up, b, b_up, a_sum, b_sum = near
        c, c_up, d, d_up, c_sum, d_sum = far
        one_up, two_up = b_up + c_up, a_up + d_up
        one, two = b + c, a + d
        kk = k(e)
        if e >= low:
            e00, f00 = kk * (d_sum + one_up), kk * (d_sum + one)
            e01, f01 = kk * (c_sum + two_up), kk * (c_sum + two)
            e10, e11, f10, f11 = carry
            put(e, (e00 + e10) + sh.ydn(e01 + e11) + sh.zdn((f00 + f10) + sh.ydn(f01 + f11)))
        if e < high:
            carry = (
                kk * (b_sum + two_up),
                kk * (a_sum + one_up),
                kk * (b_sum + two),
                kk * (a_sum + one),
            )
        near = far


def prony(dt, coef_ref, time_ref):
    decay = [jnp.exp(-dt / jnp.full((1, 128), time_ref[p], jnp.float32)) for p in range(PRONY)]
    rest = [1.0 - d for d in decay]
    f = [coef_ref[p] * decay[p] for p in range(PRONY)]
    return decay, rest, f, 1.0 / dt + (f[0] + f[1] + f[2])


def moments_out(values, red_ref):
    lane = lax.broadcasted_iota(jnp.int32, (1, 128), 1)
    packed = jnp.zeros((1, 128), jnp.float32)
    for at, field in enumerate(values):
        total = jnp.sum(jnp.sum(field, axis=0, keepdims=True), axis=1, keepdims=True)
        packed = jnp.where(lane == at, total, packed)
    red_ref[...] = jnp.broadcast_to(packed[None], red_ref.shape)


def moments_in(red_ref, first, count):
    total = jnp.sum(red_ref[...], axis=0)
    lane = lax.broadcasted_iota(jnp.int32, (1, 128), 1)
    return [
        jnp.broadcast_to(
            jnp.sum(jnp.where(lane == first + i, total, 0.0), axis=1, keepdims=True), (1, 128)
        )
        for i in range(count)
    ]


def galerkin(nu):
    m = len(nu) // 2
    mu = [nu[i] + nu[i + 1] for i in range(2 * m - 1)]
    rows = [[mu[i + j] for j in range(m)] + [nu[i]] for i in range(m)]
    for i in range(m):
        for r in range(i + 1, m):
            factor = rows[r][i] / rows[i][i]
            for j in range(i + 1, m + 1):
                rows[r][j] = rows[r][j] - factor * rows[i][j]
    c = [None] * m
    for i in reversed(range(m)):
        acc = rows[i][m]
        for j in range(i + 1, m):
            acc = acc - rows[i][j] * c[j]
        c[i] = acc / rows[i][i]
    return c


def start_kernel(
    rigid_ref, dilate_ref, heat_ref, coef_ref, time_ref,
    own_ref, lo_ref, hi_ref, lo2_ref, hi2_ref,
    kel_ref, theta_ref, inv_f_ref, inv_c_ref, state_ref,
    zf_ref, ozf_ref, oozf_ref, zc_ref, ozc_ref,
    lo1_out, hi1_out, lo2_out, hi2_out, red_ref,
    kal_ref, au_ref, w_ref,
):
    ny, nz = kel_ref.shape[1:]
    sh = Shifts(ny, nz)
    chunks = own_ref.shape[0]

    def raw(field, i):
        if i == -L - 1:
            parts = [lo2_ref[c, field, 0] for c in range(chunks)]
        elif i < 0:
            parts = [lo_ref[c, field, i + L] for c in range(chunks)]
        elif i < L:
            parts = [own_ref[c, field, i] for c in range(chunks)]
        elif i < 2 * L:
            parts = [hi_ref[c, field, i - L] for c in range(chunks)]
        else:
            parts = [hi2_ref[c, field, 0] for c in range(chunks)]
        return jnp.concatenate(parts, axis=0)

    for e in range(-4, 6):
        label = raw(0, e)
        stiff = jnp.zeros((ny, nz), jnp.float32)
        load = jnp.zeros((ny, nz), jnp.float32)
        for region in range(rigid_ref.shape[0]):
            here = label == (region + 1.0)
            stiff = jnp.where(here, rigid_ref[region], stiff)
            load = jnp.where(here, dilate_ref[region], load)
        kel_ref[e + 4] = stiff * (-1.0 / 12.0)
        kal_ref[e + 4] = 0.25 * (stiff * load)

    decay_f, rest_f, ff, shift_f = prony(1.0, coef_ref, time_ref)
    decay_c, rest_c, fc, shift_c = prony(1.0 * PACES, coef_ref, time_ref)

    for i in range(-3, 6):
        ksum = kel_ref[i + 3] + kel_ref[i + 4]
        ksum = ksum + sh.ydn(ksum)
        ksum = ksum + sh.zdn(ksum)
        diag = -4.0 * ksum
        asum = kal_ref[i + 3] + kal_ref[i + 4]
        asum = asum + sh.ydn(asum)
        theta_ref[i + 3] = sh.zdn(asum) - asum
        inside = raw(0, i) > 0.5
        inv_f_ref[i + 3] = jnp.where(inside, 1.0 / (diag + shift_f), 0.0)
        inv_c_ref[i + 3] = jnp.where(inside, 1.0 / (diag + shift_c), 0.0)

    for i in range(-4, 7):
        state_ref[i + 4] = raw(1, i)

    def u(i):
        return state_ref[i + 4]

    def k(e):
        return kel_ref[e + 4]

    def put_au(i, plane):
        au_ref[i + 3] = plane

    off_diagonal(sh, u, k, -3, 5, put_au)

    zeros = jnp.zeros((ny, nz), jnp.float32)
    acc = [zeros] * 10
    for i in range(-3, 6):
        h = [raw(2 + p, i) for p in range(PRONY)]
        fh = [ff[p] * h[p] for p in range(PRONY)]
        state_ref[11 + i + 3] = decay_f[0] * fh[0] + decay_f[1] * fh[1] + decay_f[2] * fh[2]
        ui = u(i)
        load = heat_ref[0, 0] * theta_ref[i + 3] + (fh[0] + fh[1] + fh[2])
        s = load + ui - au_ref[i + 3]
        z = inv_f_ref[i + 3] * s - ui
        zf_ref[i + 3] = z
        if 0 <= i < L:
            acc[0] = acc[0] + z * (s - ui * (1.0 / inv_f_ref[i + 3]))
        if -2 <= i < 5:
            load = heat_ref[0, 1] * theta_ref[i + 3]
            load = load + (fc[0] * h[0] + fc[1] * h[1] + fc[2] * h[2])
            s = load + ui * (1.0 / PACES) - au_ref[i + 3]
            z = inv_c_ref[i + 3] * s - ui
            w_ref[i + 2] = z
            if 0 <= i < L:
                zc_ref[i] = z
                acc[6] = acc[6] + z * (s - ui * (1.0 / inv_c_ref[i + 3]))

    def put_oz(i, plane):
        oz = inv_f_ref[i + 3] * plane
        ozf_ref[i + 2] = oz
        if 0 <= i < L:
            acc[1] = acc[1] + zf_ref[i + 3] * plane
            acc[2] = acc[2] + oz * plane

    off_diagonal(sh, lambda i: zf_ref[i + 3], k, -2, 4, put_oz)

    def put_ooz(i, plane):
        ooz = inv_f_ref[i + 3] * plane
        oozf_ref[i + 1] = ooz
        if 0 <= i < L:
            acc[3] = acc[3] + ozf_ref[i + 2] * plane
            acc[4] = acc[4] + ooz * plane

    off_diagonal(sh, lambda i: ozf_ref[i + 2], k, -1, 3, put_ooz)

    def put_last(i, plane):
        acc[5] = acc[5] + oozf_ref[i + 1] * plane

    off_diagonal(sh, lambda i: oozf_ref[i + 1], k, 0, 2, put_last)

    def put_ozc(i, plane):
        oz = inv_c_ref[i + 3] * plane
        au_ref[i + 3] = oz
        if 0 <= i < L:
            ozc_ref[i] = oz
            acc[7] = acc[7] + w_ref[i + 2] * plane
            acc[8] = acc[8] + oz * plane

    off_diagonal(sh, lambda i: w_ref[i + 2], k, -1, 3, put_ozc)

    def put_lastc(i, plane):
        acc[9] = acc[9] + au_ref[i + 3] * plane

    off_diagonal(sh, lambda i: au_ref[i + 3], k, 0, 2, put_lastc)

    moments_out(acc, red_ref)

    lo1_out[0], lo1_out[1], lo1_out[2] = ozf_ref[2 + 2], oozf_ref[1 + 1], oozf_ref[2 + 1]
    hi1_out[0], hi1_out[1], hi1_out[2] = ozf_ref[0 + 2], oozf_ref[0 + 1], oozf_ref[1 + 1]
    lo2_out[0], lo2_out[1], lo2_out[2] = zf_ref[0 + 3], ozf_ref[0 + 2], oozf_ref[0 + 1]
    hi2_out[0], hi2_out[1], hi2_out[2] = zf_ref[2 + 3], ozf_ref[2 + 2], oozf_ref[2 + 1]


def second_kernel(
    heat_ref, coef_ref, time_ref, place_ref,
    red_in, kel_ref, theta_ref, inv_f_ref, state_ref, own_ref,
    zf_ref, ozf_ref, oozf_ref, zc_ref, ozc_ref,
    lo1_ref, hi1_ref, lo2_ref, hi2_ref,
    base_ref, z_out, oz_out, ooz_out, red_ref,
    u_ref, z_ref, oz_ref, ooz_ref, au_ref,
):
    ny, nz = kel_ref.shape[1:]
    sh = Shifts(ny, nz)
    chunks = own_ref.shape[0]
    decay_f, rest_f, ff, shift_f = prony(1.0, coef_ref, time_ref)
    decay_c, rest_c, fc, shift_c = prony(1.0 * PACES, coef_ref, time_ref)
    c = galerkin(moments_in(red_in, 0, 6))
    b = galerkin(moments_in(red_in, 6, 4))

    def zf(i):
        return lo_hi(i, -3, 5, zf_ref, 3, None, None, 0)

    def lo_hi(i, low, high, ref, shift, near, off, far_at):
        if i == -4:
            return hi_lo2(True, far_at)
        if i == 6:
            return hi_lo2(False, far_at)
        if low <= i <= high:
            return ref[i + shift]
        return near[i][0][near[i][1]]

    def hi_lo2(low, at):
        return lo2_ref[at] if low else hi2_ref[at]

    near_oz = {-3: (lo1_ref, 0), 5: (hi1_ref, 0)}
    near_ooz = {-3: (lo1_ref, 1), -2: (lo1_ref, 2), 4: (hi1_ref, 1), 5: (hi1_ref, 2)}
    for i in range(-4, 7):
        z = zf(i)
        oz = lo_hi(i, -2, 4, ozf_ref, 2, near_oz, None, 1)
        ooz = lo_hi(i, -1, 3, oozf_ref, 1, near_ooz, None, 2)
        u_ref[i + 4] = state_ref[i + 4] + c[0] * z + c[1] * oz + c[2] * ooz

    def k(e):
        return kel_ref[e + 4]

    def put_au(i, plane):
        au_ref[i + 3] = plane

    off_diagonal(sh, lambda i: u_ref[i + 4], k, -3, 5, put_au)

    grow = ff[0] * rest_f[0] + ff[1] * rest_f[1] + ff[2] * rest_f[2]
    zeros = jnp.zeros((ny, nz), jnp.float32)
    acc = [zeros] * 6
    weight = jnp.where(place_ref[0] == 0, 0.0, 1.0)
    for i in range(-3, 6):
        ui = u_ref[i + 4]
        s = heat_ref[0, 1] * theta_ref[i + 3] + state_ref[11 + i + 3] + (grow + 1.0) * ui
        s = s - au_ref[i + 3]
        z = inv_f_ref[i + 3] * s - ui
        z_ref[i + 3] = z
        if 0 <= i < L:
            z_out[i] = z
            acc[0] = acc[0] + z * (s - ui * (1.0 / inv_f_ref[i + 3]))

    for i in range(L):
        u1 = u_ref[i + 4]
        g = state_ref[i + 4] + b[0] * zc_ref[i] + b[1] * ozc_ref[i]
        base_ref[i] = u1 - weight * g
        for p in range(PRONY):
            h = jnp.concatenate([own_ref[q, 2 + p, i] for q in range(chunks)], axis=0)
            h1 = decay_f[p] * h + rest_f[p] * u1
            gh = decay_c[p] * h + rest_c[p] * g
            base_ref[L * (1 + p) + i] = decay_f[p] * h1 + rest_f[p] * u1 - weight * gh

    def put_oz(i, plane):
        oz = inv_f_ref[i + 3] * plane
        oz_ref[i + 2] = oz
        if 0 <= i < L:
            oz_out[i] = oz
            acc[1] = acc[1] + z_ref[i + 3] * plane
            acc[2] = acc[2] + oz * plane

    off_diagonal(sh, lambda i: z_ref[i + 3], k, -2, 4, put_oz)

    def put_ooz(i, plane):
        ooz = inv_f_ref[i + 3] * plane
        ooz_ref[i + 1] = ooz
        if 0 <= i < L:
            ooz_out[i] = ooz
            acc[3] = acc[3] + oz_ref[i + 2] * plane
            acc[4] = acc[4] + ooz * plane

    off_diagonal(sh, lambda i: oz_ref[i + 2], k, -1, 3, put_ooz)

    def put_last(i, plane):
        acc[5] = acc[5] + ooz_ref[i + 1] * plane

    off_diagonal(sh, lambda i: ooz_ref[i + 1], k, 0, 2, put_last)
    moments_out(acc, red_ref)


def block_kernel(coef_ref, time_ref, red_in, base_ref, z_ref, oz_ref, ooz_ref, blk_ref):
    decay_f, rest_f, ff, shift_f = prony(1.0, coef_ref, time_ref)
    c = galerkin(moments_in(red_in, 0, 6))
    for i in range(L):
        delta = c[0] * z_ref[i] + c[1] * oz_ref[i] + c[2] * ooz_ref[i]
        blk_ref[i] = base_ref[i] + delta
        for p in range(PRONY):
            blk_ref[L * (1 + p) + i] = base_ref[L * (1 + p) + i] + rest_f[p] * delta


def opening_kernel(coef_ref, time_ref, blk_ref, lo_out, hi_out):
    decay, rest, f, shift = prony(1.0 * PACES, coef_ref, time_ref)

    def total(i):
        return f[0] * blk_ref[L + i] + f[1] * blk_ref[2 * L + i] + f[2] * blk_ref[3 * L + i]

    for i in range(L):
        lo_out[i] = blk_ref[i]
        hi_out[i] = blk_ref[i]
    sums = [total(i) for i in range(L)]
    lo_out[3], lo_out[4] = sums[0], sums[1]
    hi_out[3], hi_out[4] = sums[1], sums[2]


def chain_kernel(turn, count, opened, *refs):
    refs = list(refs)
    heat_ref, coef_ref, time_ref, place_ref = refs[:4]
    refs = refs[4:]
    if opened:
        base_in, lo_ref, hi_ref = refs[:3]
        refs = refs[3:]
    else:
        red_in, base_in, z_in, oz_in, lo_ref, hi_ref = refs[:6]
        refs = refs[6:]
    kel_ref, theta_ref, inv_ref, blk_ref = refs[:4]
    base_ref, z_ref, oz_ref, lo_out, hi_out, red_ref, u_ref, au_ref = refs[4:]
    ny, nz = kel_ref.shape[1:]
    sh = Shifts(ny, nz)
    decay, rest, f, shift = prony(1.0 * PACES, coef_ref, time_ref)
    grow = f[0] * rest[0] + f[1] * rest[1] + f[2] * rest[2]
    step = lax.rem(place_ref[0] + turn, count)
    heat = heat_ref[step, PACES - 1]
    opening = step == 0
    fresh = step == 1

    if not opened:
        c = galerkin(moments_in(red_in, 0, 4))

    def delta(i):
        if i == -3:
            z, oz = lo_ref[5], lo_ref[6]
        elif i == 5:
            z, oz = hi_ref[5], hi_ref[6]
        else:
            z = z_in[i + 2]
            oz = oz_in[i + 1] if -1 <= i <= 3 else (lo_ref[7] if i == -2 else hi_ref[7])
        return jnp.where(fresh, 0.0, c[0] * z + c[1] * oz)

    for i in range(-3, 6):
        base = lo_ref[i + 3] if i < 0 else hi_ref[i - L] if i >= L else base_in[i]
        if opened:
            u_ref[i + 3] = base
            d = None
        else:
            d = delta(i)
            u_ref[i + 3] = base + d
        if 0 <= i < L:
            h = [base_in[L * (1 + p) + i] for p in range(PRONY)]
            if d is not None:
                h = [h[p] + rest[p] * d for p in range(PRONY)]
            total = f[0] * h[0] + f[1] * h[1] + f[2] * h[2]
            ui = u_ref[i + 3]
            base_ref[i] = jnp.where(opening, 0.0, ui) + blk_ref[i]
            for p in range(PRONY):
                ahead = jnp.where(opening, 0.0, decay[p] * h[p] + rest[p] * ui)
                base_ref[L * (1 + p) + i] = ahead + blk_ref[L * (1 + p) + i]
        elif -2 <= i < 5:
            total = lo_ref[3 + i + 2] if i < 0 else hi_ref[3 + i - L]
            if d is not None:
                total = total + grow * d
        if -2 <= i < 5:
            au_ref[i + 2] = heat * theta_ref[i + 3] + total

    zeros = jnp.zeros((ny, nz), jnp.float32)
    acc = [zeros] * 4

    def k(e):
        return kel_ref[e + 4]

    def put_z(i, plane):
        ui = u_ref[i + 3]
        s = au_ref[i + 2] + ui * (1.0 / PACES) - plane
        inv = inv_ref[i + 3]
        z = inv * s - ui
        z_ref[i + 2] = z
        if 0 <= i < L:
            acc[0] = acc[0] + z * (s - ui * (1.0 / inv))

    off_diagonal(sh, lambda i: u_ref[i + 3], k, -2, 4, put_z)

    def put_oz(i, plane):
        oz = inv_ref[i + 3] * plane
        oz_ref[i + 1] = oz
        if 0 <= i < L:
            acc[1] = acc[1] + z_ref[i + 2] * plane
            acc[2] = acc[2] + oz * plane

    off_diagonal(sh, lambda i: z_ref[i + 2], k, -1, 3, put_oz)

    def put_last(i, plane):
        acc[3] = acc[3] + oz_ref[i + 1] * plane

    off_diagonal(sh, lambda i: oz_ref[i + 1], k, 0, 2, put_last)
    moments_out(acc, red_ref)

    def total(i):
        return f[0] * base_ref[L + i] + f[1] * base_ref[2 * L + i] + f[2] * base_ref[3 * L + i]

    sums = [total(i) for i in range(L)]
    for i in range(L):
        lo_out[i] = base_ref[i]
        hi_out[i] = base_ref[i]
    lo_out[3], lo_out[4] = sums[0], sums[1]
    hi_out[3], hi_out[4] = sums[1], sums[2]
    lo_out[5], lo_out[6], lo_out[7] = z_ref[2 + 2], oz_ref[2 + 1], oz_ref[1 + 1]
    hi_out[5], hi_out[6], hi_out[7] = z_ref[0 + 2], oz_ref[0 + 1], oz_ref[1 + 1]


def closing_kernel(coef_ref, time_ref, place_ref, red_in, base_ref, z_ref, oz_ref, out_ref):
    decay, rest, f, shift = prony(1.0 * PACES, coef_ref, time_ref)
    c = galerkin(moments_in(red_in, 0, 4))
    first = place_ref[0] == 0
    chunks, _, _, rows, _ = out_ref.shape
    for i in range(L):
        delta = jnp.where(first, 0.0, c[0] * z_ref[i + 2] + c[1] * oz_ref[i + 1])
        fields = [base_ref[i] + delta]
        for p in range(PRONY):
            fields.append(base_ref[L * (1 + p) + i] + rest[p] * delta)
        for at, field in enumerate(fields):
            for q in range(chunks):
                out_ref[q, at, i] = field[q * rows : (q + 1) * rows]


SMEM = pl.BlockSpec(memory_space=pltpu.SMEM)
VMEM = pl.BlockSpec(memory_space=pltpu.VMEM)


def call(kernel, name, small, large, outs, scratch=()):
    f32 = jnp.float32
    return pl.pallas_call(
        kernel,
        name=name,
        out_shape=[jax.ShapeDtypeStruct(s, f32) for s in outs],
        in_specs=[SMEM] * len(small) + [VMEM] * len(large),
        out_specs=[VMEM] * len(outs),
        scratch_shapes=[pltpu.VMEM(s, f32) for s in scratch],
        compiler_params=pltpu.CompilerParams(vmem_limit_bytes=LIMIT),
    )(*small, *large)


def on_device(
    segment_opening_values,
    cell_material_label,
    material_rigidity,
    dilation_mismatch,
    heat_swings_array,
    prony_coefficients,
    prony_decay_times,
):
    n_tm, n_gy = lax.axis_size("tm"), lax.axis_size("gy")
    line = lax.axis_size("gx") * n_gy
    nx, ny_part, nz = cell_material_label.shape
    ny = ny_part * n_gy
    assert nx == L * n_gy
    plane = (ny, nz)

    def up(value, by):
        return lax.ppermute(value, LINE, [(s, s + by) for s in range(line - by)])

    def down(value, by):
        return lax.ppermute(value, LINE, [(s + by, s) for s in range(line - by)])

    def exchanged(red):
        return lax.all_to_all(red, LINE, 0, 0, tiled=True)

    def ring(block):
        return lax.ppermute(block, "tm", [(s, (s - 1) % n_tm) for s in range(n_tm)])

    place = lax.axis_index("tm").astype(jnp.int32)[None]
    heats = lax.all_gather(heat_swings_array[0], "tm")
    prony_args = (prony_coefficients, prony_decay_times)

    label = cell_material_label.astype(jnp.float32)[None] + 1.0
    raw = jnp.concatenate([label, segment_opening_values[0]], axis=0)
    raw = raw.reshape(2 + PRONY, n_gy, L, ny_part, nz).transpose(1, 0, 2, 3, 4)
    own = lax.all_to_all(raw, "gy", 0, 0, tiled=True)
    lo, hi = up(own, 1), down(own, 1)
    lo2, hi2 = up(own[:, :2, L - 1 :], 2), down(own[:, :2, :1], 2)

    red_shape = (line, 1, 128)
    (kel, theta, inv_f, inv_c, state, zf, ozf, oozf, zc, ozc, lo1, hi1, lo2, hi2, red) = call(
        start_kernel,
        "start",
        (material_rigidity, dilation_mismatch, heat_swings_array, *prony_args),
        (own, lo, hi, lo2, hi2),
        [
            (10, *plane), (9, *plane), (9, *plane), (9, *plane), (20, *plane),
            (9, *plane), (7, *plane), (5, *plane), (L, *plane), (L, *plane),
            (3, *plane), (3, *plane), (3, *plane), (3, *plane), red_shape,
        ],
        [(10, *plane), (9, *plane), (7, *plane)],
    )
    red = exchanged(red)
    hi1, lo1 = down(lo1, 1), up(hi1, 1)
    hi2, lo2 = down(lo2, 2), up(hi2, 2)
    base, z, oz, ooz, red = call(
        second_kernel,
        "second",
        (heat_swings_array, *prony_args, place),
        (red, kel, theta, inv_f, state, own, zf, ozf, oozf, zc, ozc, lo1, hi1, lo2, hi2),
        [(4 * L, *plane), (L, *plane), (L, *plane), (L, *plane), red_shape],
        [(11, *plane), (9, *plane), (7, *plane), (5, *plane), (9, *plane)],
    )
    red = exchanged(red)
    (block,) = call(
        block_kernel, "block", prony_args, (red, base, z, oz, ooz), [(4 * L, *plane)]
    )
    mine = block
    block = ring(block)
    lo, hi = call(opening_kernel, "opening", prony_args, (block,), [(5, *plane)] * 2)
    hi, lo = down(lo, 1), up(hi, 1)
    base = block
    red = z = oz = None
    for turn in range(2, n_tm + 1):
        block = ring(block) if turn < n_tm else mine
        opened = turn == 2
        past = (base, lo, hi) if opened else (red, base, z, oz, lo, hi)
        base, z, oz, lo, hi, red = call(
            functools.partial(chain_kernel, turn, n_tm, opened),
            f"chain{turn}",
            (heats, *prony_args, place),
            (*past, kel, theta, inv_c, block),
            [(4 * L, *plane), (7, *plane), (5, *plane), (8, *plane), (8, *plane), red_shape],
            [(9, *plane), (7, *plane)],
        )
        red = exchanged(red)
        if turn < n_tm:
            hi, lo = down(lo, 1), up(hi, 1)
    (out,) = call(
        closing_kernel,
        "closing",
        (*prony_args, place),
        (red, base, z, oz),
        [(n_gy, 1 + PRONY, L, ny_part, nz)],
    )
    out = lax.all_to_all(out, "gy", 0, 0, tiled=True)
    return out.transpose(1, 0, 2, 3, 4).reshape(1, 1 + PRONY, nx, ny_part, nz)


def solution(mesh):
    placed = (
        P("tm", None, "gx", "gy", None),
        P("gx", "gy", None),
        P(),
        P(),
        P("tm", None),
        P(),
        P(),
    )
    return jax.shard_map(
        on_device,
        mesh=mesh,
        in_specs=placed,
        out_specs=P("tm", None, "gx", "gy", None),
        check_vma=False,
    )
```

```python
import functools

import jax
import jax.numpy as jnp
from jax import lax
from jax.experimental import pallas as pl
from jax.experimental.pallas import tpu as pltpu
from jax.sharding import PartitionSpec as P

PACES = 2
SHARP = 3
LOOSE = 2
PRONY = 3
L = 3
LINE = ("gx", "gy")
LIMIT = 14 << 20


def masks(ny, nz):
    row = lax.broadcasted_iota(jnp.int32, (ny, nz), 0)
    lane = lax.broadcasted_iota(jnp.int32, (ny, nz), 1)
    return row == 0, row == ny - 1, lane == 0, lane == nz - 1


class Shifts:
    def __init__(self, ny, nz):
        self.ny, self.nz = ny, nz
        self.row_first, self.row_last, self.lane_first, self.lane_last = masks(ny, nz)

    def zup(self, v):
        return jnp.where(self.lane_last, 0.0, pltpu.roll(v, self.nz - 1, 1))

    def zdn(self, v):
        return jnp.where(self.lane_first, 0.0, pltpu.roll(v, 1, 1))

    def yup(self, v):
        return jnp.where(self.row_last, 0.0, pltpu.roll(v, self.ny - 1, 0))

    def ydn(self, v):
        return jnp.where(self.row_first, 0.0, pltpu.roll(v, 1, 0))


def off_diagonal(sh, v, k, low, high, put):
    def spread(plane):
        up = sh.zup(plane)
        side, side_up = sh.yup(plane), sh.yup(up)
        return plane, up, side, side_up, plane + up, side + side_up

    near = spread(v(low - 1))
    carry = None
    for e in range(low - 1, high + 1):
        far = spread(v(e + 1))
        a, a_up, b, b_up, a_sum, b_sum = near
        c, c_up, d, d_up, c_sum, d_sum = far
        one_up, two_up = b_up + c_up, a_up + d_up
        one, two = b + c, a + d
        kk = k(e)
        if e >= low:
            e00, f00 = kk * (d_sum + one_up), kk * (d_sum + one)
            e01, f01 = kk * (c_sum + two_up), kk * (c_sum + two)
            e10, e11, f10, f11 = carry
            put(e, (e00 + e10) + sh.ydn(e01 + e11) + sh.zdn((f00 + f10) + sh.ydn(f01 + f11)))
        if e < high:
            carry = (
                kk * (b_sum + two_up),
                kk * (a_sum + one_up),
                kk * (b_sum + two),
                kk * (a_sum + one),
            )
        near = far


def prony(dt, coef_ref, time_ref):
    decay = [jnp.exp(-dt / jnp.full((1, 128), time_ref[p], jnp.float32)) for p in range(PRONY)]
    rest = [1.0 - d for d in decay]
    f = [coef_ref[p] * decay[p] for p in range(PRONY)]
    return decay, rest, f, 1.0 / dt + (f[0] + f[1] + f[2])


def moments_out(values, red_ref):
    lane = lax.broadcasted_iota(jnp.int32, (1, 128), 1)
    packed = jnp.zeros((1, 128), jnp.float32)
    for at, field in enumerate(values):
        total = jnp.sum(jnp.sum(field, axis=0, keepdims=True), axis=1, keepdims=True)
        packed = jnp.where(lane == at, total, packed)
    red_ref[...] = jnp.broadcast_to(packed[None], red_ref.shape)


def moments_in(red_ref, first, count):
    total = jnp.sum(red_ref[...], axis=0)
    lane = lax.broadcasted_iota(jnp.int32, (1, 128), 1)
    return [
        jnp.broadcast_to(
            jnp.sum(jnp.where(lane == first + i, total, 0.0), axis=1, keepdims=True), (1, 128)
        )
        for i in range(count)
    ]


def galerkin(nu):
    m = len(nu) // 2
    mu = [nu[i] + nu[i + 1] for i in range(2 * m - 1)]
    rows = [[mu[i + j] for j in range(m)] + [nu[i]] for i in range(m)]
    for i in range(m):
        for r in range(i + 1, m):
            factor = rows[r][i] / rows[i][i]
            for j in range(i + 1, m + 1):
                rows[r][j] = rows[r][j] - factor * rows[i][j]
    c = [None] * m
    for i in reversed(range(m)):
        acc = rows[i][m]
        for j in range(i + 1, m):
            acc = acc - rows[i][j] * c[j]
        c[i] = acc / rows[i][i]
    return c


def send(odd_side, lo, hi, even_out, odd_out):
    for at, (low, high) in enumerate(zip(lo, hi)):
        even_out[at] = jnp.where(odd_side == 0, high, low)
        odd_out[at] = jnp.where(odd_side == 0, low, high)


def below(odd_side, even_ref, odd_ref, at):
    return jnp.where(odd_side == 0, odd_ref[at], even_ref[at])


def above(odd_side, even_ref, odd_ref, at):
    return jnp.where(odd_side == 0, even_ref[at], odd_ref[at])


def start_kernel(
    rigid_ref, dilate_ref, heat_ref, coef_ref, time_ref, place_ref,
    own_ref, even_ref, odd_ref, even2_ref, odd2_ref,
    kel_ref, theta_ref, inv_f_ref, inv_c_ref, state_ref,
    zf_ref, ozf_ref, oozf_ref, zc_ref, ozc_ref,
    even_out, odd_out, even2_out, odd2_out, red_ref,
    kal_ref, au_ref, w_ref,
):
    ny, nz = kel_ref.shape[1:]
    sh = Shifts(ny, nz)
    chunks = own_ref.shape[0]

    def raw(field, i):
        if i == -L - 1:
            parts = [below(place_ref[2], even2_ref, odd2_ref, (c, field, 0)) for c in range(chunks)]
        elif i < 0:
            parts = [below(place_ref[1], even_ref, odd_ref, (c, field, i + L)) for c in range(chunks)]
        elif i < L:
            parts = [own_ref[c, field, i] for c in range(chunks)]
        elif i < 2 * L:
            parts = [above(place_ref[1], even_ref, odd_ref, (c, field, i - L)) for c in range(chunks)]
        else:
            parts = [above(place_ref[2], even2_ref, odd2_ref, (c, field, 0)) for c in range(chunks)]
        return jnp.concatenate(parts, axis=0)

    for e in range(-4, 6):
        label = raw(0, e)
        stiff = jnp.zeros((ny, nz), jnp.float32)
        load = jnp.zeros((ny, nz), jnp.float32)
        for region in range(rigid_ref.shape[0]):
            here = label == (region + 1.0)
            stiff = jnp.where(here, rigid_ref[region], stiff)
            load = jnp.where(here, dilate_ref[region], load)
        kel_ref[e + 4] = stiff * (-1.0 / 12.0)
        kal_ref[e + 4] = 0.25 * (stiff * load)

    decay_f, rest_f, ff, shift_f = prony(1.0, coef_ref, time_ref)
    decay_c, rest_c, fc, shift_c = prony(1.0 * PACES, coef_ref, time_ref)

    for i in range(-3, 6):
        ksum = kel_ref[i + 3] + kel_ref[i + 4]
        ksum = ksum + sh.ydn(ksum)
        ksum = ksum + sh.zdn(ksum)
        diag = -4.0 * ksum
        asum = kal_ref[i + 3] + kal_ref[i + 4]
        asum = asum + sh.ydn(asum)
        theta_ref[i + 3] = sh.zdn(asum) - asum
        inside = raw(0, i) > 0.5
        inv_f_ref[i + 3] = jnp.where(inside, 1.0 / (diag + shift_f), 0.0)
        inv_c_ref[i + 3] = jnp.where(inside, 1.0 / (diag + shift_c), 0.0)

    for i in range(-4, 7):
        state_ref[i + 4] = raw(1, i)

    def u(i):
        return state_ref[i + 4]

    def k(e):
        return kel_ref[e + 4]

    def put_au(i, plane):
        au_ref[i + 3] = plane

    off_diagonal(sh, u, k, -3, 5, put_au)

    zeros = jnp.zeros((ny, nz), jnp.float32)
    acc = [zeros] * 10
    for i in range(-3, 6):
        h = [raw(2 + p, i) for p in range(PRONY)]
        fh = [ff[p] * h[p] for p in range(PRONY)]
        state_ref[11 + i + 3] = decay_f[0] * fh[0] + decay_f[1] * fh[1] + decay_f[2] * fh[2]
        ui = u(i)
        load = heat_ref[0, 0] * theta_ref[i + 3] + (fh[0] + fh[1] + fh[2])
        s = load + ui - au_ref[i + 3]
        z = inv_f_ref[i + 3] * s - ui
        zf_ref[i + 3] = z
        if 0 <= i < L:
            acc[0] = acc[0] + z * (s - ui * (1.0 / inv_f_ref[i + 3]))
        if -2 <= i < 5:
            load = heat_ref[0, 1] * theta_ref[i + 3]
            load = load + (fc[0] * h[0] + fc[1] * h[1] + fc[2] * h[2])
            s = load + ui * (1.0 / PACES) - au_ref[i + 3]
            z = inv_c_ref[i + 3] * s - ui
            w_ref[i + 2] = z
            if 0 <= i < L:
                zc_ref[i] = z
                acc[6] = acc[6] + z * (s - ui * (1.0 / inv_c_ref[i + 3]))

    def put_oz(i, plane):
        oz = inv_f_ref[i + 3] * plane
        ozf_ref[i + 2] = oz
        if 0 <= i < L:
            acc[1] = acc[1] + zf_ref[i + 3] * plane
            acc[2] = acc[2] + oz * plane

    off_diagonal(sh, lambda i: zf_ref[i + 3], k, -2, 4, put_oz)

    def put_ooz(i, plane):
        ooz = inv_f_ref[i + 3] * plane
        oozf_ref[i + 1] = ooz
        if 0 <= i < L:
            acc[3] = acc[3] + ozf_ref[i + 2] * plane
            acc[4] = acc[4] + ooz * plane

    off_diagonal(sh, lambda i: ozf_ref[i + 2], k, -1, 3, put_ooz)

    def put_last(i, plane):
        acc[5] = acc[5] + oozf_ref[i + 1] * plane

    off_diagonal(sh, lambda i: oozf_ref[i + 1], k, 0, 2, put_last)

    def put_ozc(i, plane):
        oz = inv_c_ref[i + 3] * plane
        au_ref[i + 3] = oz
        if 0 <= i < L:
            ozc_ref[i] = oz
            acc[7] = acc[7] + w_ref[i + 2] * plane
            acc[8] = acc[8] + oz * plane

    off_diagonal(sh, lambda i: w_ref[i + 2], k, -1, 3, put_ozc)

    def put_lastc(i, plane):
        acc[9] = acc[9] + au_ref[i + 3] * plane

    off_diagonal(sh, lambda i: au_ref[i + 3], k, 0, 2, put_lastc)

    moments_out(acc, red_ref)

    lo1 = [ozf_ref[2 + 2], oozf_ref[1 + 1], oozf_ref[2 + 1]]
    hi1 = [ozf_ref[0 + 2], oozf_ref[0 + 1], oozf_ref[1 + 1]]
    lo2 = [zf_ref[0 + 3], ozf_ref[0 + 2], oozf_ref[0 + 1]]
    hi2 = [zf_ref[2 + 3], ozf_ref[2 + 2], oozf_ref[2 + 1]]
    send(place_ref[1], lo1, hi1, even_out, odd_out)
    send(place_ref[2], lo2, hi2, even2_out, odd2_out)


def second_kernel(
    heat_ref, coef_ref, time_ref, place_ref,
    red_in, kel_ref, theta_ref, inv_f_ref, state_ref, own_ref,
    zf_ref, ozf_ref, oozf_ref, zc_ref, ozc_ref,
    even_ref, odd_ref, even2_ref, odd2_ref,
    base_ref, z_out, oz_out, ooz_out, red_ref,
    u_ref, z_ref, oz_ref, ooz_ref, au_ref,
):
    ny, nz = kel_ref.shape[1:]
    sh = Shifts(ny, nz)
    chunks = own_ref.shape[0]
    decay_f, rest_f, ff, shift_f = prony(1.0, coef_ref, time_ref)
    decay_c, rest_c, fc, shift_c = prony(1.0 * PACES, coef_ref, time_ref)
    c = galerkin(moments_in(red_in, 0, 6))
    b = galerkin(moments_in(red_in, 6, 4))

    near, far = place_ref[1], place_ref[2]

    def basis(i, at, ref, reach):
        if i == -4:
            return below(far, even2_ref, odd2_ref, at)
        if i == 6:
            return above(far, even2_ref, odd2_ref, at)
        if -reach <= i <= L - 1 + reach:
            return ref[i + reach]
        if at == 1:
            return (below if i < 0 else above)(near, even_ref, odd_ref, 0)
        if i < 0:
            return below(near, even_ref, odd_ref, i + 4)
        return above(near, even_ref, odd_ref, i - 3)

    for i in range(-4, 7):
        z, oz, ooz = basis(i, 0, zf_ref, 3), basis(i, 1, ozf_ref, 2), basis(i, 2, oozf_ref, 1)
        u_ref[i + 4] = state_ref[i + 4] + c[0] * z + c[1] * oz + c[2] * ooz

    def k(e):
        return kel_ref[e + 4]

    def put_au(i, plane):
        au_ref[i + 3] = plane

    off_diagonal(sh, lambda i: u_ref[i + 4], k, -3, 5, put_au)

    grow = ff[0] * rest_f[0] + ff[1] * rest_f[1] + ff[2] * rest_f[2]
    zeros = jnp.zeros((ny, nz), jnp.float32)
    acc = [zeros] * 6
    weight = jnp.where(place_ref[0] == 0, 0.0, 1.0)
    for i in range(-3, 6):
        ui = u_ref[i + 4]
        s = heat_ref[0, 1] * theta_ref[i + 3] + state_ref[11 + i + 3] + (grow + 1.0) * ui
        s = s - au_ref[i + 3]
        z = inv_f_ref[i + 3] * s - ui
        z_ref[i + 3] = z
        if 0 <= i < L:
            z_out[i] = z
            acc[0] = acc[0] + z * (s - ui * (1.0 / inv_f_ref[i + 3]))

    for i in range(L):
        u1 = u_ref[i + 4]
        g = state_ref[i + 4] + b[0] * zc_ref[i] + b[1] * ozc_ref[i]
        base_ref[i] = u1 - weight * g
        for p in range(PRONY):
            h = jnp.concatenate([own_ref[q, 2 + p, i] for q in range(chunks)], axis=0)
            h1 = decay_f[p] * h + rest_f[p] * u1
            gh = decay_c[p] * h + rest_c[p] * g
            base_ref[L * (1 + p) + i] = decay_f[p] * h1 + rest_f[p] * u1 - weight * gh

    def put_oz(i, plane):
        oz = inv_f_ref[i + 3] * plane
        oz_ref[i + 2] = oz
        if 0 <= i < L:
            oz_out[i] = oz
            acc[1] = acc[1] + z_ref[i + 3] * plane
            acc[2] = acc[2] + oz * plane

    off_diagonal(sh, lambda i: z_ref[i + 3], k, -2, 4, put_oz)

    def put_ooz(i, plane):
        ooz = inv_f_ref[i + 3] * plane
        ooz_ref[i + 1] = ooz
        if 0 <= i < L:
            ooz_out[i] = ooz
            acc[3] = acc[3] + oz_ref[i + 2] * plane
            acc[4] = acc[4] + ooz * plane

    off_diagonal(sh, lambda i: oz_ref[i + 2], k, -1, 3, put_ooz)

    def put_last(i, plane):
        acc[5] = acc[5] + ooz_ref[i + 1] * plane

    off_diagonal(sh, lambda i: ooz_ref[i + 1], k, 0, 2, put_last)
    moments_out(acc, red_ref)


def block_kernel(heat_ref, coef_ref, time_ref, red_in, base_ref, z_ref, oz_ref, ooz_ref, blk_ref):
    decay_f, rest_f, ff, shift_f = prony(1.0, coef_ref, time_ref)
    c = galerkin(moments_in(red_in, 0, 6))
    ny = z_ref.shape[1]
    for i in range(L):
        delta = c[0] * z_ref[i] + c[1] * oz_ref[i] + c[2] * ooz_ref[i]
        blk_ref[i * ny : (i + 1) * ny] = base_ref[i] + delta
        for p in range(PRONY):
            at = L * (1 + p) + i
            blk_ref[at * ny : (at + 1) * ny] = base_ref[at] + rest_f[p] * delta
    blk_ref[4 * L * ny :] = jnp.full((8, blk_ref.shape[1]), heat_ref[0, PACES - 1], jnp.float32)


def halo_base(f, base_ref):
    sums = [
        f[0] * base_ref[L + i] + f[1] * base_ref[2 * L + i] + f[2] * base_ref[3 * L + i]
        for i in range(L)
    ]
    u = [base_ref[i] for i in range(L)]
    return u + [sums[0], sums[1]], u + [sums[1], sums[2]]


def opening_kernel(coef_ref, time_ref, place_ref, blk_ref, base_ref, even_out, odd_out):
    decay, rest, f, shift = prony(1.0 * PACES, coef_ref, time_ref)
    ny = even_out.shape[1]
    for at in range(4 * L):
        base_ref[at] = blk_ref[at * ny : (at + 1) * ny]
    lo, hi = halo_base(f, base_ref)
    send(place_ref[1], lo, hi, even_out, odd_out)


def chain_kernel(turn, count, opened, *refs):
    refs = list(refs)
    coef_ref, time_ref, place_ref = refs[:3]
    refs = refs[3:]
    if opened:
        base_in, even_ref, odd_ref = refs[:3]
        refs = refs[3:]
    else:
        red_in, base_in, z_in, oz_in, even_ref, odd_ref = refs[:6]
        refs = refs[6:]
    kel_ref, theta_ref, inv_ref, blk_ref = refs[:4]
    base_ref, z_ref, oz_ref, even_out, odd_out, red_ref, u_ref, au_ref = refs[4:]
    ny, nz = kel_ref.shape[1:]
    sh = Shifts(ny, nz)
    decay, rest, f, shift = prony(1.0 * PACES, coef_ref, time_ref)
    grow = f[0] * rest[0] + f[1] * rest[1] + f[2] * rest[2]
    step = lax.rem(place_ref[0] + turn, count)
    heat = blk_ref[4 * L * ny : 4 * L * ny + 1]
    opening = step == 0
    fresh = step == 1
    side = place_ref[1]

    if not opened:
        c = galerkin(moments_in(red_in, 0, 4))

    def near(i, low_at, high_at):
        if i < 0:
            return below(side, even_ref, odd_ref, low_at)
        return above(side, even_ref, odd_ref, high_at)

    def delta(i):
        z = z_in[i + 2] if -2 <= i <= 4 else near(i, 5, 5)
        if -1 <= i <= 3:
            oz = oz_in[i + 1]
        else:
            at = 6 if i in (-3, 5) else 7
            oz = near(i, at, at)
        return jnp.where(fresh, 0.0, c[0] * z + c[1] * oz)

    for i in range(-3, 6):
        base = base_in[i] if 0 <= i < L else near(i, i + 3, i - L)
        d = None if opened else delta(i)
        u_ref[i + 3] = base if opened else base + d
        if 0 <= i < L:
            h = [base_in[L * (1 + p) + i] for p in range(PRONY)]
            if not opened:
                h = [h[p] + rest[p] * d for p in range(PRONY)]
            total = f[0] * h[0] + f[1] * h[1] + f[2] * h[2]
            ui = u_ref[i + 3]
            base_ref[i] = jnp.where(opening, 0.0, ui) + blk_ref[i * ny : (i + 1) * ny]
            for p in range(PRONY):
                at = L * (1 + p) + i
                ahead = jnp.where(opening, 0.0, decay[p] * h[p] + rest[p] * ui)
                base_ref[at] = ahead + blk_ref[at * ny : (at + 1) * ny]
        elif -2 <= i < 5:
            total = near(i, 3 + i + 2, 3 + i - L)
            if not opened:
                total = total + grow * d
        if -2 <= i < 5:
            au_ref[i + 2] = heat * theta_ref[i + 3] + total

    zeros = jnp.zeros((ny, nz), jnp.float32)
    acc = [zeros] * 4

    def k(e):
        return kel_ref[e + 4]

    def put_z(i, plane):
        ui = u_ref[i + 3]
        s = au_ref[i + 2] + ui * (1.0 / PACES) - plane
        inv = inv_ref[i + 3]
        z = inv * s - ui
        z_ref[i + 2] = z
        if 0 <= i < L:
            acc[0] = acc[0] + z * (s - ui * (1.0 / inv))

    off_diagonal(sh, lambda i: u_ref[i + 3], k, -2, 4, put_z)

    def put_oz(i, plane):
        oz = inv_ref[i + 3] * plane
        oz_ref[i + 1] = oz
        if 0 <= i < L:
            acc[1] = acc[1] + z_ref[i + 2] * plane
            acc[2] = acc[2] + oz * plane

    off_diagonal(sh, lambda i: z_ref[i + 2], k, -1, 3, put_oz)

    def put_last(i, plane):
        acc[3] = acc[3] + oz_ref[i + 1] * plane

    off_diagonal(sh, lambda i: oz_ref[i + 1], k, 0, 2, put_last)
    moments_out(acc, red_ref)

    lo, hi = halo_base(f, base_ref)
    lo = lo + [z_ref[2 + 2], oz_ref[2 + 1], oz_ref[1 + 1]]
    hi = hi + [z_ref[0 + 2], oz_ref[0 + 1], oz_ref[1 + 1]]
    send(side, lo, hi, even_out, odd_out)


def closing_kernel(coef_ref, time_ref, place_ref, red_in, base_ref, z_ref, oz_ref, out_ref):
    decay, rest, f, shift = prony(1.0 * PACES, coef_ref, time_ref)
    c = galerkin(moments_in(red_in, 0, 4))
    first = place_ref[0] == 0
    chunks, _, _, rows, _ = out_ref.shape
    for i in range(L):
        delta = jnp.where(first, 0.0, c[0] * z_ref[i + 2] + c[1] * oz_ref[i + 1])
        fields = [base_ref[i] + delta]
        for p in range(PRONY):
            fields.append(base_ref[L * (1 + p) + i] + rest[p] * delta)
        for at, field in enumerate(fields):
            for q in range(chunks):
                out_ref[q, at, i] = field[q * rows : (q + 1) * rows]


def layers_of(place_ref, q, chunks):
    return jnp.where(place_ref[3] == 0, q, chunks - 1 - q) * L


def gather_kernel(place_ref, parts_ref, out_ref):
    chunks = parts_ref.shape[0]
    for q in range(chunks):
        first = layers_of(place_ref, q, chunks)
        for i in range(L):
            for field in range(1 + PRONY):
                out_ref[0, field, first + i] = parts_ref[q, field, i]


def spread_kernel(place_ref, label_ref, values_ref, out_ref):
    chunks = out_ref.shape[0]
    for q in range(chunks):
        first = layers_of(place_ref, q, chunks)
        for i in range(L):
            out_ref[q, 0, i] = label_ref[first + i].astype(jnp.float32) + 1.0
            for field in range(1 + PRONY):
                out_ref[q, 1 + field, i] = values_ref[0, field, first + i]


SMEM = pl.BlockSpec(memory_space=pltpu.SMEM)
VMEM = pl.BlockSpec(memory_space=pltpu.VMEM)


def call(kernel, name, small, large, outs, scratch=()):
    f32 = jnp.float32
    return pl.pallas_call(
        kernel,
        name=name,
        out_shape=[jax.ShapeDtypeStruct(s, f32) for s in outs],
        in_specs=[SMEM] * len(small) + [VMEM] * len(large),
        out_specs=[VMEM] * len(outs),
        scratch_shapes=[pltpu.VMEM(s, f32) for s in scratch],
        compiler_params=pltpu.CompilerParams(vmem_limit_bytes=LIMIT),
    )(*small, *large)


def on_device(
    segment_opening_values,
    cell_material_label,
    material_rigidity,
    dilation_mismatch,
    heat_swings_array,
    prony_coefficients,
    prony_decay_times,
):
    n_tm, n_gy = lax.axis_size("tm"), lax.axis_size("gy")
    line = lax.axis_size("gx") * n_gy
    nx, ny_part, nz = cell_material_label.shape
    ny = ny_part * n_gy
    assert nx == L * n_gy
    plane = (ny, nz)

    def device(position):
        row, column = divmod(position, n_gy)
        return row * n_gy + (column if row % 2 == 0 else n_gy - 1 - column)

    def trade(even, odd, by):
        received = []
        for side, value in enumerate((even, odd)):
            pairs = [(p, p + by) for p in range(line - by) if p // by % 2 == side]
            both = pairs + [(b, a) for a, b in pairs]
            perm = sorted((device(a), device(b)) for a, b in both)
            received.append(lax.ppermute(value, LINE, perm))
        return received

    def exchanged(red):
        return lax.all_to_all(red, LINE, 0, 0, tiled=True)

    def ring(block):
        return lax.ppermute(block, "tm", [(s, (s - 1) % n_tm) for s in range(n_tm)])

    gx, gy = lax.axis_index("gx"), lax.axis_index("gy")
    flip = gx % 2
    position = gx * n_gy + jnp.where(flip == 0, gy, n_gy - 1 - gy)
    place = jnp.stack([lax.axis_index("tm"), position % 2, position // 2 % 2, flip])
    place = place.astype(jnp.int32)
    prony_args = (prony_coefficients, prony_decay_times)

    (raw,) = call(
        spread_kernel,
        "spread",
        (place,),
        (cell_material_label, segment_opening_values),
        [(n_gy, 2 + PRONY, L, ny_part, nz)],
    )
    own = lax.all_to_all(raw, "gy", 0, 0, tiled=True)
    near = trade(own, own, 1)
    top, bottom = own[:, :2, L - 1 :], own[:, :2, :1]
    upward = position // 2 % 2 == 0
    far = trade(jnp.where(upward, top, bottom), jnp.where(upward, bottom, top), 2)

    red_shape = (line, 1, 128)
    (kel, theta, inv_f, inv_c, state, zf, ozf, oozf, zc, ozc, even, odd, even2, odd2, red) = call(
        start_kernel,
        "start",
        (material_rigidity, dilation_mismatch, heat_swings_array, *prony_args, place),
        (own, *near, *far),
        [
            (10, *plane), (9, *plane), (9, *plane), (9, *plane), (20, *plane),
            (9, *plane), (7, *plane), (5, *plane), (L, *plane), (L, *plane),
            (3, *plane), (3, *plane), (3, *plane), (3, *plane), red_shape,
        ],
        [(10, *plane), (9, *plane), (7, *plane)],
    )
    red = exchanged(red)
    near, far = trade(even, odd, 1), trade(even2, odd2, 2)
    base, z, oz, ooz, red = call(
        second_kernel,
        "second",
        (heat_swings_array, *prony_args, place),
        (red, kel, theta, inv_f, state, own, zf, ozf, oozf, zc, ozc, *near, *far),
        [(4 * L, *plane), (L, *plane), (L, *plane), (L, *plane), red_shape],
        [(11, *plane), (9, *plane), (7, *plane), (5, *plane), (9, *plane)],
    )
    red = exchanged(red)
    (block,) = call(
        block_kernel,
        "block",
        (heat_swings_array, *prony_args),
        (red, base, z, oz, ooz),
        [(4 * L * ny + 8, nz)],
    )
    mine = block
    block = ring(block)
    base, even, odd = call(
        opening_kernel,
        "opening",
        (*prony_args, place),
        (block,),
        [(4 * L, *plane), (5, *plane), (5, *plane)],
    )
    past = (base,)
    for turn in range(2, n_tm + 1):
        if turn < n_tm:
            block, even = lax.optimization_barrier((block, even))
            block = ring(block)
        else:
            block = mine
        past = (*past, *trade(even, odd, 1))
        base, z, oz, even, odd, red = call(
            functools.partial(chain_kernel, turn, n_tm, turn == 2),
            f"chain{turn}",
            (*prony_args, place),
            (*past, kel, theta, inv_c, block),
            [(4 * L, *plane), (7, *plane), (5, *plane), (8, *plane), (8, *plane), red_shape],
            [(9, *plane), (7, *plane)],
        )
        past = (exchanged(red), base, z, oz)
    (parts,) = call(
        closing_kernel,
        "closing",
        (*prony_args, place),
        past,
        [(n_gy, 1 + PRONY, L, ny_part, nz)],
    )
    parts = lax.all_to_all(parts, "gy", 0, 0, tiled=True)
    (out,) = call(
        gather_kernel, "gather", (place,), (parts,), [(1, 1 + PRONY, nx, ny_part, nz)]
    )
    return out


def solution(mesh):
    placed = (
        P("tm", None, "gx", "gy", None),
        P("gx", "gy", None),
        P(),
        P(),
        P("tm", None),
        P(),
        P(),
    )
    return jax.shard_map(
        on_device,
        mesh=mesh,
        in_specs=placed,
        out_specs=P("tm", None, "gx", "gy", None),
        check_vma=False,
    )
```

```python
import functools

import jax
import jax.numpy as jnp
from jax import lax
from jax.experimental import pallas as pl
from jax.experimental.pallas import tpu as pltpu
from jax.sharding import PartitionSpec as P

PACES = 2
SHARP = 3
LOOSE = 2
PRONY = 3
L = 3
LINE = ("gx", "gy")
LIMIT = 14 << 20


def masks(ny, nz):
    row = lax.broadcasted_iota(jnp.int32, (ny, nz), 0)
    lane = lax.broadcasted_iota(jnp.int32, (ny, nz), 1)
    return row == 0, row == ny - 1, lane == 0, lane == nz - 1


class Shifts:
    def __init__(self, ny, nz):
        self.ny, self.nz = ny, nz
        self.row_first, self.row_last, self.lane_first, self.lane_last = masks(ny, nz)

    def zup(self, v):
        return jnp.where(self.lane_last, 0.0, pltpu.roll(v, self.nz - 1, 1))

    def zdn(self, v):
        return jnp.where(self.lane_first, 0.0, pltpu.roll(v, 1, 1))

    def yup(self, v):
        return jnp.where(self.row_last, 0.0, pltpu.roll(v, self.ny - 1, 0))

    def ydn(self, v):
        return jnp.where(self.row_first, 0.0, pltpu.roll(v, 1, 0))


def off_diagonal(sh, v, k, low, high, put):
    def spread(plane):
        up = sh.zup(plane)
        side, side_up = sh.yup(plane), sh.yup(up)
        return plane, up, side, side_up, plane + up, side + side_up

    near = spread(v(low - 1))
    carry = None
    for e in range(low - 1, high + 1):
        far = spread(v(e + 1))
        a, a_up, b, b_up, a_sum, b_sum = near
        c, c_up, d, d_up, c_sum, d_sum = far
        one_up, two_up = b_up + c_up, a_up + d_up
        one, two = b + c, a + d
        kk = k(e)
        if e >= low:
            e00, f00 = kk * (d_sum + one_up), kk * (d_sum + one)
            e01, f01 = kk * (c_sum + two_up), kk * (c_sum + two)
            e10, e11, f10, f11 = carry
            put(e, (e00 + e10) + sh.ydn(e01 + e11) + sh.zdn((f00 + f10) + sh.ydn(f01 + f11)))
        if e < high:
            carry = (
                kk * (b_sum + two_up),
                kk * (a_sum + one_up),
                kk * (b_sum + two),
                kk * (a_sum + one),
            )
        near = far


def prony(dt, coef_ref, time_ref):
    decay = [jnp.exp(-dt / jnp.full((1, 128), time_ref[p], jnp.float32)) for p in range(PRONY)]
    rest = [1.0 - d for d in decay]
    f = [coef_ref[p] * decay[p] for p in range(PRONY)]
    return decay, rest, f, 1.0 / dt + (f[0] + f[1] + f[2])


def moments_out(values, red_ref):
    lane = lax.broadcasted_iota(jnp.int32, (1, 128), 1)
    packed = jnp.zeros((1, 128), jnp.float32)
    for at, field in enumerate(values):
        total = jnp.sum(jnp.sum(field, axis=0, keepdims=True), axis=1, keepdims=True)
        packed = jnp.where(lane == at, total, packed)
    red_ref[...] = jnp.broadcast_to(packed[None], red_ref.shape)


def moments_in(red_ref, first, count):
    total = jnp.sum(red_ref[...], axis=0)
    lane = lax.broadcasted_iota(jnp.int32, (1, 128), 1)
    return [
        jnp.broadcast_to(
            jnp.sum(jnp.where(lane == first + i, total, 0.0), axis=1, keepdims=True), (1, 128)
        )
        for i in range(count)
    ]


def galerkin(nu):
    m = len(nu) // 2
    mu = [nu[i] + nu[i + 1] for i in range(2 * m - 1)]
    rows = [[mu[i + j] for j in range(m)] + [nu[i]] for i in range(m)]
    for i in range(m):
        for r in range(i + 1, m):
            factor = rows[r][i] / rows[i][i]
            for j in range(i + 1, m + 1):
                rows[r][j] = rows[r][j] - factor * rows[i][j]
    c = [None] * m
    for i in reversed(range(m)):
        acc = rows[i][m]
        for j in range(i + 1, m):
            acc = acc - rows[i][j] * c[j]
        c[i] = acc / rows[i][i]
    return c


def send(odd_side, lo, hi, even_out, odd_out):
    for at, (low, high) in enumerate(zip(lo, hi)):
        even_out[at] = jnp.where(odd_side == 0, high, low)
        odd_out[at] = jnp.where(odd_side == 0, low, high)


def below(odd_side, even_ref, odd_ref, at):
    return jnp.where(odd_side == 0, odd_ref[at], even_ref[at])


def above(odd_side, even_ref, odd_ref, at):
    return jnp.where(odd_side == 0, even_ref[at], odd_ref[at])


def start_kernel(
    rigid_ref, dilate_ref, heat_ref, coef_ref, time_ref, place_ref,
    own_ref, even_ref, odd_ref, even2_ref, odd2_ref,
    kel_ref, theta_ref, inv_f_ref, inv_c_ref, state_ref,
    zf_ref, ozf_ref, oozf_ref, zc_ref, ozc_ref,
    even_out, odd_out, even2_out, odd2_out, red_ref,
    kal_ref, au_ref, w_ref,
):
    ny, nz = kel_ref.shape[1:]
    sh = Shifts(ny, nz)
    chunks = own_ref.shape[0]

    def raw(field, i):
        if i == -L - 1:
            parts = [below(place_ref[2], even2_ref, odd2_ref, (c, field, 0)) for c in range(chunks)]
        elif i < 0:
            parts = [below(place_ref[1], even_ref, odd_ref, (c, field, i + L)) for c in range(chunks)]
        elif i < L:
            parts = [own_ref[c, field, i] for c in range(chunks)]
        elif i < 2 * L:
            parts = [above(place_ref[1], even_ref, odd_ref, (c, field, i - L)) for c in range(chunks)]
        else:
            parts = [above(place_ref[2], even2_ref, odd2_ref, (c, field, 0)) for c in range(chunks)]
        return jnp.concatenate(parts, axis=0)

    for e in range(-4, 6):
        label = raw(0, e)
        stiff = jnp.zeros((ny, nz), jnp.float32)
        load = jnp.zeros((ny, nz), jnp.float32)
        for region in range(rigid_ref.shape[0]):
            here = label == (region + 1.0)
            stiff = jnp.where(here, rigid_ref[region], stiff)
            load = jnp.where(here, dilate_ref[region], load)
        kel_ref[e + 4] = stiff * (-1.0 / 12.0)
        kal_ref[e + 4] = 0.25 * (stiff * load)

    decay_f, rest_f, ff, shift_f = prony(1.0, coef_ref, time_ref)
    decay_c, rest_c, fc, shift_c = prony(1.0 * PACES, coef_ref, time_ref)

    for i in range(-3, 6):
        ksum = kel_ref[i + 3] + kel_ref[i + 4]
        ksum = ksum + sh.ydn(ksum)
        ksum = ksum + sh.zdn(ksum)
        diag = -4.0 * ksum
        asum = kal_ref[i + 3] + kal_ref[i + 4]
        asum = asum + sh.ydn(asum)
        theta_ref[i + 3] = sh.zdn(asum) - asum
        inside = raw(0, i) > 0.5
        inv_f_ref[i + 3] = jnp.where(inside, 1.0 / (diag + shift_f), 0.0)
        inv_c_ref[i + 3] = jnp.where(inside, 1.0 / (diag + shift_c), 0.0)

    for i in range(-4, 7):
        state_ref[i + 4] = raw(1, i)

    def u(i):
        return state_ref[i + 4]

    def k(e):
        return kel_ref[e + 4]

    def put_au(i, plane):
        au_ref[i + 3] = plane

    off_diagonal(sh, u, k, -3, 5, put_au)

    zeros = jnp.zeros((ny, nz), jnp.float32)
    acc = [zeros] * 10
    for i in range(-3, 6):
        h = [raw(2 + p, i) for p in range(PRONY)]
        fh = [ff[p] * h[p] for p in range(PRONY)]
        state_ref[11 + i + 3] = decay_f[0] * fh[0] + decay_f[1] * fh[1] + decay_f[2] * fh[2]
        ui = u(i)
        load = heat_ref[0, 0] * theta_ref[i + 3] + (fh[0] + fh[1] + fh[2])
        s = load + ui - au_ref[i + 3]
        z = inv_f_ref[i + 3] * s - ui
        zf_ref[i + 3] = z
        if 0 <= i < L:
            acc[0] = acc[0] + z * (s - ui * (1.0 / inv_f_ref[i + 3]))
        if -2 <= i < 5:
            load = heat_ref[0, 1] * theta_ref[i + 3]
            load = load + (fc[0] * h[0] + fc[1] * h[1] + fc[2] * h[2])
            s = load + ui * (1.0 / PACES) - au_ref[i + 3]
            z = inv_c_ref[i + 3] * s - ui
            w_ref[i + 2] = z
            if 0 <= i < L:
                zc_ref[i] = z
                acc[6] = acc[6] + z * (s - ui * (1.0 / inv_c_ref[i + 3]))

    def put_oz(i, plane):
        oz = inv_f_ref[i + 3] * plane
        ozf_ref[i + 2] = oz
        if 0 <= i < L:
            acc[1] = acc[1] + zf_ref[i + 3] * plane
            acc[2] = acc[2] + oz * plane

    off_diagonal(sh, lambda i: zf_ref[i + 3], k, -2, 4, put_oz)

    def put_ooz(i, plane):
        ooz = inv_f_ref[i + 3] * plane
        oozf_ref[i + 1] = ooz
        if 0 <= i < L:
            acc[3] = acc[3] + ozf_ref[i + 2] * plane
            acc[4] = acc[4] + ooz * plane

    off_diagonal(sh, lambda i: ozf_ref[i + 2], k, -1, 3, put_ooz)

    def put_last(i, plane):
        acc[5] = acc[5] + oozf_ref[i + 1] * plane

    off_diagonal(sh, lambda i: oozf_ref[i + 1], k, 0, 2, put_last)

    def put_ozc(i, plane):
        oz = inv_c_ref[i + 3] * plane
        au_ref[i + 3] = oz
        if 0 <= i < L:
            ozc_ref[i] = oz
            acc[7] = acc[7] + w_ref[i + 2] * plane
            acc[8] = acc[8] + oz * plane

    off_diagonal(sh, lambda i: w_ref[i + 2], k, -1, 3, put_ozc)

    def put_lastc(i, plane):
        acc[9] = acc[9] + au_ref[i + 3] * plane

    off_diagonal(sh, lambda i: au_ref[i + 3], k, 0, 2, put_lastc)

    moments_out(acc, red_ref)

    lo1 = [ozf_ref[2 + 2], oozf_ref[1 + 1], oozf_ref[2 + 1]]
    hi1 = [ozf_ref[0 + 2], oozf_ref[0 + 1], oozf_ref[1 + 1]]
    lo2 = [zf_ref[0 + 3], ozf_ref[0 + 2], oozf_ref[0 + 1]]
    hi2 = [zf_ref[2 + 3], ozf_ref[2 + 2], oozf_ref[2 + 1]]
    send(place_ref[1], lo1, hi1, even_out, odd_out)
    send(place_ref[2], lo2, hi2, even2_out, odd2_out)


def second_kernel(
    heat_ref, coef_ref, time_ref, place_ref,
    red_in, kel_ref, theta_ref, inv_f_ref, state_ref, own_ref,
    zf_ref, ozf_ref, oozf_ref, zc_ref, ozc_ref,
    even_ref, odd_ref, even2_ref, odd2_ref,
    base_ref, z_out, oz_out, ooz_out, red_ref,
    u_ref, z_ref, oz_ref, ooz_ref, au_ref,
):
    ny, nz = kel_ref.shape[1:]
    sh = Shifts(ny, nz)
    chunks = own_ref.shape[0]
    decay_f, rest_f, ff, shift_f = prony(1.0, coef_ref, time_ref)
    decay_c, rest_c, fc, shift_c = prony(1.0 * PACES, coef_ref, time_ref)
    c = galerkin(moments_in(red_in, 0, 6))
    b = galerkin(moments_in(red_in, 6, 4))

    near, far = place_ref[1], place_ref[2]

    def basis(i, at, ref, reach):
        if i == -4:
            return below(far, even2_ref, odd2_ref, at)
        if i == 6:
            return above(far, even2_ref, odd2_ref, at)
        if -reach <= i <= L - 1 + reach:
            return ref[i + reach]
        if at == 1:
            return (below if i < 0 else above)(near, even_ref, odd_ref, 0)
        if i < 0:
            return below(near, even_ref, odd_ref, i + 4)
        return above(near, even_ref, odd_ref, i - 3)

    for i in range(-4, 7):
        z, oz, ooz = basis(i, 0, zf_ref, 3), basis(i, 1, ozf_ref, 2), basis(i, 2, oozf_ref, 1)
        u_ref[i + 4] = state_ref[i + 4] + c[0] * z + c[1] * oz + c[2] * ooz

    def k(e):
        return kel_ref[e + 4]

    def put_au(i, plane):
        au_ref[i + 3] = plane

    off_diagonal(sh, lambda i: u_ref[i + 4], k, -3, 5, put_au)

    grow = ff[0] * rest_f[0] + ff[1] * rest_f[1] + ff[2] * rest_f[2]
    zeros = jnp.zeros((ny, nz), jnp.float32)
    acc = [zeros] * 6
    weight = jnp.where(place_ref[0] == 0, 0.0, 1.0)
    for i in range(-3, 6):
        ui = u_ref[i + 4]
        s = heat_ref[0, 1] * theta_ref[i + 3] + state_ref[11 + i + 3] + (grow + 1.0) * ui
        s = s - au_ref[i + 3]
        z = inv_f_ref[i + 3] * s - ui
        z_ref[i + 3] = z
        if 0 <= i < L:
            z_out[i] = z
            acc[0] = acc[0] + z * (s - ui * (1.0 / inv_f_ref[i + 3]))

    for i in range(L):
        u1 = u_ref[i + 4]
        g = state_ref[i + 4] + b[0] * zc_ref[i] + b[1] * ozc_ref[i]
        base_ref[i] = u1 - weight * g
        for p in range(PRONY):
            h = jnp.concatenate([own_ref[q, 2 + p, i] for q in range(chunks)], axis=0)
            h1 = decay_f[p] * h + rest_f[p] * u1
            gh = decay_c[p] * h + rest_c[p] * g
            base_ref[L * (1 + p) + i] = decay_f[p] * h1 + rest_f[p] * u1 - weight * gh

    def put_oz(i, plane):
        oz = inv_f_ref[i + 3] * plane
        oz_ref[i + 2] = oz
        if 0 <= i < L:
            oz_out[i] = oz
            acc[1] = acc[1] + z_ref[i + 3] * plane
            acc[2] = acc[2] + oz * plane

    off_diagonal(sh, lambda i: z_ref[i + 3], k, -2, 4, put_oz)

    def put_ooz(i, plane):
        ooz = inv_f_ref[i + 3] * plane
        ooz_ref[i + 1] = ooz
        if 0 <= i < L:
            ooz_out[i] = ooz
            acc[3] = acc[3] + oz_ref[i + 2] * plane
            acc[4] = acc[4] + ooz * plane

    off_diagonal(sh, lambda i: oz_ref[i + 2], k, -1, 3, put_ooz)

    def put_last(i, plane):
        acc[5] = acc[5] + ooz_ref[i + 1] * plane

    off_diagonal(sh, lambda i: ooz_ref[i + 1], k, 0, 2, put_last)
    moments_out(acc, red_ref)


def block_kernel(heat_ref, coef_ref, time_ref, red_in, base_ref, z_ref, oz_ref, ooz_ref, blk_ref):
    decay_f, rest_f, ff, shift_f = prony(1.0, coef_ref, time_ref)
    c = galerkin(moments_in(red_in, 0, 6))
    ny = z_ref.shape[1]
    for i in range(L):
        delta = c[0] * z_ref[i] + c[1] * oz_ref[i] + c[2] * ooz_ref[i]
        blk_ref[i * ny : (i + 1) * ny] = base_ref[i] + delta
        for p in range(PRONY):
            at = L * (1 + p) + i
            blk_ref[at * ny : (at + 1) * ny] = base_ref[at] + rest_f[p] * delta
    blk_ref[4 * L * ny :] = jnp.full((8, blk_ref.shape[1]), heat_ref[0, PACES - 1], jnp.float32)


def halo_base(f, base_ref):
    sums = [
        f[0] * base_ref[L + i] + f[1] * base_ref[2 * L + i] + f[2] * base_ref[3 * L + i]
        for i in range(L)
    ]
    u = [base_ref[i] for i in range(L)]
    return u + [sums[0], sums[1]], u + [sums[1], sums[2]]


def opening_kernel(coef_ref, time_ref, place_ref, blk_ref, base_ref, even_out, odd_out):
    decay, rest, f, shift = prony(1.0 * PACES, coef_ref, time_ref)
    ny = even_out.shape[1]
    for at in range(4 * L):
        base_ref[at] = blk_ref[at * ny : (at + 1) * ny]
    lo, hi = halo_base(f, base_ref)
    send(place_ref[1], lo, hi, even_out, odd_out)


def chain_kernel(turn, count, opened, *refs):
    refs = list(refs)
    coef_ref, time_ref, place_ref = refs[:3]
    refs = refs[3:]
    if opened:
        base_in, even_ref, odd_ref = refs[:3]
        refs = refs[3:]
    else:
        red_in, base_in, z_in, oz_in, even_ref, odd_ref = refs[:6]
        refs = refs[6:]
    kel_ref, theta_ref, inv_ref, blk_ref = refs[:4]
    base_ref, z_ref, oz_ref, even_out, odd_out, red_ref, u_ref, au_ref = refs[4:]
    ny, nz = kel_ref.shape[1:]
    sh = Shifts(ny, nz)
    decay, rest, f, shift = prony(1.0 * PACES, coef_ref, time_ref)
    grow = f[0] * rest[0] + f[1] * rest[1] + f[2] * rest[2]
    step = lax.rem(place_ref[0] + turn, count)
    heat = blk_ref[4 * L * ny : 4 * L * ny + 1]
    opening = step == 0
    fresh = step == 1
    side = place_ref[1]

    if not opened:
        c = galerkin(moments_in(red_in, 0, 4))

    def near(i, low_at, high_at):
        if i < 0:
            return below(side, even_ref, odd_ref, low_at)
        return above(side, even_ref, odd_ref, high_at)

    def delta(i):
        z = z_in[i + 2] if -2 <= i <= 4 else near(i, 5, 5)
        if -1 <= i <= 3:
            oz = oz_in[i + 1]
        else:
            at = 6 if i in (-3, 5) else 7
            oz = near(i, at, at)
        return jnp.where(fresh, 0.0, c[0] * z + c[1] * oz)

    for i in range(-3, 6):
        base = base_in[i] if 0 <= i < L else near(i, i + 3, i - L)
        d = None if opened else delta(i)
        u_ref[i + 3] = base if opened else base + d
        if 0 <= i < L:
            h = [base_in[L * (1 + p) + i] for p in range(PRONY)]
            if not opened:
                h = [h[p] + rest[p] * d for p in range(PRONY)]
            total = f[0] * h[0] + f[1] * h[1] + f[2] * h[2]
            ui = u_ref[i + 3]
            base_ref[i] = jnp.where(opening, 0.0, ui) + blk_ref[i * ny : (i + 1) * ny]
            for p in range(PRONY):
                at = L * (1 + p) + i
                ahead = jnp.where(opening, 0.0, decay[p] * h[p] + rest[p] * ui)
                base_ref[at] = ahead + blk_ref[at * ny : (at + 1) * ny]
        elif -2 <= i < 5:
            total = near(i, 3 + i + 2, 3 + i - L)
            if not opened:
                total = total + grow * d
        if -2 <= i < 5:
            au_ref[i + 2] = heat * theta_ref[i + 3] + total

    zeros = jnp.zeros((ny, nz), jnp.float32)
    acc = [zeros] * 4

    def k(e):
        return kel_ref[e + 4]

    def put_z(i, plane):
        ui = u_ref[i + 3]
        s = au_ref[i + 2] + ui * (1.0 / PACES) - plane
        inv = inv_ref[i + 3]
        z = inv * s - ui
        z_ref[i + 2] = z
        if 0 <= i < L:
            acc[0] = acc[0] + z * (s - ui * (1.0 / inv))

    off_diagonal(sh, lambda i: u_ref[i + 3], k, -2, 4, put_z)

    def put_oz(i, plane):
        oz = inv_ref[i + 3] * plane
        oz_ref[i + 1] = oz
        if 0 <= i < L:
            acc[1] = acc[1] + z_ref[i + 2] * plane
            acc[2] = acc[2] + oz * plane

    off_diagonal(sh, lambda i: z_ref[i + 2], k, -1, 3, put_oz)

    def put_last(i, plane):
        acc[3] = acc[3] + oz_ref[i + 1] * plane

    off_diagonal(sh, lambda i: oz_ref[i + 1], k, 0, 2, put_last)
    moments_out(acc, red_ref)

    lo, hi = halo_base(f, base_ref)
    lo = lo + [z_ref[2 + 2], oz_ref[2 + 1], oz_ref[1 + 1]]
    hi = hi + [z_ref[0 + 2], oz_ref[0 + 1], oz_ref[1 + 1]]
    send(side, lo, hi, even_out, odd_out)


def closing_kernel(coef_ref, time_ref, place_ref, red_in, base_ref, z_ref, oz_ref, out_ref):
    decay, rest, f, shift = prony(1.0 * PACES, coef_ref, time_ref)
    c = galerkin(moments_in(red_in, 0, 4))
    first = place_ref[0] == 0
    chunks, _, _, rows, _ = out_ref.shape
    for i in range(L):
        delta = jnp.where(first, 0.0, c[0] * z_ref[i + 2] + c[1] * oz_ref[i + 1])
        fields = [base_ref[i] + delta]
        for p in range(PRONY):
            fields.append(base_ref[L * (1 + p) + i] + rest[p] * delta)
        for at, field in enumerate(fields):
            for q in range(chunks):
                out_ref[q, at, i] = field[q * rows : (q + 1) * rows]


def chip_of(place_ref, x, chips):
    return jnp.where(place_ref[3] == 0, x, chips - 1 - x)


def spread_kernel(place_ref, label_ref, values_ref, keep_out, send_out):
    core = place_ref[1]
    for j in range(keep_out.shape[0]):
        for out_ref, first in ((keep_out, (2 * j + core) * L), (send_out, (2 * j + 1 - core) * L)):
            for i in range(L):
                out_ref[j, 0, i] = label_ref[first + i].astype(jnp.float32) + 1.0
                for field in range(1 + PRONY):
                    out_ref[j, 1 + field, i] = values_ref[0, field, first + i]


def join_kernel(place_ref, keep_ref, got_ref, out_ref):
    core, chips, half = place_ref[1], out_ref.shape[0], keep_ref.shape[0]
    for j in range(half):
        for ref, x in ((keep_ref, half * core + j), (got_ref, half * (1 - core) + j)):
            to = chip_of(place_ref, x, chips)
            for field in range(2 + PRONY):
                for i in range(L):
                    out_ref[to, field, i] = ref[j, field, i]


def gather_kernel(place_ref, parts_ref, got_ref, out_ref):
    core, chips, half = place_ref[1], parts_ref.shape[0], got_ref.shape[0]
    for j in range(half):
        own = chip_of(place_ref, half * core + j, chips)
        other = jnp.where(place_ref[3] == 0, j, half - 1 - j)
        for i in range(L):
            for field in range(1 + PRONY):
                out_ref[0, field, (2 * j + core) * L + i] = parts_ref[own, field, i]
                out_ref[0, field, (2 * j + 1 - core) * L + i] = got_ref[other, field, i]


SMEM = pl.BlockSpec(memory_space=pltpu.SMEM)
VMEM = pl.BlockSpec(memory_space=pltpu.VMEM)


def call(kernel, name, small, large, outs, scratch=()):
    f32 = jnp.float32
    return pl.pallas_call(
        kernel,
        name=name,
        out_shape=[jax.ShapeDtypeStruct(s, f32) for s in outs],
        in_specs=[SMEM] * len(small) + [VMEM] * len(large),
        out_specs=[VMEM] * len(outs),
        scratch_shapes=[pltpu.VMEM(s, f32) for s in scratch],
        compiler_params=pltpu.CompilerParams(vmem_limit_bytes=LIMIT),
    )(*small, *large)


def on_device(
    segment_opening_values,
    cell_material_label,
    material_rigidity,
    dilation_mismatch,
    heat_swings_array,
    prony_coefficients,
    prony_decay_times,
):
    n_tm, n_gy = lax.axis_size("tm"), lax.axis_size("gy")
    line = lax.axis_size("gx") * n_gy
    nx, ny_part, nz = cell_material_label.shape
    ny = ny_part * n_gy
    assert nx == L * n_gy
    plane = (ny, nz)

    def device(position):
        row, rest = divmod(position, 2 * n_gy)
        x, core = divmod(rest, 2)
        return (2 * row + core) * n_gy + (x if row % 2 == 0 else n_gy - 1 - x)

    def other_core(value):
        return lax.ppermute(value, "gx", [(p, p ^ 1) for p in range(line // n_gy)])

    def trade(even, odd, by):
        received = []
        for side, value in enumerate((even, odd)):
            pairs = [(p, p + by) for p in range(line - by) if p // by % 2 == side]
            both = pairs + [(b, a) for a, b in pairs]
            perm = sorted((device(a), device(b)) for a, b in both)
            received.append(lax.ppermute(value, LINE, perm))
        return received

    def exchanged(red):
        return lax.all_to_all(red, LINE, 0, 0, tiled=True)

    def ring(block):
        return lax.ppermute(block, "tm", [(s, (s - 1) % n_tm) for s in range(n_tm)])

    gx, gy = lax.axis_index("gx"), lax.axis_index("gy")
    core, flip = gx % 2, gx // 2 % 2
    x = jnp.where(flip == 0, gy, n_gy - 1 - gy)
    place = jnp.stack([lax.axis_index("tm"), core, x % 2, flip]).astype(jnp.int32)
    prony_args = (prony_coefficients, prony_decay_times)

    half = n_gy // 2
    keep, give = call(
        spread_kernel,
        "spread",
        (place,),
        (cell_material_label, segment_opening_values),
        [(half, 2 + PRONY, L, ny_part, nz)] * 2,
    )
    (raw,) = call(
        join_kernel,
        "join",
        (place,),
        (keep, other_core(give)),
        [(n_gy, 2 + PRONY, L, ny_part, nz)],
    )
    own = lax.all_to_all(raw, "gy", 0, 0, tiled=True)
    near = trade(own, own, 1)
    top, bottom = own[:, :2, L - 1 :], own[:, :2, :1]
    upward = x % 2 == 0
    far = trade(jnp.where(upward, top, bottom), jnp.where(upward, bottom, top), 2)

    red_shape = (line, 1, 128)
    (kel, theta, inv_f, inv_c, state, zf, ozf, oozf, zc, ozc, even, odd, even2, odd2, red) = call(
        start_kernel,
        "start",
        (material_rigidity, dilation_mismatch, heat_swings_array, *prony_args, place),
        (own, *near, *far),
        [
            (10, *plane), (9, *plane), (9, *plane), (9, *plane), (20, *plane),
            (9, *plane), (7, *plane), (5, *plane), (L, *plane), (L, *plane),
            (3, *plane), (3, *plane), (3, *plane), (3, *plane), red_shape,
        ],
        [(10, *plane), (9, *plane), (7, *plane)],
    )
    red = exchanged(red)
    near, far = trade(even, odd, 1), trade(even2, odd2, 2)
    base, z, oz, ooz, red = call(
        second_kernel,
        "second",
        (heat_swings_array, *prony_args, place),
        (red, kel, theta, inv_f, state, own, zf, ozf, oozf, zc, ozc, *near, *far),
        [(4 * L, *plane), (L, *plane), (L, *plane), (L, *plane), red_shape],
        [(11, *plane), (9, *plane), (7, *plane), (5, *plane), (9, *plane)],
    )
    red = exchanged(red)
    (block,) = call(
        block_kernel,
        "block",
        (heat_swings_array, *prony_args),
        (red, base, z, oz, ooz),
        [(4 * L * ny + 8, nz)],
    )
    mine = block
    block = ring(block)
    base, even, odd = call(
        opening_kernel,
        "opening",
        (*prony_args, place),
        (block,),
        [(4 * L, *plane), (5, *plane), (5, *plane)],
    )
    past = (base,)
    for turn in range(2, n_tm + 1):
        if turn < n_tm:
            block, even = lax.optimization_barrier((block, even))
            block = ring(block)
        else:
            block = mine
        past = (*past, *trade(even, odd, 1))
        base, z, oz, even, odd, red = call(
            functools.partial(chain_kernel, turn, n_tm, turn == 2),
            f"chain{turn}",
            (*prony_args, place),
            (*past, kel, theta, inv_c, block),
            [(4 * L, *plane), (7, *plane), (5, *plane), (8, *plane), (8, *plane), red_shape],
            [(9, *plane), (7, *plane)],
        )
        past = (exchanged(red), base, z, oz)
    (parts,) = call(
        closing_kernel,
        "closing",
        (*prony_args, place),
        past,
        [(n_gy, 1 + PRONY, L, ny_part, nz)],
    )
    parts = lax.all_to_all(parts, "gy", 0, 0, tiled=True)
    first = half * (1 - core)
    first = jnp.where(flip == 0, first, n_gy - half - first)
    got = other_core(lax.dynamic_slice_in_dim(parts, first, half, 0))
    (out,) = call(
        gather_kernel, "gather", (place,), (parts, got), [(1, 1 + PRONY, nx, ny_part, nz)]
    )
    return out


def solution(mesh):
    placed = (
        P("tm", None, "gx", "gy", None),
        P("gx", "gy", None),
        P(),
        P(),
        P("tm", None),
        P(),
        P(),
    )
    return jax.shard_map(
        on_device,
        mesh=mesh,
        in_specs=placed,
        out_specs=P("tm", None, "gx", "gy", None),
        check_vma=False,
    )
```

```python
import functools

import jax
import jax.numpy as jnp
from jax import lax
from jax.experimental import pallas as pl
from jax.experimental.pallas import tpu as pltpu
from jax.sharding import PartitionSpec as P

PACES = 2
SHARP = 3
LOOSE = 2
PRONY = 3
L = 3
LINE = ("gx", "gy")
LIMIT = 14 << 20


def masks(ny, nz):
    row = lax.broadcasted_iota(jnp.int32, (ny, nz), 0)
    lane = lax.broadcasted_iota(jnp.int32, (ny, nz), 1)
    return row == 0, row == ny - 1, lane == 0, lane == nz - 1


class Shifts:
    def __init__(self, ny, nz):
        self.ny, self.nz = ny, nz
        self.row_first, self.row_last, self.lane_first, self.lane_last = masks(ny, nz)

    def zup(self, v):
        return jnp.where(self.lane_last, 0.0, pltpu.roll(v, self.nz - 1, 1))

    def zdn(self, v):
        return jnp.where(self.lane_first, 0.0, pltpu.roll(v, 1, 1))

    def yup(self, v):
        return jnp.where(self.row_last, 0.0, pltpu.roll(v, self.ny - 1, 0))

    def ydn(self, v):
        return jnp.where(self.row_first, 0.0, pltpu.roll(v, 1, 0))


def off_diagonal(sh, v, k, low, high, put):
    def spread(plane):
        up = sh.zup(plane)
        side, side_up = sh.yup(plane), sh.yup(up)
        return plane, up, side, side_up, plane + up, side + side_up

    near = spread(v(low - 1))
    carry = None
    for e in range(low - 1, high + 1):
        far = spread(v(e + 1))
        a, a_up, b, b_up, a_sum, b_sum = near
        c, c_up, d, d_up, c_sum, d_sum = far
        one_up, two_up = b_up + c_up, a_up + d_up
        one, two = b + c, a + d
        kk = k(e)
        if e >= low:
            e00, f00 = kk * (d_sum + one_up), kk * (d_sum + one)
            e01, f01 = kk * (c_sum + two_up), kk * (c_sum + two)
            e10, e11, f10, f11 = carry
            put(e, (e00 + e10) + sh.ydn(e01 + e11) + sh.zdn((f00 + f10) + sh.ydn(f01 + f11)))
        if e < high:
            carry = (
                kk * (b_sum + two_up),
                kk * (a_sum + one_up),
                kk * (b_sum + two),
                kk * (a_sum + one),
            )
        near = far


def prony(dt, coef_ref, time_ref):
    decay = [jnp.exp(-dt / jnp.full((1, 128), time_ref[p], jnp.float32)) for p in range(PRONY)]
    rest = [1.0 - d for d in decay]
    f = [coef_ref[p] * decay[p] for p in range(PRONY)]
    return decay, rest, f, 1.0 / dt + (f[0] + f[1] + f[2])


def moments_out(values, red_ref):
    lane = lax.broadcasted_iota(jnp.int32, (1, 128), 1)
    packed = jnp.zeros((1, 128), jnp.float32)
    for at, field in enumerate(values):
        total = jnp.sum(jnp.sum(field, axis=0, keepdims=True), axis=1, keepdims=True)
        packed = jnp.where(lane == at, total, packed)
    red_ref[...] = jnp.broadcast_to(packed[None], red_ref.shape)


def moments_in(red_ref, first, count):
    total = jnp.sum(red_ref[...], axis=0)
    lane = lax.broadcasted_iota(jnp.int32, (1, 128), 1)
    return [
        jnp.broadcast_to(
            jnp.sum(jnp.where(lane == first + i, total, 0.0), axis=1, keepdims=True), (1, 128)
        )
        for i in range(count)
    ]


def galerkin(nu):
    m = len(nu) // 2
    mu = [nu[i] + nu[i + 1] for i in range(2 * m - 1)]
    rows = [[mu[i + j] for j in range(m)] + [nu[i]] for i in range(m)]
    for i in range(m):
        for r in range(i + 1, m):
            factor = rows[r][i] / rows[i][i]
            for j in range(i + 1, m + 1):
                rows[r][j] = rows[r][j] - factor * rows[i][j]
    c = [None] * m
    for i in reversed(range(m)):
        acc = rows[i][m]
        for j in range(i + 1, m):
            acc = acc - rows[i][j] * c[j]
        c[i] = acc / rows[i][i]
    return c


def send(odd_side, lo, hi, even_out, odd_out):
    for at, (low, high) in enumerate(zip(lo, hi)):
        even_out[at] = jnp.where(odd_side == 0, high, low)
        odd_out[at] = jnp.where(odd_side == 0, low, high)


def below(odd_side, even_ref, odd_ref, at):
    return jnp.where(odd_side == 0, odd_ref[at], even_ref[at])


def above(odd_side, even_ref, odd_ref, at):
    return jnp.where(odd_side == 0, even_ref[at], odd_ref[at])


def start_kernel(
    rigid_ref, dilate_ref, heat_ref, coef_ref, time_ref, place_ref,
    own_ref, even_ref, odd_ref, far_ref,
    kel_ref, theta_ref, inv_f_ref, inv_c_ref, state_ref,
    zf_ref, ozf_ref, oozf_ref, zc_ref, ozc_ref,
    even_out, odd_out, far_out, red_ref,
    kal_ref, au_ref, w_ref,
):
    ny, nz = kel_ref.shape[1:]
    sh = Shifts(ny, nz)
    chunks = own_ref.shape[0]
    side = place_ref[1]

    def raw(field, i):
        if i < 0:
            parts = [below(side, even_ref, odd_ref, (c, field, i + L)) for c in range(chunks)]
        elif i < L:
            parts = [own_ref[c, field, i] for c in range(chunks)]
        elif i < 2 * L:
            parts = [above(side, even_ref, odd_ref, (c, field, i - L)) for c in range(chunks)]
        else:
            parts = [far_ref[c, 0, 0] for c in range(chunks)]
        return jnp.concatenate(parts, axis=0)

    for e in range(-3, 6):
        label = raw(0, e)
        stiff = jnp.zeros((ny, nz), jnp.float32)
        load = jnp.zeros((ny, nz), jnp.float32)
        for region in range(rigid_ref.shape[0]):
            here = label == (region + 1.0)
            stiff = jnp.where(here, rigid_ref[region], stiff)
            load = jnp.where(here, dilate_ref[region], load)
        kel_ref[e + 3] = stiff * (-1.0 / 12.0)
        kal_ref[e + 3] = 0.25 * (stiff * load)

    decay_f, rest_f, ff, shift_f = prony(1.0, coef_ref, time_ref)
    decay_c, rest_c, fc, shift_c = prony(1.0 * PACES, coef_ref, time_ref)

    for i in range(-2, 6):
        ksum = kel_ref[i + 2] + kel_ref[i + 3]
        ksum = ksum + sh.ydn(ksum)
        ksum = ksum + sh.zdn(ksum)
        diag = -4.0 * ksum
        asum = kal_ref[i + 2] + kal_ref[i + 3]
        asum = asum + sh.ydn(asum)
        theta_ref[i + 2] = sh.zdn(asum) - asum
        inside = raw(0, i) > 0.5
        inv_f_ref[i + 2] = jnp.where(inside, 1.0 / (diag + shift_f), 0.0)
        inv_c_ref[i + 2] = jnp.where(inside, 1.0 / (diag + shift_c), 0.0)

    for i in range(-3, 7):
        state_ref[i + 3] = raw(1, i)

    def k(e):
        return kel_ref[e + 3]

    def put_au(i, plane):
        au_ref[i + 2] = plane

    off_diagonal(sh, lambda i: state_ref[i + 3], k, -2, 5, put_au)

    zeros = jnp.zeros((ny, nz), jnp.float32)
    acc = [zeros] * 10
    for i in range(-2, 6):
        h = [raw(2 + p, i) for p in range(PRONY)]
        fh = [ff[p] * h[p] for p in range(PRONY)]
        state_ref[10 + i + 2] = decay_f[0] * fh[0] + decay_f[1] * fh[1] + decay_f[2] * fh[2]
        ui = state_ref[i + 3]
        load = heat_ref[0, 0] * theta_ref[i + 2] + (fh[0] + fh[1] + fh[2])
        s = load + ui - au_ref[i + 2]
        z = inv_f_ref[i + 2] * s - ui
        zf_ref[i + 2] = z
        if 0 <= i < L:
            acc[0] = acc[0] + z * (s - ui * (1.0 / inv_f_ref[i + 2]))
        if i < 5:
            load = heat_ref[0, 1] * theta_ref[i + 2]
            load = load + (fc[0] * h[0] + fc[1] * h[1] + fc[2] * h[2])
            s = load + ui * (1.0 / PACES) - au_ref[i + 2]
            z = inv_c_ref[i + 2] * s - ui
            w_ref[i + 2] = z
            if 0 <= i < L:
                zc_ref[i] = z
                acc[6] = acc[6] + z * (s - ui * (1.0 / inv_c_ref[i + 2]))

    def put_oz(i, plane):
        oz = inv_f_ref[i + 2] * plane
        ozf_ref[i + 1] = oz
        if 0 <= i < L:
            acc[1] = acc[1] + zf_ref[i + 2] * plane
            acc[2] = acc[2] + oz * plane

    off_diagonal(sh, lambda i: zf_ref[i + 2], k, -1, 4, put_oz)

    def put_ooz(i, plane):
        ooz = inv_f_ref[i + 2] * plane
        oozf_ref[i] = ooz
        if i < L:
            acc[3] = acc[3] + ozf_ref[i + 1] * plane
            acc[4] = acc[4] + ooz * plane

    off_diagonal(sh, lambda i: ozf_ref[i + 1], k, 0, 3, put_ooz)

    def put_last(i, plane):
        acc[5] = acc[5] + oozf_ref[i] * plane

    by_elements(sh, lambda i: oozf_ref[i], k, put_last)

    def put_ozc(i, plane):
        oz = inv_c_ref[i + 2] * plane
        au_ref[i + 2] = oz
        if 0 <= i < L:
            ozc_ref[i] = oz
            acc[7] = acc[7] + w_ref[i + 2] * plane
            acc[8] = acc[8] + oz * plane

    off_diagonal(sh, lambda i: w_ref[i + 2], k, -1, 3, put_ozc)

    def put_lastc(i, plane):
        acc[9] = acc[9] + au_ref[i + 2] * plane

    off_diagonal(sh, lambda i: au_ref[i + 2], k, 0, 2, put_lastc)
    moments_out(acc, red_ref)

    hi = [zf_ref[2], ozf_ref[1], ozf_ref[2], oozf_ref[0], oozf_ref[1], oozf_ref[2]]
    lo = [ozf_ref[3], oozf_ref[1], oozf_ref[2]]
    send(side, lo + lo, hi, even_out, odd_out)
    far_out[0], far_out[1], far_out[2] = zf_ref[2], ozf_ref[1], oozf_ref[0]


def by_elements(sh, v, k, put):
    none = jnp.zeros((sh.ny, sh.nz), jnp.float32)

    def nodes(i):
        return v(i) if 0 <= i <= L else none

    def elements(e):
        return k(e) if 0 <= e < L else none

    off_diagonal(sh, nodes, elements, 0, L, put)


def second_kernel(
    heat_ref, coef_ref, time_ref, place_ref,
    red_in, kel_ref, theta_ref, inv_f_ref, state_ref, own_ref,
    zf_ref, ozf_ref, oozf_ref, zc_ref, ozc_ref,
    even_ref, odd_ref, far_ref,
    base_ref, z_out, oz_out, ooz_out, red_ref,
    u_ref, z_ref, oz_ref, ooz_ref, au_ref,
):
    ny, nz = kel_ref.shape[1:]
    sh = Shifts(ny, nz)
    chunks = own_ref.shape[0]
    decay_f, rest_f, ff, shift_f = prony(1.0, coef_ref, time_ref)
    decay_c, rest_c, fc, shift_c = prony(1.0 * PACES, coef_ref, time_ref)
    c = galerkin(moments_in(red_in, 0, 6))
    b = galerkin(moments_in(red_in, 6, 4))
    side = place_ref[1]

    def basis(i, at, ref, low, high, up, down):
        if i == 6:
            return far_ref[at]
        if i < low:
            return below(side, even_ref, odd_ref, up + i + L)
        if i > high:
            return above(side, even_ref, odd_ref, down + i - high - 1)
        return ref[i - low]

    for i in range(-3, 7):
        z = basis(i, 0, zf_ref, -2, 5, 0, None)
        oz = basis(i, 1, ozf_ref, -1, 4, 1, 0)
        ooz = basis(i, 2, oozf_ref, 0, 3, 3, 1)
        u_ref[i + 3] = state_ref[i + 3] + c[0] * z + c[1] * oz + c[2] * ooz

    def k(e):
        return kel_ref[e + 3]

    def put_au(i, plane):
        au_ref[i + 2] = plane

    off_diagonal(sh, lambda i: u_ref[i + 3], k, -2, 5, put_au)

    grow = ff[0] * rest_f[0] + ff[1] * rest_f[1] + ff[2] * rest_f[2]
    zeros = jnp.zeros((ny, nz), jnp.float32)
    acc = [zeros] * 6
    weight = jnp.where(place_ref[0] == 0, 0.0, 1.0)
    for i in range(-2, 6):
        ui = u_ref[i + 3]
        s = heat_ref[0, 1] * theta_ref[i + 2] + state_ref[10 + i + 2] + (grow + 1.0) * ui
        s = s - au_ref[i + 2]
        z = inv_f_ref[i + 2] * s - ui
        z_ref[i + 2] = z
        if 0 <= i < L:
            z_out[i] = z
            acc[0] = acc[0] + z * (s - ui * (1.0 / inv_f_ref[i + 2]))

    for i in range(L):
        u1 = u_ref[i + 3]
        g = state_ref[i + 3] + b[0] * zc_ref[i] + b[1] * ozc_ref[i]
        base_ref[i] = u1 - weight * g
        for p in range(PRONY):
            h = jnp.concatenate([own_ref[q, 2 + p, i] for q in range(chunks)], axis=0)
            h1 = decay_f[p] * h + rest_f[p] * u1
            gh = decay_c[p] * h + rest_c[p] * g
            base_ref[L * (1 + p) + i] = decay_f[p] * h1 + rest_f[p] * u1 - weight * gh

    def put_oz(i, plane):
        oz = inv_f_ref[i + 2] * plane
        oz_ref[i + 1] = oz
        if 0 <= i < L:
            oz_out[i] = oz
            acc[1] = acc[1] + z_ref[i + 2] * plane
            acc[2] = acc[2] + oz * plane

    off_diagonal(sh, lambda i: z_ref[i + 2], k, -1, 4, put_oz)

    def put_ooz(i, plane):
        ooz = inv_f_ref[i + 2] * plane
        ooz_ref[i] = ooz
        if i < L:
            ooz_out[i] = ooz
            acc[3] = acc[3] + oz_ref[i + 1] * plane
            acc[4] = acc[4] + ooz * plane

    off_diagonal(sh, lambda i: oz_ref[i + 1], k, 0, 3, put_ooz)

    def put_last(i, plane):
        acc[5] = acc[5] + ooz_ref[i] * plane

    by_elements(sh, lambda i: ooz_ref[i], k, put_last)
    moments_out(acc, red_ref)


def block_kernel(heat_ref, coef_ref, time_ref, red_in, base_ref, z_ref, oz_ref, ooz_ref, blk_ref):
    decay_f, rest_f, ff, shift_f = prony(1.0, coef_ref, time_ref)
    c = galerkin(moments_in(red_in, 0, 6))
    ny = z_ref.shape[1]
    for i in range(L):
        delta = c[0] * z_ref[i] + c[1] * oz_ref[i] + c[2] * ooz_ref[i]
        blk_ref[i * ny : (i + 1) * ny] = base_ref[i] + delta
        for p in range(PRONY):
            at = L * (1 + p) + i
            blk_ref[at * ny : (at + 1) * ny] = base_ref[at] + rest_f[p] * delta
    blk_ref[4 * L * ny :] = jnp.full((8, blk_ref.shape[1]), heat_ref[0, PACES - 1], jnp.float32)


def halo_base(f, base_ref):
    sums = [
        f[0] * base_ref[L + i] + f[1] * base_ref[2 * L + i] + f[2] * base_ref[3 * L + i]
        for i in range(L)
    ]
    u = [base_ref[i] for i in range(L)]
    return u + [sums[0], sums[1]], u + [sums[1], sums[2]]


def opening_kernel(coef_ref, time_ref, place_ref, blk_ref, base_ref, even_out, odd_out):
    decay, rest, f, shift = prony(1.0 * PACES, coef_ref, time_ref)
    ny = even_out.shape[1]
    for at in range(4 * L):
        base_ref[at] = blk_ref[at * ny : (at + 1) * ny]
    lo, hi = halo_base(f, base_ref)
    send(place_ref[1], lo, hi, even_out, odd_out)


def chain_kernel(turn, count, opened, rounds, *refs):
    refs = list(refs)
    coef_ref, time_ref, place_ref = refs[:3]
    refs = refs[3:]
    if opened:
        base_in, even_ref, odd_ref = refs[:3]
        refs = refs[3:]
    else:
        red_in, base_in, z_in, oz_in, even_ref, odd_ref = refs[:6]
        refs = refs[6:]
    kel_ref, theta_ref, inv_ref, blk_ref = refs[:4]
    if rounds:
        outs, (red_ref, u_ref, au_ref, base_ref, z_ref, oz_ref) = refs[4 : 4 + rounds], refs[4 + rounds :]
    else:
        base_ref, z_ref, oz_ref, even_out, odd_out, red_ref, u_ref, au_ref = refs[4:]
    ny, nz = kel_ref.shape[1:]
    sh = Shifts(ny, nz)
    decay, rest, f, shift = prony(1.0 * PACES, coef_ref, time_ref)
    grow = f[0] * rest[0] + f[1] * rest[1] + f[2] * rest[2]
    step = lax.rem(place_ref[0] + turn, count)
    heat = blk_ref[4 * L * ny : 4 * L * ny + 1]
    opening = step == 0
    fresh = step == 1
    side = place_ref[1]

    if not opened:
        c = galerkin(moments_in(red_in, 0, 4))

    def near(i, low_at, high_at):
        if i < 0:
            return below(side, even_ref, odd_ref, low_at)
        return above(side, even_ref, odd_ref, high_at)

    def delta(i):
        z = z_in[i + 2] if -2 <= i <= 4 else near(i, 5, 5)
        if -1 <= i <= 3:
            oz = oz_in[i + 1]
        else:
            at = 6 if i in (-3, 5) else 7
            oz = near(i, at, at)
        return jnp.where(fresh, 0.0, c[0] * z + c[1] * oz)

    for i in range(-3, 6):
        base = base_in[i] if 0 <= i < L else near(i, i + 3, i - L)
        d = None if opened else delta(i)
        u_ref[i + 3] = base if opened else base + d
        if 0 <= i < L:
            h = [base_in[L * (1 + p) + i] for p in range(PRONY)]
            if not opened:
                h = [h[p] + rest[p] * d for p in range(PRONY)]
            total = f[0] * h[0] + f[1] * h[1] + f[2] * h[2]
            ui = u_ref[i + 3]
            base_ref[i] = jnp.where(opening, 0.0, ui) + blk_ref[i * ny : (i + 1) * ny]
            for p in range(PRONY):
                at = L * (1 + p) + i
                ahead = jnp.where(opening, 0.0, decay[p] * h[p] + rest[p] * ui)
                base_ref[at] = ahead + blk_ref[at * ny : (at + 1) * ny]
        elif -2 <= i < 5:
            total = near(i, 3 + i + 2, 3 + i - L)
            if not opened:
                total = total + grow * d
        if -2 <= i < 5:
            au_ref[i + 2] = heat * theta_ref[i + 2] + total

    zeros = jnp.zeros((ny, nz), jnp.float32)
    acc = [zeros] * 4

    def k(e):
        return kel_ref[e + 3]

    def put_z(i, plane):
        ui = u_ref[i + 3]
        s = au_ref[i + 2] + ui * (1.0 / PACES) - plane
        inv = inv_ref[i + 2]
        z = inv * s - ui
        z_ref[i + 2] = z
        if 0 <= i < L:
            acc[0] = acc[0] + z * (s - ui * (1.0 / inv))

    off_diagonal(sh, lambda i: u_ref[i + 3], k, -2, 4, put_z)

    def put_oz(i, plane):
        oz = inv_ref[i + 2] * plane
        oz_ref[i + 1] = oz
        if 0 <= i < L:
            acc[1] = acc[1] + z_ref[i + 2] * plane
            acc[2] = acc[2] + oz * plane

    off_diagonal(sh, lambda i: z_ref[i + 2], k, -1, 3, put_oz)

    def put_last(i, plane):
        acc[3] = acc[3] + oz_ref[i + 1] * plane

    off_diagonal(sh, lambda i: oz_ref[i + 1], k, 0, 2, put_last)
    moments_out(acc, red_ref)

    if rounds:
        width = ny // rounds
        for r, out_ref in enumerate(outs):
            cut = lax.rem(2 * place_ref[2] + side + r, rounds) * width
            rows = pl.ds(pl.multiple_of(cut, width), width)
            for i in range(L):
                for field in range(1 + PRONY):
                    out_ref[field, i] = base_ref[L * field + i, rows]
                out_ref[4, i] = z_ref[i + 2, rows]
                out_ref[5, i] = oz_ref[i + 1, rows]
        return

    lo, hi = halo_base(f, base_ref)
    lo = lo + [z_ref[2 + 2], oz_ref[2 + 1], oz_ref[1 + 1]]
    hi = hi + [z_ref[0 + 2], oz_ref[0 + 1], oz_ref[1 + 1]]
    send(side, lo, hi, even_out, odd_out)


def closing_kernel(coef_ref, time_ref, place_ref, red_in, *refs):
    parts, out_ref = refs[:-1], refs[-1]
    decay, rest, f, shift = prony(1.0 * PACES, coef_ref, time_ref)
    c = galerkin(moments_in(red_in, 0, 4))
    first = place_ref[0] == 0
    count = len(parts)
    for r, part_ref in enumerate(parts):
        at = lax.rem(place_ref[4] + count - r, count) * L
        for i in range(L):
            delta = jnp.where(first, 0.0, c[0] * part_ref[4, i] + c[1] * part_ref[5, i])
            out_ref[0, 0, at + i] = part_ref[0, i] + delta
            for p in range(PRONY):
                out_ref[0, 1 + p, at + i] = part_ref[1 + p, i] + rest[p] * delta


def spread_kernel(place_ref, label_ref, values_ref, *out_refs):
    count = len(out_refs)
    for r, out_ref in enumerate(out_refs):
        first = lax.rem(place_ref[4] + count - r, count) * L
        for i in range(L):
            out_ref[0, i] = label_ref[first + i].astype(jnp.float32) + 1.0
            for field in range(1 + PRONY):
                out_ref[1 + field, i] = values_ref[0, field, first + i]


def join_kernel(place_ref, *refs):
    got_refs, out_ref = refs[:-1], refs[-1]
    count = len(got_refs)
    for r, got_ref in enumerate(got_refs):
        to = lax.rem(2 * place_ref[2] + place_ref[1] + r, count)
        for field in range(2 + PRONY):
            for i in range(L):
                out_ref[to, field, i] = got_ref[field, i]


SMEM = pl.BlockSpec(memory_space=pltpu.SMEM)
VMEM = pl.BlockSpec(memory_space=pltpu.VMEM)


def call(kernel, name, small, large, outs, scratch=()):
    f32 = jnp.float32
    return pl.pallas_call(
        kernel,
        name=name,
        out_shape=[jax.ShapeDtypeStruct(s, f32) for s in outs],
        in_specs=[SMEM] * len(small) + [VMEM] * len(large),
        out_specs=[VMEM] * len(outs),
        scratch_shapes=[pltpu.VMEM(s, f32) for s in scratch],
        compiler_params=pltpu.CompilerParams(vmem_limit_bytes=LIMIT),
    )(*small, *large)


def on_device(
    segment_opening_values,
    cell_material_label,
    material_rigidity,
    dilation_mismatch,
    heat_swings_array,
    prony_coefficients,
    prony_decay_times,
):
    n_tm, n_gy = lax.axis_size("tm"), lax.axis_size("gy")
    line = lax.axis_size("gx") * n_gy
    nx, ny_part, nz = cell_material_label.shape
    ny = ny_part * n_gy
    assert nx == L * n_gy and n_gy == 4
    plane = (ny, nz)

    def device(position):
        row, rest = divmod(position, 2 * n_gy)
        x, core = divmod(rest, 2)
        return (2 * row + core) * n_gy + (x if row % 2 == 0 else n_gy - 1 - x)

    def deal(values, back=False):
        received = []
        for r, value in enumerate(values):
            perm = []
            for position in range(line):
                row, rest = divmod(position, 2 * n_gy)
                x, core = divmod(rest, 2)
                to = (2 * row + x // 2) * n_gy + (2 * (x % 2) + core + r) % n_gy
                perm.append((to, device(position)) if back else (device(position), to))
            received.append(lax.ppermute(value, LINE, sorted(perm)))
        return received

    def trade(even, odd):
        received = []
        for side, value in enumerate((even, odd)):
            pairs = [(device(p), device(p + 1)) for p in range(side, line - 1, 2)]
            both = pairs + [(b, a) for a, b in pairs]
            received.append(lax.ppermute(value, LINE, sorted(both)))
        return received

    def from_next_but_one(value):
        perm = [(device(p + 2), device(p)) for p in range(line - 2)]
        return lax.ppermute(value, LINE, sorted(perm))

    def exchanged(red):
        return lax.all_to_all(red, LINE, 0, 0, tiled=True)

    def ring(block):
        return lax.ppermute(block, "tm", [(s, (s - 1) % n_tm) for s in range(n_tm)])

    gx, gy = lax.axis_index("gx"), lax.axis_index("gy")
    core, flip = gx % 2, gx // 2 % 2
    x = jnp.where(flip == 0, gy, n_gy - 1 - gy)
    place = jnp.stack([lax.axis_index("tm"), core, x % 2, flip, gy]).astype(jnp.int32)
    prony_args = (prony_coefficients, prony_decay_times)

    parts = call(
        spread_kernel,
        "spread",
        (place,),
        (cell_material_label, segment_opening_values),
        [(2 + PRONY, L, ny_part, nz)] * n_gy,
    )
    (own,) = call(
        join_kernel, "join", (place,), deal(parts, True), [(n_gy, 2 + PRONY, L, ny_part, nz)]
    )
    near, far = trade(own, own), from_next_but_one(own[:, 1:2, :1])

    red_shape = (line, 1, 128)
    (kel, theta, inv_f, inv_c, state, zf, ozf, oozf, zc, ozc, even, odd, far, red) = call(
        start_kernel,
        "start",
        (material_rigidity, dilation_mismatch, heat_swings_array, *prony_args, place),
        (own, *near, far),
        [
            (9, *plane), (8, *plane), (8, *plane), (8, *plane), (18, *plane),
            (8, *plane), (6, *plane), (4, *plane), (L, *plane), (L, *plane),
            (6, *plane), (6, *plane), (3, *plane), red_shape,
        ],
        [(9, *plane), (8, *plane), (7, *plane)],
    )
    red = exchanged(red)
    near, far = trade(even, odd), from_next_but_one(far)
    base, z, oz, ooz, red = call(
        second_kernel,
        "second",
        (heat_swings_array, *prony_args, place),
        (red, kel, theta, inv_f, state, own, zf, ozf, oozf, zc, ozc, *near, far),
        [(4 * L, *plane), (L, *plane), (L, *plane), (L, *plane), red_shape],
        [(10, *plane), (8, *plane), (6, *plane), (4, *plane), (8, *plane)],
    )
    red = exchanged(red)
    (block,) = call(
        block_kernel,
        "block",
        (heat_swings_array, *prony_args),
        (red, base, z, oz, ooz),
        [(4 * L * ny + 8, nz)],
    )
    mine = block
    block = ring(block)
    base, even, odd = call(
        opening_kernel,
        "opening",
        (*prony_args, place),
        (block,),
        [(4 * L, *plane), (5, *plane), (5, *plane)],
    )
    past = (base,)
    for turn in range(2, n_tm + 1):
        if turn < n_tm:
            block, even = lax.optimization_barrier((block, even))
            block = ring(block)
        else:
            block = mine
        past = (*past, *trade(even, odd))
        last = turn == n_tm
        state = [(4 * L, *plane), (7, *plane), (5, *plane)]
        work = [(9, *plane), (7, *plane)]
        *outs, red = call(
            functools.partial(chain_kernel, turn, n_tm, turn == 2, n_gy if last else 0),
            f"chain{turn}",
            (*prony_args, place),
            (*past, kel, theta, inv_c, block),
            [(3 + PRONY, L, ny_part, nz)] * n_gy + [red_shape]
            if last
            else [*state, (8, *plane), (8, *plane), red_shape],
            work + state if last else work,
        )
        if last:
            break
        base, z, oz, even, odd = outs
        past = (exchanged(red), base, z, oz)
    parts = deal(outs)
    (out,) = call(
        closing_kernel,
        "closing",
        (*prony_args, place),
        (exchanged(red), *parts),
        [(1, 1 + PRONY, nx, ny_part, nz)],
    )
    return out


def solution(mesh):
    placed = (
        P("tm", None, "gx", "gy", None),
        P("gx", "gy", None),
        P(),
        P(),
        P("tm", None),
        P(),
        P(),
    )
    return jax.shard_map(
        on_device,
        mesh=mesh,
        in_specs=placed,
        out_specs=P("tm", None, "gx", "gy", None),
        check_vma=False,
    )
```

```python
import functools

import jax
import jax.numpy as jnp
from jax import lax
from jax.experimental import pallas as pl
from jax.experimental.pallas import tpu as pltpu
from jax.sharding import PartitionSpec as P

PACES = 2
SHARP = 3
LOOSE = 2
PRONY = 3
L = 3
LINE = ("gx", "gy")
LIMIT = 14 << 20


class Shifts:
    def __init__(self, ny, nz):
        self.ny, self.nz = ny, nz
        lane = lax.broadcasted_iota(jnp.int32, (ny, nz), 1)
        row = lax.broadcasted_iota(jnp.int32, (8, nz), 0)
        self.lane_first, self.lane_last = lane == 0, lane == nz - 1
        self.row_first, self.row_last = row == 0, row == 7

    def zup(self, v):
        return jnp.where(self.lane_last, 0.0, pltpu.roll(v, self.nz - 1, 1))

    def zdn(self, v):
        return jnp.where(self.lane_first, 0.0, pltpu.roll(v, 1, 1))

    def yup(self, v):
        v = pltpu.roll(v, self.ny - 1, 0)
        end = jnp.where(self.row_last, 0.0, v[self.ny - 8 :])
        return jnp.concatenate([v[: self.ny - 8], end], axis=0)

    def ydn(self, v):
        v = pltpu.roll(v, 1, 0)
        return jnp.concatenate([jnp.where(self.row_first, 0.0, v[:8]), v[8:]], axis=0)


def off_diagonal(sh, v, k, low, high, put):
    def spread(plane):
        up = sh.zup(plane)
        side, side_up = sh.yup(plane), sh.yup(up)
        return plane, up, side, side_up, plane + up, side + side_up

    near = spread(v(low - 1))
    carry = None
    for e in range(low - 1, high + 1):
        far = spread(v(e + 1))
        a, a_up, b, b_up, a_sum, b_sum = near
        c, c_up, d, d_up, c_sum, d_sum = far
        one_up, two_up = b_up + c_up, a_up + d_up
        one, two = b + c, a + d
        kk = k(e)
        if e >= low:
            e00, f00 = kk * (d_sum + one_up), kk * (d_sum + one)
            e01, f01 = kk * (c_sum + two_up), kk * (c_sum + two)
            e10, e11, f10, f11 = carry
            put(e, (e00 + e10) + sh.ydn(e01 + e11) + sh.zdn((f00 + f10) + sh.ydn(f01 + f11)))
        if e < high:
            carry = (
                kk * (b_sum + two_up),
                kk * (a_sum + one_up),
                kk * (b_sum + two),
                kk * (a_sum + one),
            )
        near = far


COARSE, HEAT, SLICE, SIDE, PART, CHIP, RIGID = 10, 20, 22, 23, 24, 25, 26


def fill_constants(heat_ref, coef_ref, time_ref, rigid_ref, dilate_ref, place_ref, const_ref):
    def put(at, value):
        const_ref[at : at + 1] = jnp.broadcast_to(value, (1, 128))

    def entry(ref, i):
        return jnp.broadcast_to(ref[0:1, i : i + 1], (1, 128))

    for first, dt in ((0, 1.0), (COARSE, 1.0 * PACES)):
        total = jnp.full((1, 128), 1.0 / dt, jnp.float32)
        for p in range(PRONY):
            decay = jnp.exp(-dt / entry(time_ref, p))
            f = entry(coef_ref, p) * decay
            put(first + p, decay)
            put(first + 3 + p, 1.0 - decay)
            put(first + 6 + p, f)
            total = total + f
        put(first + 9, total)
    put(HEAT, entry(heat_ref, 0))
    put(HEAT + 1, entry(heat_ref, PACES - 1))
    for i in range(4):
        put(SLICE + i, entry(place_ref, i))
    regions = rigid_ref.shape[1]
    for i in range(regions):
        put(RIGID + i, entry(rigid_ref, i))
        put(RIGID + regions + i, entry(dilate_ref, i))


def prony(const_ref, first):
    rows = [const_ref[first + i : first + i + 1] for i in range(10)]
    return rows[:3], rows[3:6], rows[6:9], rows[9]


def holds(const_ref, row, value, shape):
    return jnp.broadcast_to(const_ref[row : row + 1], shape) == float(value)


def moments_out(values, red_ref):
    lane = lax.broadcasted_iota(jnp.int32, (1, 128), 1)
    packed = jnp.zeros((1, 128), jnp.float32)
    for at, field in enumerate(values):
        total = jnp.sum(jnp.sum(field, axis=0, keepdims=True), axis=1, keepdims=True)
        packed = jnp.where(lane == at, total, packed)
    red_ref[...] = jnp.broadcast_to(packed[None], red_ref.shape)


def moments_in(red_ref, first, count):
    total = jnp.sum(red_ref[...], axis=0)
    lane = lax.broadcasted_iota(jnp.int32, (1, 128), 1)
    return [
        jnp.broadcast_to(
            jnp.sum(jnp.where(lane == first + i, total, 0.0), axis=1, keepdims=True), (1, 128)
        )
        for i in range(count)
    ]


def galerkin(nu):
    m = len(nu) // 2
    mu = [nu[i] + nu[i + 1] for i in range(2 * m - 1)]
    rows = [[mu[i + j] for j in range(m)] + [nu[i]] for i in range(m)]
    for i in range(m):
        for r in range(i + 1, m):
            factor = rows[r][i] / rows[i][i]
            for j in range(i + 1, m + 1):
                rows[r][j] = rows[r][j] - factor * rows[i][j]
    c = [None] * m
    for i in reversed(range(m)):
        acc = rows[i][m]
        for j in range(i + 1, m):
            acc = acc - rows[i][j] * c[j]
        c[i] = acc / rows[i][i]
    return c


def send(even_place, lo, hi, even_out, odd_out):
    for at, (low, high) in enumerate(zip(lo, hi)):
        even_out[at] = jnp.where(even_place, high, low)
        odd_out[at] = jnp.where(even_place, low, high)


def below(even_place, even_ref, odd_ref, at):
    return jnp.where(even_place, odd_ref[at], even_ref[at])


def above(even_place, even_ref, odd_ref, at):
    return jnp.where(even_place, even_ref[at], odd_ref[at])


def chosen(const_ref, row, values):
    value = values[-1]
    for v in range(len(values) - 1):
        value = jnp.where(holds(const_ref, row, v, value.shape), values[v], value)
    return value


def start_kernel(
    own_ref, even_ref, odd_ref, far_ref, const_ref,
    kel_ref, theta_ref, inv_f_ref, inv_c_ref, state_ref,
    zf_ref, ozf_ref, oozf_ref, zc_ref, ozc_ref,
    even_out, odd_out, far_out, red_ref,
    kal_ref, au_ref, w_ref,
):
    ny, nz = kel_ref.shape[1:]
    sh = Shifts(ny, nz)
    chunks = own_ref.shape[0]
    side = holds(const_ref, SIDE, 0, (ny, nz))
    side_part = holds(const_ref, SIDE, 0, (ny // chunks, nz))

    def raw(field, i):
        if i < 0:
            parts = [below(side_part, even_ref, odd_ref, (c, field, i + L)) for c in range(chunks)]
        elif i < L:
            parts = [own_ref[c, field, i] for c in range(chunks)]
        elif i < 2 * L:
            parts = [above(side_part, even_ref, odd_ref, (c, field, i - L)) for c in range(chunks)]
        else:
            parts = [far_ref[c, 0, 0] for c in range(chunks)]
        return jnp.concatenate(parts, axis=0)

    regions = (const_ref.shape[0] - RIGID) // 2
    table = [const_ref[RIGID + i : RIGID + i + 1] for i in range(2 * regions)]

    for e in range(-3, 6):
        label = raw(0, e)
        stiff = jnp.zeros((ny, nz), jnp.float32)
        load = jnp.zeros((ny, nz), jnp.float32)
        for region in range(regions):
            here = label == (region + 1.0)
            stiff = jnp.where(here, table[region], stiff)
            load = jnp.where(here, table[regions + region], load)
        kel_ref[e + 3] = stiff * (-1.0 / 12.0)
        kal_ref[e + 3] = 0.25 * (stiff * load)

    heat = [const_ref[HEAT + i : HEAT + i + 1] for i in range(2)]
    decay_f, rest_f, ff, shift_f = prony(const_ref, 0)
    decay_c, rest_c, fc, shift_c = prony(const_ref, COARSE)

    for i in range(-2, 6):
        ksum = kel_ref[i + 2] + kel_ref[i + 3]
        ksum = ksum + sh.ydn(ksum)
        ksum = ksum + sh.zdn(ksum)
        diag = -4.0 * ksum
        asum = kal_ref[i + 2] + kal_ref[i + 3]
        asum = asum + sh.ydn(asum)
        theta_ref[i + 2] = sh.zdn(asum) - asum
        inside = raw(0, i) > 0.5
        inv_f_ref[i + 2] = jnp.where(inside, 1.0 / (diag + shift_f), 0.0)
        inv_c_ref[i + 2] = jnp.where(inside, 1.0 / (diag + shift_c), 0.0)

    for i in range(-3, 7):
        state_ref[i + 3] = raw(1, i)

    def k(e):
        return kel_ref[e + 3]

    def put_au(i, plane):
        au_ref[i + 2] = plane

    off_diagonal(sh, lambda i: state_ref[i + 3], k, -2, 5, put_au)

    zeros = jnp.zeros((ny, nz), jnp.float32)
    acc = [zeros] * 10
    for i in range(-2, 6):
        h = [raw(2 + p, i) for p in range(PRONY)]
        fh = [ff[p] * h[p] for p in range(PRONY)]
        state_ref[10 + i + 2] = decay_f[0] * fh[0] + decay_f[1] * fh[1] + decay_f[2] * fh[2]
        ui = state_ref[i + 3]
        load = heat[0] * theta_ref[i + 2] + (fh[0] + fh[1] + fh[2])
        s = load + ui - au_ref[i + 2]
        z = inv_f_ref[i + 2] * s - ui
        zf_ref[i + 2] = z
        if 0 <= i < L:
            acc[0] = acc[0] + z * (s - ui * (1.0 / inv_f_ref[i + 2]))
        if i < 5:
            load = heat[1] * theta_ref[i + 2]
            load = load + (fc[0] * h[0] + fc[1] * h[1] + fc[2] * h[2])
            s = load + ui * (1.0 / PACES) - au_ref[i + 2]
            z = inv_c_ref[i + 2] * s - ui
            w_ref[i + 2] = z
            if 0 <= i < L:
                zc_ref[i] = z
                acc[6] = acc[6] + z * (s - ui * (1.0 / inv_c_ref[i + 2]))

    def put_oz(i, plane):
        oz = inv_f_ref[i + 2] * plane
        ozf_ref[i + 1] = oz
        if 0 <= i < L:
            acc[1] = acc[1] + zf_ref[i + 2] * plane
            acc[2] = acc[2] + oz * plane

    off_diagonal(sh, lambda i: zf_ref[i + 2], k, -1, 4, put_oz)

    def put_ooz(i, plane):
        ooz = inv_f_ref[i + 2] * plane
        oozf_ref[i] = ooz
        if i < L:
            acc[3] = acc[3] + ozf_ref[i + 1] * plane
            acc[4] = acc[4] + ooz * plane

    off_diagonal(sh, lambda i: ozf_ref[i + 1], k, 0, 3, put_ooz)

    def put_last(i, plane):
        acc[5] = acc[5] + oozf_ref[i] * plane

    by_elements(sh, lambda i: oozf_ref[i], k, put_last)

    def put_ozc(i, plane):
        oz = inv_c_ref[i + 2] * plane
        au_ref[i + 2] = oz
        if 0 <= i < L:
            ozc_ref[i] = oz
            acc[7] = acc[7] + w_ref[i + 2] * plane
            acc[8] = acc[8] + oz * plane

    off_diagonal(sh, lambda i: w_ref[i + 2], k, -1, 3, put_ozc)

    def put_lastc(i, plane):
        acc[9] = acc[9] + au_ref[i + 2] * plane

    off_diagonal(sh, lambda i: au_ref[i + 2], k, 0, 2, put_lastc)
    moments_out(acc, red_ref)

    hi = [zf_ref[2], ozf_ref[1], ozf_ref[2], oozf_ref[0], oozf_ref[1], oozf_ref[2]]
    lo = [ozf_ref[3], oozf_ref[1], oozf_ref[2]]
    send(side, lo + lo, hi, even_out, odd_out)
    far_out[0], far_out[1], far_out[2] = zf_ref[2], ozf_ref[1], oozf_ref[0]


def by_elements(sh, v, k, put):
    none = jnp.zeros((sh.ny, sh.nz), jnp.float32)

    def nodes(i):
        return v(i) if 0 <= i <= L else none

    def elements(e):
        return k(e) if 0 <= e < L else none

    off_diagonal(sh, nodes, elements, 0, L, put)


def second_kernel(
    const_ref, red_in, kel_ref, theta_ref, inv_f_ref, state_ref, own_ref,
    zf_ref, ozf_ref, oozf_ref, zc_ref, ozc_ref,
    even_ref, odd_ref, far_ref,
    base_ref, z_out, oz_out, ooz_out, red_ref,
    u_ref, z_ref, oz_ref, ooz_ref, au_ref,
):
    ny, nz = kel_ref.shape[1:]
    sh = Shifts(ny, nz)
    chunks = own_ref.shape[0]
    decay_f, rest_f, ff, shift_f = prony(const_ref, 0)
    decay_c, rest_c, fc, shift_c = prony(const_ref, COARSE)
    c = galerkin(moments_in(red_in, 0, 6))
    b = galerkin(moments_in(red_in, 6, 4))
    side = holds(const_ref, SIDE, 0, (ny, nz))
    heat = const_ref[HEAT + 1 : HEAT + 2]

    def basis(i, at, ref, low, high, up, down):
        if i == 6:
            return far_ref[at]
        if i < low:
            return below(side, even_ref, odd_ref, up + i + L)
        if i > high:
            return above(side, even_ref, odd_ref, down + i - high - 1)
        return ref[i - low]

    for i in range(-3, 7):
        z = basis(i, 0, zf_ref, -2, 5, 0, None)
        oz = basis(i, 1, ozf_ref, -1, 4, 1, 0)
        ooz = basis(i, 2, oozf_ref, 0, 3, 3, 1)
        u_ref[i + 3] = state_ref[i + 3] + c[0] * z + c[1] * oz + c[2] * ooz

    def k(e):
        return kel_ref[e + 3]

    def put_au(i, plane):
        au_ref[i + 2] = plane

    off_diagonal(sh, lambda i: u_ref[i + 3], k, -2, 5, put_au)

    grow = ff[0] * rest_f[0] + ff[1] * rest_f[1] + ff[2] * rest_f[2]
    zeros = jnp.zeros((ny, nz), jnp.float32)
    acc = [zeros] * 6
    weight = jnp.where(holds(const_ref, SLICE, 0, (1, nz)), 0.0, 1.0)
    for i in range(-2, 6):
        ui = u_ref[i + 3]
        s = heat * theta_ref[i + 2] + state_ref[10 + i + 2] + (grow + 1.0) * ui
        s = s - au_ref[i + 2]
        z = inv_f_ref[i + 2] * s - ui
        z_ref[i + 2] = z
        if 0 <= i < L:
            z_out[i] = z
            acc[0] = acc[0] + z * (s - ui * (1.0 / inv_f_ref[i + 2]))

    for i in range(L):
        u1 = u_ref[i + 3]
        g = state_ref[i + 3] + b[0] * zc_ref[i] + b[1] * ozc_ref[i]
        base_ref[i] = u1 - weight * g
        for p in range(PRONY):
            h = jnp.concatenate([own_ref[q, 2 + p, i] for q in range(chunks)], axis=0)
            h1 = decay_f[p] * h + rest_f[p] * u1
            gh = decay_c[p] * h + rest_c[p] * g
            base_ref[L * (1 + p) + i] = decay_f[p] * h1 + rest_f[p] * u1 - weight * gh

    def put_oz(i, plane):
        oz = inv_f_ref[i + 2] * plane
        oz_ref[i + 1] = oz
        if 0 <= i < L:
            oz_out[i] = oz
            acc[1] = acc[1] + z_ref[i + 2] * plane
            acc[2] = acc[2] + oz * plane

    off_diagonal(sh, lambda i: z_ref[i + 2], k, -1, 4, put_oz)

    def put_ooz(i, plane):
        ooz = inv_f_ref[i + 2] * plane
        ooz_ref[i] = ooz
        if i < L:
            ooz_out[i] = ooz
            acc[3] = acc[3] + oz_ref[i + 1] * plane
            acc[4] = acc[4] + ooz * plane

    off_diagonal(sh, lambda i: oz_ref[i + 1], k, 0, 3, put_ooz)

    def put_last(i, plane):
        acc[5] = acc[5] + ooz_ref[i] * plane

    by_elements(sh, lambda i: ooz_ref[i], k, put_last)
    moments_out(acc, red_ref)


def block_kernel(const_ref, red_in, base_ref, z_ref, oz_ref, ooz_ref, blk_ref):
    decay_f, rest_f, ff, shift_f = prony(const_ref, 0)
    c = galerkin(moments_in(red_in, 0, 6))
    ny = z_ref.shape[1]
    for i in range(L):
        delta = c[0] * z_ref[i] + c[1] * oz_ref[i] + c[2] * ooz_ref[i]
        blk_ref[i * ny : (i + 1) * ny] = base_ref[i] + delta
        for p in range(PRONY):
            at = L * (1 + p) + i
            blk_ref[at * ny : (at + 1) * ny] = base_ref[at] + rest_f[p] * delta
    blk_ref[4 * L * ny :] = jnp.broadcast_to(const_ref[HEAT + 1 : HEAT + 2], (8, blk_ref.shape[1]))


def halo_base(f, base_ref):
    sums = [
        f[0] * base_ref[L + i] + f[1] * base_ref[2 * L + i] + f[2] * base_ref[3 * L + i]
        for i in range(L)
    ]
    u = [base_ref[i] for i in range(L)]
    return u + [sums[0], sums[1]], u + [sums[1], sums[2]]


def opening_kernel(const_ref, blk_ref, base_ref, even_out, odd_out):
    decay, rest, f, shift = prony(const_ref, COARSE)
    ny = even_out.shape[1]
    for at in range(4 * L):
        base_ref[at] = blk_ref[at * ny : (at + 1) * ny]
    lo, hi = halo_base(f, base_ref)
    send(holds(const_ref, SIDE, 0, even_out.shape[1:]), lo, hi, even_out, odd_out)


def chain_kernel(turn, count, opened, rounds, *refs):
    refs = list(refs)
    const_ref = refs.pop(0)
    if opened:
        base_in, even_ref, odd_ref = refs[:3]
        refs = refs[3:]
    else:
        red_in, base_in, z_in, oz_in, even_ref, odd_ref = refs[:6]
        refs = refs[6:]
    kel_ref, theta_ref, inv_ref, blk_ref = refs[:4]
    if rounds:
        outs, (red_ref, u_ref, au_ref, base_ref, z_ref, oz_ref) = refs[4 : 4 + rounds], refs[4 + rounds :]
    else:
        base_ref, z_ref, oz_ref, even_out, odd_out, red_ref, u_ref, au_ref = refs[4:]
    ny, nz = kel_ref.shape[1:]
    sh = Shifts(ny, nz)
    decay, rest, f, shift = prony(const_ref, COARSE)
    grow = f[0] * rest[0] + f[1] * rest[1] + f[2] * rest[2]
    heat = blk_ref[4 * L * ny : 4 * L * ny + 1]
    opening = holds(const_ref, SLICE, -turn % count, (ny, nz))
    fresh = holds(const_ref, SLICE, (1 - turn) % count, (ny, nz))
    side = holds(const_ref, SIDE, 0, (ny, nz))

    if not opened:
        c = galerkin(moments_in(red_in, 0, 4))

    def near(i, low_at, high_at):
        if i < 0:
            return below(side, even_ref, odd_ref, low_at)
        return above(side, even_ref, odd_ref, high_at)

    def delta(i):
        z = z_in[i + 2] if -2 <= i <= 4 else near(i, 5, 5)
        if -1 <= i <= 3:
            oz = oz_in[i + 1]
        else:
            at = 6 if i in (-3, 5) else 7
            oz = near(i, at, at)
        return jnp.where(fresh, 0.0, c[0] * z + c[1] * oz)

    for i in range(-3, 6):
        base = base_in[i] if 0 <= i < L else near(i, i + 3, i - L)
        d = None if opened else delta(i)
        u_ref[i + 3] = base if opened else base + d
        if 0 <= i < L:
            h = [base_in[L * (1 + p) + i] for p in range(PRONY)]
            if not opened:
                h = [h[p] + rest[p] * d for p in range(PRONY)]
            total = f[0] * h[0] + f[1] * h[1] + f[2] * h[2]
            ui = u_ref[i + 3]
            base_ref[i] = jnp.where(opening, 0.0, ui) + blk_ref[i * ny : (i + 1) * ny]
            for p in range(PRONY):
                at = L * (1 + p) + i
                ahead = jnp.where(opening, 0.0, decay[p] * h[p] + rest[p] * ui)
                base_ref[at] = ahead + blk_ref[at * ny : (at + 1) * ny]
        elif -2 <= i < 5:
            total = near(i, 3 + i + 2, 3 + i - L)
            if not opened:
                total = total + grow * d
        if -2 <= i < 5:
            au_ref[i + 2] = heat * theta_ref[i + 2] + total

    zeros = jnp.zeros((ny, nz), jnp.float32)
    acc = [zeros] * 4

    def k(e):
        return kel_ref[e + 3]

    def put_z(i, plane):
        ui = u_ref[i + 3]
        s = au_ref[i + 2] + ui * (1.0 / PACES) - plane
        inv = inv_ref[i + 2]
        z = inv * s - ui
        z_ref[i + 2] = z
        if 0 <= i < L:
            acc[0] = acc[0] + z * (s - ui * (1.0 / inv))

    off_diagonal(sh, lambda i: u_ref[i + 3], k, -2, 4, put_z)

    def put_oz(i, plane):
        oz = inv_ref[i + 2] * plane
        oz_ref[i + 1] = oz
        if 0 <= i < L:
            acc[1] = acc[1] + z_ref[i + 2] * plane
            acc[2] = acc[2] + oz * plane

    off_diagonal(sh, lambda i: z_ref[i + 2], k, -1, 3, put_oz)

    def put_last(i, plane):
        acc[3] = acc[3] + oz_ref[i + 1] * plane

    off_diagonal(sh, lambda i: oz_ref[i + 1], k, 0, 2, put_last)
    moments_out(acc, red_ref)

    if rounds:
        width = ny // rounds
        for i in range(L):
            fields = [base_ref[L * field + i] for field in range(1 + PRONY)]
            for at, field in enumerate(fields + [z_ref[i + 2], oz_ref[i + 1]]):
                cuts = [field[q * width : (q + 1) * width] for q in range(rounds)]
                for r, out_ref in enumerate(outs):
                    ahead = [cuts[(v + r) % rounds] for v in range(rounds)]
                    out_ref[at, i] = chosen(const_ref, PART, ahead)
        return

    lo, hi = halo_base(f, base_ref)
    lo = lo + [z_ref[2 + 2], oz_ref[2 + 1], oz_ref[1 + 1]]
    hi = hi + [z_ref[0 + 2], oz_ref[0 + 1], oz_ref[1 + 1]]
    send(side, lo, hi, even_out, odd_out)


def closing_kernel(const_ref, red_in, *refs):
    parts, out_ref = refs[:-1], refs[-1]
    decay, rest, f, shift = prony(const_ref, COARSE)
    c = galerkin(moments_in(red_in, 0, 4))
    first = holds(const_ref, SLICE, 0, out_ref.shape[3:])
    count = len(parts)
    for k in range(count):
        for i in range(L):
            base_u, *base_h, z, oz = [
                chosen(const_ref, CHIP, [parts[(v - k) % count][at, i] for v in range(count)])
                for at in range(3 + PRONY)
            ]
            delta = jnp.where(first, 0.0, c[0] * z + c[1] * oz)
            out_ref[0, 0, k * L + i] = base_u + delta
            for p in range(PRONY):
                out_ref[0, 1 + p, k * L + i] = base_h[p] + rest[p] * delta


def spread_kernel(
    heat_ref, coef_ref, time_ref, rigid_ref, dilate_ref, place_ref, label_ref, values_ref,
    const_ref, *out_refs,
):
    fill_constants(heat_ref, coef_ref, time_ref, rigid_ref, dilate_ref, place_ref, const_ref)
    count = len(out_refs)
    for i in range(L):
        labels = [label_ref[k * L + i].astype(jnp.float32) + 1.0 for k in range(count)]
        fields = [labels]
        for field in range(1 + PRONY):
            fields.append([values_ref[0, field, k * L + i] for k in range(count)])
        for at, blocks in enumerate(fields):
            for r, out_ref in enumerate(out_refs):
                ahead = [blocks[(v - r) % count] for v in range(count)]
                out_ref[at, i] = chosen(const_ref, CHIP, ahead)


def join_kernel(const_ref, *refs):
    got_refs, out_ref = refs[:-1], refs[-1]
    count = len(got_refs)
    for q in range(count):
        for field in range(2 + PRONY):
            for i in range(L):
                parts = [got_refs[(q - v) % count][field, i] for v in range(count)]
                out_ref[q, field, i] = chosen(const_ref, PART, parts)


VMEM = pl.BlockSpec(memory_space=pltpu.VMEM)


def call(kernel, name, arrays, outs, scratch=()):
    f32 = jnp.float32
    return pl.pallas_call(
        kernel,
        name=name,
        out_shape=[jax.ShapeDtypeStruct(s, f32) for s in outs],
        in_specs=[VMEM] * len(arrays),
        out_specs=[VMEM] * len(outs),
        scratch_shapes=[pltpu.VMEM(s, f32) for s in scratch],
        compiler_params=pltpu.CompilerParams(vmem_limit_bytes=LIMIT),
    )(*arrays)


def on_device(
    segment_opening_values,
    cell_material_label,
    material_rigidity,
    dilation_mismatch,
    heat_swings_array,
    prony_coefficients,
    prony_decay_times,
):
    n_tm, n_gy = lax.axis_size("tm"), lax.axis_size("gy")
    line = lax.axis_size("gx") * n_gy
    nx, ny_part, nz = cell_material_label.shape
    ny = ny_part * n_gy
    assert nx == L * n_gy and n_gy == 4
    plane = (ny, nz)

    def device(position):
        row, rest = divmod(position, 2 * n_gy)
        x, core = divmod(rest, 2)
        return (2 * row + core) * n_gy + (x if row % 2 == 0 else n_gy - 1 - x)

    def deal(values, back=False):
        received = []
        for r, value in enumerate(values):
            perm = []
            for position in range(line):
                row, rest = divmod(position, 2 * n_gy)
                x, core = divmod(rest, 2)
                to = (2 * row + x // 2) * n_gy + (2 * (x % 2) + core + r) % n_gy
                perm.append((to, device(position)) if back else (device(position), to))
            received.append(lax.ppermute(value, LINE, sorted(perm)))
        return received

    def trade(even, odd):
        received = []
        for side, value in enumerate((even, odd)):
            pairs = [(device(p), device(p + 1)) for p in range(side, line - 1, 2)]
            both = pairs + [(b, a) for a, b in pairs]
            received.append(lax.ppermute(value, LINE, sorted(both)))
        return received

    def from_next_but_one(value):
        perm = [(device(p + 2), device(p)) for p in range(line - 2)]
        return lax.ppermute(value, LINE, sorted(perm))

    def exchanged(red):
        return lax.all_to_all(red, LINE, 0, 0, tiled=True)

    def ring(block):
        return lax.ppermute(block, "tm", [(s, (s - 1) % n_tm) for s in range(n_tm)])

    gx, gy = lax.axis_index("gx"), lax.axis_index("gy")
    core, flip = gx % 2, gx // 2 % 2
    x = jnp.where(flip == 0, gy, n_gy - 1 - gy)
    place = jnp.stack([lax.axis_index("tm"), core, 2 * (x % 2) + core, gy])
    place = place.astype(jnp.float32)[None]
    regions = material_rigidity.shape[0]
    tables = (prony_coefficients, prony_decay_times, material_rigidity, dilation_mismatch)

    const, *parts = call(
        spread_kernel,
        "spread",
        (
            heat_swings_array,
            *[table[None] for table in tables],
            place,
            cell_material_label,
            segment_opening_values,
        ),
        [(RIGID + 2 * regions, nz)] + [(2 + PRONY, L, ny_part, nz)] * n_gy,
    )
    (own,) = call(
        join_kernel, "join", (const, *deal(parts, True)), [(n_gy, 2 + PRONY, L, ny_part, nz)]
    )
    near, far = trade(own, own), from_next_but_one(own[:, 1:2, :1])

    red_shape = (line, 1, 128)
    (kel, theta, inv_f, inv_c, state, zf, ozf, oozf, zc, ozc, even, odd, far, red) = call(
        start_kernel,
        "start",
        (own, *near, far, const),
        [
            (9, *plane), (8, *plane), (8, *plane), (8, *plane), (18, *plane),
            (8, *plane), (6, *plane), (4, *plane), (L, *plane), (L, *plane),
            (6, *plane), (6, *plane), (3, *plane), red_shape,
        ],
        [(9, *plane), (8, *plane), (7, *plane)],
    )
    red = exchanged(red)
    near, far = trade(even, odd), from_next_but_one(far)
    base, z, oz, ooz, red = call(
        second_kernel,
        "second",
        (const, red, kel, theta, inv_f, state, own, zf, ozf, oozf, zc, ozc, *near, far),
        [(4 * L, *plane), (L, *plane), (L, *plane), (L, *plane), red_shape],
        [(10, *plane), (8, *plane), (6, *plane), (4, *plane), (8, *plane)],
    )
    red = exchanged(red)
    (block,) = call(
        block_kernel,
        "block",
        (const, red, base, z, oz, ooz),
        [(4 * L * ny + 8, nz)],
    )
    mine = block
    block = ring(block)
    base, even, odd = call(
        opening_kernel,
        "opening",
        (const, block),
        [(4 * L, *plane), (5, *plane), (5, *plane)],
    )
    past = (base,)
    for turn in range(2, n_tm + 1):
        if turn < n_tm:
            block, even = lax.optimization_barrier((block, even))
            block = ring(block)
        else:
            block = mine
        past = (*past, *trade(even, odd))
        last = turn == n_tm
        state = [(4 * L, *plane), (7, *plane), (5, *plane)]
        work = [(9, *plane), (7, *plane)]
        *outs, red = call(
            functools.partial(chain_kernel, turn, n_tm, turn == 2, n_gy if last else 0),
            f"chain{turn}",
            (const, *past, kel, theta, inv_c, block),
            [(3 + PRONY, L, ny_part, nz)] * n_gy + [red_shape]
            if last
            else [*state, (8, *plane), (8, *plane), red_shape],
            work + state if last else work,
        )
        if last:
            break
        base, z, oz, even, odd = outs
        past = (exchanged(red), base, z, oz)
    parts = deal(outs)
    (out,) = call(
        closing_kernel,
        "closing",
        (const, exchanged(red), *parts),
        [(1, 1 + PRONY, nx, ny_part, nz)],
    )
    return out


def solution(mesh):
    placed = (
        P("tm", None, "gx", "gy", None),
        P("gx", "gy", None),
        P(),
        P(),
        P("tm", None),
        P(),
        P(),
    )
    return jax.shard_map(
        on_device,
        mesh=mesh,
        in_specs=placed,
        out_specs=P("tm", None, "gx", "gy", None),
        check_vma=False,
    )
```

```python
import functools

import jax
import jax.numpy as jnp
from jax import lax
from jax.experimental import pallas as pl
from jax.experimental.pallas import tpu as pltpu
from jax.sharding import PartitionSpec as P

PACES = 2
SHARP = 3
LOOSE = 2
PRONY = 3
L = 3
LINE = ("gx", "gy")
LIMIT = 14 << 20


class Shifts:
    def __init__(self, ny, nz):
        self.ny, self.nz = ny, nz
        lane = lax.broadcasted_iota(jnp.int32, (ny, nz), 1)
        row = lax.broadcasted_iota(jnp.int32, (8, nz), 0)
        self.lane_first, self.lane_last = lane == 0, lane == nz - 1
        self.row_first, self.row_last = row == 0, row == 7

    def zup(self, v):
        return jnp.where(self.lane_last, 0.0, pltpu.roll(v, self.nz - 1, 1))

    def zdn(self, v):
        return jnp.where(self.lane_first, 0.0, pltpu.roll(v, 1, 1))

    def yup(self, v):
        v = pltpu.roll(v, self.ny - 1, 0)
        end = jnp.where(self.row_last, 0.0, v[self.ny - 8 :])
        return jnp.concatenate([v[: self.ny - 8], end], axis=0)

    def ydn(self, v):
        v = pltpu.roll(v, 1, 0)
        return jnp.concatenate([jnp.where(self.row_first, 0.0, v[:8]), v[8:]], axis=0)


def off_diagonal(sh, v, k, low, high, put):
    def spread(plane):
        up = sh.zup(plane)
        side, side_up = sh.yup(plane), sh.yup(up)
        return plane, up, side, side_up, plane + up, side + side_up

    near = spread(v(low - 1))
    carry = None
    for e in range(low - 1, high + 1):
        far = spread(v(e + 1))
        a, a_up, b, b_up, a_sum, b_sum = near
        c, c_up, d, d_up, c_sum, d_sum = far
        one_up, two_up = b_up + c_up, a_up + d_up
        one, two = b + c, a + d
        kk = k(e)
        if e >= low:
            e00, f00 = kk * (d_sum + one_up), kk * (d_sum + one)
            e01, f01 = kk * (c_sum + two_up), kk * (c_sum + two)
            e10, e11, f10, f11 = carry
            put(e, (e00 + e10) + sh.ydn(e01 + e11) + sh.zdn((f00 + f10) + sh.ydn(f01 + f11)))
        if e < high:
            carry = (
                kk * (b_sum + two_up),
                kk * (a_sum + one_up),
                kk * (b_sum + two),
                kk * (a_sum + one),
            )
        near = far


COARSE, HEAT, SLICE, SIDE, PART, CHIP, RIGID = 10, 20, 22, 23, 24, 25, 26


def fill_constants(heat_ref, coef_ref, time_ref, rigid_ref, dilate_ref, place_ref, const_ref):
    def put(at, value):
        const_ref[at : at + 1] = jnp.broadcast_to(value, (1, 128))

    def entry(ref, i):
        return jnp.broadcast_to(ref[0:1, i : i + 1], (1, 128))

    for first, dt in ((0, 1.0), (COARSE, 1.0 * PACES)):
        total = jnp.full((1, 128), 1.0 / dt, jnp.float32)
        for p in range(PRONY):
            decay = jnp.exp(-dt / entry(time_ref, p))
            f = entry(coef_ref, p) * decay
            put(first + p, decay)
            put(first + 3 + p, 1.0 - decay)
            put(first + 6 + p, f)
            total = total + f
        put(first + 9, total)
    put(HEAT, entry(heat_ref, 0))
    put(HEAT + 1, entry(heat_ref, PACES - 1))
    for i in range(4):
        put(SLICE + i, entry(place_ref, i))
    regions = rigid_ref.shape[1]
    for i in range(regions):
        put(RIGID + i, entry(rigid_ref, i))
        put(RIGID + regions + i, entry(dilate_ref, i))


def prony(const_ref, first):
    rows = [const_ref[first + i : first + i + 1] for i in range(10)]
    return rows[:3], rows[3:6], rows[6:9], rows[9]


def holds(const_ref, row, value, shape):
    return jnp.broadcast_to(const_ref[row : row + 1], shape) == float(value)


def moments_out(values, red_ref):
    lane = lax.broadcasted_iota(jnp.int32, (1, 128), 1)
    packed = jnp.zeros((1, 128), jnp.float32)
    for at, field in enumerate(values):
        total = jnp.sum(jnp.sum(field, axis=0, keepdims=True), axis=1, keepdims=True)
        packed = jnp.where(lane == at, total, packed)
    red_ref[...] = jnp.broadcast_to(packed[None], red_ref.shape)


def moments_in(red_ref, first, count):
    total = jnp.sum(red_ref[...], axis=0)
    lane = lax.broadcasted_iota(jnp.int32, (1, 128), 1)
    return [
        jnp.broadcast_to(
            jnp.sum(jnp.where(lane == first + i, total, 0.0), axis=1, keepdims=True), (1, 128)
        )
        for i in range(count)
    ]


def galerkin(nu):
    m = len(nu) // 2
    mu = [nu[i] + nu[i + 1] for i in range(2 * m - 1)]
    rows = [[mu[i + j] for j in range(m)] + [nu[i]] for i in range(m)]
    for i in range(m):
        for r in range(i + 1, m):
            factor = rows[r][i] / rows[i][i]
            for j in range(i + 1, m + 1):
                rows[r][j] = rows[r][j] - factor * rows[i][j]
    c = [None] * m
    for i in reversed(range(m)):
        acc = rows[i][m]
        for j in range(i + 1, m):
            acc = acc - rows[i][j] * c[j]
        c[i] = acc / rows[i][i]
    return c


def send(even_place, lo, hi, even_out, odd_out):
    for at, (low, high) in enumerate(zip(lo, hi)):
        even_out[at] = jnp.where(even_place, high, low)
        odd_out[at] = jnp.where(even_place, low, high)


def below(even_place, even_ref, odd_ref, at):
    return jnp.where(even_place, odd_ref[at], even_ref[at])


def above(even_place, even_ref, odd_ref, at):
    return jnp.where(even_place, even_ref[at], odd_ref[at])


def chosen(const_ref, row, values):
    value = values[-1]
    for v in range(len(values) - 1):
        value = jnp.where(holds(const_ref, row, v, value.shape), values[v], value)
    return value


def start_kernel(
    own_ref, even_ref, odd_ref, far_ref, const_ref,
    kel_ref, theta_ref, inv_f_ref, inv_c_ref, state_ref,
    zf_ref, ozf_ref, oozf_ref, zc_ref, ozc_ref,
    even_out, odd_out, far_out, red_ref,
    kal_ref, au_ref, w_ref,
):
    ny, nz = kel_ref.shape[1:]
    sh = Shifts(ny, nz)
    chunks = own_ref.shape[0]
    side = holds(const_ref, SIDE, 0, (ny, nz))
    side_part = holds(const_ref, SIDE, 0, (ny // chunks, nz))

    def raw(field, i):
        if i < 0:
            parts = [below(side_part, even_ref, odd_ref, (c, field, i + L)) for c in range(chunks)]
        elif i < L:
            parts = [own_ref[c, field, i] for c in range(chunks)]
        elif i < 2 * L:
            parts = [above(side_part, even_ref, odd_ref, (c, field, i - L)) for c in range(chunks)]
        else:
            parts = [far_ref[c, 0, 0] for c in range(chunks)]
        return jnp.concatenate(parts, axis=0)

    regions = (const_ref.shape[0] - RIGID) // 2
    table = [const_ref[RIGID + i : RIGID + i + 1] for i in range(2 * regions)]

    for e in range(-3, 6):
        label = raw(0, e)
        stiff = jnp.zeros((ny, nz), jnp.float32)
        load = jnp.zeros((ny, nz), jnp.float32)
        for region in range(regions):
            here = label == (region + 1.0)
            stiff = jnp.where(here, table[region], stiff)
            load = jnp.where(here, table[regions + region], load)
        kel_ref[e + 3] = stiff * (-1.0 / 12.0)
        kal_ref[e + 3] = 0.25 * (stiff * load)

    heat = [const_ref[HEAT + i : HEAT + i + 1] for i in range(2)]
    shift_f, shift_c = prony(const_ref, 0)[3], prony(const_ref, COARSE)[3]

    for i in range(-2, 6):
        ksum = kel_ref[i + 2] + kel_ref[i + 3]
        ksum = ksum + sh.ydn(ksum)
        ksum = ksum + sh.zdn(ksum)
        diag = -4.0 * ksum
        asum = kal_ref[i + 2] + kal_ref[i + 3]
        asum = asum + sh.ydn(asum)
        theta_ref[i + 2] = sh.zdn(asum) - asum
        inside = raw(0, i) > 0.5
        inv_f_ref[i + 2] = jnp.where(inside, 1.0 / (diag + shift_f), 0.0)
        inv_c_ref[i + 2] = jnp.where(inside, 1.0 / (diag + shift_c), 0.0)

    for i in range(-3, 7):
        state_ref[i + 3] = raw(1, i)

    def k(e):
        return kel_ref[e + 3]

    def put_au(i, plane):
        au_ref[i + 2] = plane

    off_diagonal(sh, lambda i: state_ref[i + 3], k, -2, 5, put_au)

    zeros = jnp.zeros((ny, nz), jnp.float32)
    acc = [zeros] * 10
    for i in range(-2, 6):
        later = raw(3, i)
        state_ref[10 + i + 2] = later
        ui = state_ref[i + 3]
        load = heat[0] * theta_ref[i + 2] + raw(2, i)
        s = load + ui - au_ref[i + 2]
        z = inv_f_ref[i + 2] * s - ui
        zf_ref[i + 2] = z
        if 0 <= i < L:
            acc[0] = acc[0] + z * (s - ui * (1.0 / inv_f_ref[i + 2]))
        if i < 5:
            load = heat[1] * theta_ref[i + 2] + later
            s = load + ui * (1.0 / PACES) - au_ref[i + 2]
            z = inv_c_ref[i + 2] * s - ui
            w_ref[i + 2] = z
            if 0 <= i < L:
                zc_ref[i] = z
                acc[6] = acc[6] + z * (s - ui * (1.0 / inv_c_ref[i + 2]))

    def put_oz(i, plane):
        oz = inv_f_ref[i + 2] * plane
        ozf_ref[i + 1] = oz
        if 0 <= i < L:
            acc[1] = acc[1] + zf_ref[i + 2] * plane
            acc[2] = acc[2] + oz * plane

    off_diagonal(sh, lambda i: zf_ref[i + 2], k, -1, 4, put_oz)

    def put_ooz(i, plane):
        ooz = inv_f_ref[i + 2] * plane
        oozf_ref[i] = ooz
        if i < L:
            acc[3] = acc[3] + ozf_ref[i + 1] * plane
            acc[4] = acc[4] + ooz * plane

    off_diagonal(sh, lambda i: ozf_ref[i + 1], k, 0, 3, put_ooz)

    def put_last(i, plane):
        acc[5] = acc[5] + oozf_ref[i] * plane

    by_elements(sh, lambda i: oozf_ref[i], k, put_last)

    def put_ozc(i, plane):
        oz = inv_c_ref[i + 2] * plane
        au_ref[i + 2] = oz
        if 0 <= i < L:
            ozc_ref[i] = oz
            acc[7] = acc[7] + w_ref[i + 2] * plane
            acc[8] = acc[8] + oz * plane

    off_diagonal(sh, lambda i: w_ref[i + 2], k, -1, 3, put_ozc)

    def put_lastc(i, plane):
        acc[9] = acc[9] + au_ref[i + 2] * plane

    off_diagonal(sh, lambda i: au_ref[i + 2], k, 0, 2, put_lastc)
    moments_out(acc, red_ref)

    hi = [zf_ref[2], ozf_ref[1], ozf_ref[2], oozf_ref[0], oozf_ref[1], oozf_ref[2]]
    lo = [ozf_ref[3], oozf_ref[1], oozf_ref[2]]
    send(side, lo + lo, hi, even_out, odd_out)
    far_out[0], far_out[1], far_out[2] = zf_ref[2], ozf_ref[1], oozf_ref[0]


def by_elements(sh, v, k, put):
    none = jnp.zeros((sh.ny, sh.nz), jnp.float32)

    def nodes(i):
        return v(i) if 0 <= i <= L else none

    def elements(e):
        return k(e) if 0 <= e < L else none

    off_diagonal(sh, nodes, elements, 0, L, put)


def second_kernel(
    const_ref, red_in, kel_ref, theta_ref, inv_f_ref, state_ref, own_ref,
    zf_ref, ozf_ref, oozf_ref, zc_ref, ozc_ref,
    even_ref, odd_ref, far_ref,
    base_ref, z_out, oz_out, ooz_out, red_ref,
    u_ref, z_ref, oz_ref, ooz_ref, au_ref,
):
    ny, nz = kel_ref.shape[1:]
    sh = Shifts(ny, nz)
    chunks = own_ref.shape[0]
    decay_f, rest_f, ff, shift_f = prony(const_ref, 0)
    decay_c, rest_c, fc, shift_c = prony(const_ref, COARSE)
    c = galerkin(moments_in(red_in, 0, 6))
    b = galerkin(moments_in(red_in, 6, 4))
    side = holds(const_ref, SIDE, 0, (ny, nz))
    heat = const_ref[HEAT + 1 : HEAT + 2]

    def basis(i, at, ref, low, high, up, down):
        if i == 6:
            return far_ref[at]
        if i < low:
            return below(side, even_ref, odd_ref, up + i + L)
        if i > high:
            return above(side, even_ref, odd_ref, down + i - high - 1)
        return ref[i - low]

    for i in range(-3, 7):
        z = basis(i, 0, zf_ref, -2, 5, 0, None)
        oz = basis(i, 1, ozf_ref, -1, 4, 1, 0)
        ooz = basis(i, 2, oozf_ref, 0, 3, 3, 1)
        u_ref[i + 3] = state_ref[i + 3] + c[0] * z + c[1] * oz + c[2] * ooz

    def k(e):
        return kel_ref[e + 3]

    def put_au(i, plane):
        au_ref[i + 2] = plane

    off_diagonal(sh, lambda i: u_ref[i + 3], k, -2, 5, put_au)

    grow = ff[0] * rest_f[0] + ff[1] * rest_f[1] + ff[2] * rest_f[2]
    zeros = jnp.zeros((ny, nz), jnp.float32)
    acc = [zeros] * 6
    weight = jnp.where(holds(const_ref, SLICE, 0, (1, nz)), 0.0, 1.0)
    for i in range(-2, 6):
        ui = u_ref[i + 3]
        s = heat * theta_ref[i + 2] + state_ref[10 + i + 2] + (grow + 1.0) * ui
        s = s - au_ref[i + 2]
        z = inv_f_ref[i + 2] * s - ui
        z_ref[i + 2] = z
        if 0 <= i < L:
            z_out[i] = z
            acc[0] = acc[0] + z * (s - ui * (1.0 / inv_f_ref[i + 2]))

    for i in range(L):
        u1 = u_ref[i + 3]
        g = state_ref[i + 3] + b[0] * zc_ref[i] + b[1] * ozc_ref[i]
        base_ref[i] = u1 - weight * g
        for p in range(PRONY):
            h = jnp.concatenate([own_ref[q, p, i] for q in range(chunks)], axis=0)
            h1 = decay_f[p] * h + rest_f[p] * u1
            gh = decay_c[p] * h + rest_c[p] * g
            base_ref[L * (1 + p) + i] = decay_f[p] * h1 + rest_f[p] * u1 - weight * gh

    def put_oz(i, plane):
        oz = inv_f_ref[i + 2] * plane
        oz_ref[i + 1] = oz
        if 0 <= i < L:
            oz_out[i] = oz
            acc[1] = acc[1] + z_ref[i + 2] * plane
            acc[2] = acc[2] + oz * plane

    off_diagonal(sh, lambda i: z_ref[i + 2], k, -1, 4, put_oz)

    def put_ooz(i, plane):
        ooz = inv_f_ref[i + 2] * plane
        ooz_ref[i] = ooz
        if i < L:
            ooz_out[i] = ooz
            acc[3] = acc[3] + oz_ref[i + 1] * plane
            acc[4] = acc[4] + ooz * plane

    off_diagonal(sh, lambda i: oz_ref[i + 1], k, 0, 3, put_ooz)

    def put_last(i, plane):
        acc[5] = acc[5] + ooz_ref[i] * plane

    by_elements(sh, lambda i: ooz_ref[i], k, put_last)
    moments_out(acc, red_ref)


def block_kernel(const_ref, red_in, base_ref, z_ref, oz_ref, ooz_ref, blk_ref):
    decay_f, rest_f, ff, shift_f = prony(const_ref, 0)
    c = galerkin(moments_in(red_in, 0, 6))
    ny = z_ref.shape[1]
    for i in range(L):
        delta = c[0] * z_ref[i] + c[1] * oz_ref[i] + c[2] * ooz_ref[i]
        blk_ref[i * ny : (i + 1) * ny] = base_ref[i] + delta
        for p in range(PRONY):
            at = L * (1 + p) + i
            blk_ref[at * ny : (at + 1) * ny] = base_ref[at] + rest_f[p] * delta
    blk_ref[4 * L * ny :] = jnp.broadcast_to(const_ref[HEAT + 1 : HEAT + 2], (8, blk_ref.shape[1]))


def halo_base(f, base_ref):
    sums = [
        f[0] * base_ref[L + i] + f[1] * base_ref[2 * L + i] + f[2] * base_ref[3 * L + i]
        for i in range(L)
    ]
    u = [base_ref[i] for i in range(L)]
    return u + [sums[0], sums[1]], u + [sums[1], sums[2]]


def opening_kernel(const_ref, blk_ref, base_ref, even_out, odd_out):
    decay, rest, f, shift = prony(const_ref, COARSE)
    ny = even_out.shape[1]
    for at in range(4 * L):
        base_ref[at] = blk_ref[at * ny : (at + 1) * ny]
    lo, hi = halo_base(f, base_ref)
    send(holds(const_ref, SIDE, 0, even_out.shape[1:]), lo, hi, even_out, odd_out)


def chain_kernel(turn, count, opened, rounds, *refs):
    refs = list(refs)
    const_ref = refs.pop(0)
    if opened:
        base_in, even_ref, odd_ref = refs[:3]
        refs = refs[3:]
    else:
        red_in, base_in, z_in, oz_in, even_ref, odd_ref = refs[:6]
        refs = refs[6:]
    kel_ref, theta_ref, inv_ref, blk_ref = refs[:4]
    if rounds:
        outs, (red_ref, u_ref, au_ref, base_ref, z_ref, oz_ref) = refs[4 : 4 + rounds], refs[4 + rounds :]
    else:
        base_ref, z_ref, oz_ref, even_out, odd_out, red_ref, u_ref, au_ref = refs[4:]
    ny, nz = kel_ref.shape[1:]
    sh = Shifts(ny, nz)
    decay, rest, f, shift = prony(const_ref, COARSE)
    grow = f[0] * rest[0] + f[1] * rest[1] + f[2] * rest[2]
    heat = blk_ref[4 * L * ny : 4 * L * ny + 1]
    opening = holds(const_ref, SLICE, -turn % count, (ny, nz))
    fresh = holds(const_ref, SLICE, (1 - turn) % count, (ny, nz))
    side = holds(const_ref, SIDE, 0, (ny, nz))

    if not opened:
        c = galerkin(moments_in(red_in, 0, 4))

    def near(i, low_at, high_at):
        if i < 0:
            return below(side, even_ref, odd_ref, low_at)
        return above(side, even_ref, odd_ref, high_at)

    def delta(i):
        z = z_in[i + 2] if -2 <= i <= 4 else near(i, 5, 5)
        if -1 <= i <= 3:
            oz = oz_in[i + 1]
        else:
            at = 6 if i in (-3, 5) else 7
            oz = near(i, at, at)
        return jnp.where(fresh, 0.0, c[0] * z + c[1] * oz)

    for i in range(-3, 6):
        base = base_in[i] if 0 <= i < L else near(i, i + 3, i - L)
        d = None if opened else delta(i)
        u_ref[i + 3] = base if opened else base + d
        if 0 <= i < L:
            h = [base_in[L * (1 + p) + i] for p in range(PRONY)]
            if not opened:
                h = [h[p] + rest[p] * d for p in range(PRONY)]
            total = f[0] * h[0] + f[1] * h[1] + f[2] * h[2]
            ui = u_ref[i + 3]
            base_ref[i] = jnp.where(opening, 0.0, ui) + blk_ref[i * ny : (i + 1) * ny]
            for p in range(PRONY):
                at = L * (1 + p) + i
                ahead = jnp.where(opening, 0.0, decay[p] * h[p] + rest[p] * ui)
                base_ref[at] = ahead + blk_ref[at * ny : (at + 1) * ny]
        elif -2 <= i < 5:
            total = near(i, 3 + i + 2, 3 + i - L)
            if not opened:
                total = total + grow * d
        if -2 <= i < 5:
            au_ref[i + 2] = heat * theta_ref[i + 2] + total

    zeros = jnp.zeros((ny, nz), jnp.float32)
    acc = [zeros] * 4

    def k(e):
        return kel_ref[e + 3]

    def put_z(i, plane):
        ui = u_ref[i + 3]
        s = au_ref[i + 2] + ui * (1.0 / PACES) - plane
        inv = inv_ref[i + 2]
        z = inv * s - ui
        z_ref[i + 2] = z
        if 0 <= i < L:
            acc[0] = acc[0] + z * (s - ui * (1.0 / inv))

    off_diagonal(sh, lambda i: u_ref[i + 3], k, -2, 4, put_z)

    def put_oz(i, plane):
        oz = inv_ref[i + 2] * plane
        oz_ref[i + 1] = oz
        if 0 <= i < L:
            acc[1] = acc[1] + z_ref[i + 2] * plane
            acc[2] = acc[2] + oz * plane

    off_diagonal(sh, lambda i: z_ref[i + 2], k, -1, 3, put_oz)

    def put_last(i, plane):
        acc[3] = acc[3] + oz_ref[i + 1] * plane

    off_diagonal(sh, lambda i: oz_ref[i + 1], k, 0, 2, put_last)
    moments_out(acc, red_ref)

    if rounds:
        width = ny // rounds
        for i in range(L):
            fields = [base_ref[L * field + i] for field in range(1 + PRONY)]
            for at, field in enumerate(fields + [z_ref[i + 2], oz_ref[i + 1]]):
                cuts = [field[q * width : (q + 1) * width] for q in range(rounds)]
                for r, out_ref in enumerate(outs):
                    ahead = [cuts[(v + r) % rounds] for v in range(rounds)]
                    out_ref[at, i] = chosen(const_ref, PART, ahead)
        return

    lo, hi = halo_base(f, base_ref)
    lo = lo + [z_ref[2 + 2], oz_ref[2 + 1], oz_ref[1 + 1]]
    hi = hi + [z_ref[0 + 2], oz_ref[0 + 1], oz_ref[1 + 1]]
    send(side, lo, hi, even_out, odd_out)


def closing_kernel(const_ref, red_in, *refs):
    parts, out_ref = refs[:-1], refs[-1]
    decay, rest, f, shift = prony(const_ref, COARSE)
    c = galerkin(moments_in(red_in, 0, 4))
    first = holds(const_ref, SLICE, 0, out_ref.shape[3:])
    count = len(parts)
    for k in range(count):
        for i in range(L):
            base_u, *base_h, z, oz = [
                chosen(const_ref, CHIP, [parts[(v - k) % count][at, i] for v in range(count)])
                for at in range(3 + PRONY)
            ]
            delta = jnp.where(first, 0.0, c[0] * z + c[1] * oz)
            out_ref[0, 0, k * L + i] = base_u + delta
            for p in range(PRONY):
                out_ref[0, 1 + p, k * L + i] = base_h[p] + rest[p] * delta


def spread_kernel(
    heat_ref, coef_ref, time_ref, rigid_ref, dilate_ref, place_ref, label_ref, values_ref,
    const_ref, *out_refs,
):
    fill_constants(heat_ref, coef_ref, time_ref, rigid_ref, dilate_ref, place_ref, const_ref)
    count = len(out_refs)
    for i in range(L):
        labels = [label_ref[k * L + i].astype(jnp.float32) + 1.0 for k in range(count)]
        fields = [labels]
        for field in range(1 + PRONY):
            fields.append([values_ref[0, field, k * L + i] for k in range(count)])
        for at, blocks in enumerate(fields):
            for r, out_ref in enumerate(out_refs):
                ahead = [blocks[(v - r) % count] for v in range(count)]
                out_ref[at, i] = chosen(const_ref, CHIP, ahead)


def join_kernel(const_ref, *refs):
    got_refs, (out_ref, past_ref) = refs[:-2], refs[-2:]
    decay, rest, f, shift = prony(const_ref, 0)
    count = len(got_refs)
    for q in range(count):
        for i in range(L):
            label, u, *h = [
                chosen(const_ref, PART, [got_refs[(q - v) % count][at, i] for v in range(count)])
                for at in range(2 + PRONY)
            ]
            fh = [f[p] * h[p] for p in range(PRONY)]
            out_ref[q, 0, i], out_ref[q, 1, i] = label, u
            out_ref[q, 2, i] = fh[0] + fh[1] + fh[2]
            out_ref[q, 3, i] = decay[0] * fh[0] + decay[1] * fh[1] + decay[2] * fh[2]
            for p in range(PRONY):
                past_ref[q, p, i] = h[p]


VMEM = pl.BlockSpec(memory_space=pltpu.VMEM)


def call(kernel, name, arrays, outs, scratch=()):
    f32 = jnp.float32
    return pl.pallas_call(
        kernel,
        name=name,
        out_shape=[jax.ShapeDtypeStruct(s, f32) for s in outs],
        in_specs=[VMEM] * len(arrays),
        out_specs=[VMEM] * len(outs),
        scratch_shapes=[pltpu.VMEM(s, f32) for s in scratch],
        compiler_params=pltpu.CompilerParams(vmem_limit_bytes=LIMIT),
    )(*arrays)


def on_device(
    segment_opening_values,
    cell_material_label,
    material_rigidity,
    dilation_mismatch,
    heat_swings_array,
    prony_coefficients,
    prony_decay_times,
):
    n_tm, n_gy = lax.axis_size("tm"), lax.axis_size("gy")
    line = lax.axis_size("gx") * n_gy
    nx, ny_part, nz = cell_material_label.shape
    ny = ny_part * n_gy
    assert nx == L * n_gy and n_gy == 4
    plane = (ny, nz)

    def device(position):
        row, rest = divmod(position, 2 * n_gy)
        x, core = divmod(rest, 2)
        return (2 * row + core) * n_gy + (x if row % 2 == 0 else n_gy - 1 - x)

    def deal(values, back=False):
        received = []
        for r, value in enumerate(values):
            perm = []
            for position in range(line):
                row, rest = divmod(position, 2 * n_gy)
                x, core = divmod(rest, 2)
                to = (2 * row + x // 2) * n_gy + (2 * (x % 2) + core + r) % n_gy
                perm.append((to, device(position)) if back else (device(position), to))
            received.append(lax.ppermute(value, LINE, sorted(perm)))
        return received

    def trade(even, odd):
        received = []
        for side, value in enumerate((even, odd)):
            pairs = [(device(p), device(p + 1)) for p in range(side, line - 1, 2)]
            both = pairs + [(b, a) for a, b in pairs]
            received.append(lax.ppermute(value, LINE, sorted(both)))
        return received

    def from_next_but_one(value):
        perm = [(device(p + 2), device(p)) for p in range(line - 2)]
        return lax.ppermute(value, LINE, sorted(perm))

    def exchanged(red):
        return lax.all_to_all(red, LINE, 0, 0, tiled=True)

    def ring(block):
        return lax.ppermute(block, "tm", [(s, (s - 1) % n_tm) for s in range(n_tm)])

    gx, gy = lax.axis_index("gx"), lax.axis_index("gy")
    core, flip = gx % 2, gx // 2 % 2
    x = jnp.where(flip == 0, gy, n_gy - 1 - gy)
    place = jnp.stack([lax.axis_index("tm"), core, 2 * (x % 2) + core, gy])
    place = place.astype(jnp.float32)[None]
    regions = material_rigidity.shape[0]
    tables = (prony_coefficients, prony_decay_times, material_rigidity, dilation_mismatch)

    const, *parts = call(
        spread_kernel,
        "spread",
        (
            heat_swings_array,
            *[table[None] for table in tables],
            place,
            cell_material_label,
            segment_opening_values,
        ),
        [(RIGID + 2 * regions, nz)] + [(2 + PRONY, L, ny_part, nz)] * n_gy,
    )
    own, past = call(
        join_kernel,
        "join",
        (const, *deal(parts, True)),
        [(n_gy, 4, L, ny_part, nz), (n_gy, PRONY, L, ny_part, nz)],
    )
    near, far = trade(own, own), from_next_but_one(own[:, 1:2, :1])

    red_shape = (line, 1, 128)
    (kel, theta, inv_f, inv_c, state, zf, ozf, oozf, zc, ozc, even, odd, far, red) = call(
        start_kernel,
        "start",
        (own, *near, far, const),
        [
            (9, *plane), (8, *plane), (8, *plane), (8, *plane), (18, *plane),
            (8, *plane), (6, *plane), (4, *plane), (L, *plane), (L, *plane),
            (6, *plane), (6, *plane), (3, *plane), red_shape,
        ],
        [(9, *plane), (8, *plane), (7, *plane)],
    )
    red = exchanged(red)
    near, far = trade(even, odd), from_next_but_one(far)
    base, z, oz, ooz, red = call(
        second_kernel,
        "second",
        (const, red, kel, theta, inv_f, state, past, zf, ozf, oozf, zc, ozc, *near, far),
        [(4 * L, *plane), (L, *plane), (L, *plane), (L, *plane), red_shape],
        [(10, *plane), (8, *plane), (6, *plane), (4, *plane), (8, *plane)],
    )
    red = exchanged(red)
    (block,) = call(
        block_kernel,
        "block",
        (const, red, base, z, oz, ooz),
        [(4 * L * ny + 8, nz)],
    )
    mine = block
    block = ring(block)
    base, even, odd = call(
        opening_kernel,
        "opening",
        (const, block),
        [(4 * L, *plane), (5, *plane), (5, *plane)],
    )
    past = (base,)
    for turn in range(2, n_tm + 1):
        if turn < n_tm:
            block, even = lax.optimization_barrier((block, even))
            block = ring(block)
        else:
            block = mine
        past = (*past, *trade(even, odd))
        last = turn == n_tm
        state = [(4 * L, *plane), (7, *plane), (5, *plane)]
        work = [(9, *plane), (7, *plane)]
        *outs, red = call(
            functools.partial(chain_kernel, turn, n_tm, turn == 2, n_gy if last else 0),
            f"chain{turn}",
            (const, *past, kel, theta, inv_c, block),
            [(3 + PRONY, L, ny_part, nz)] * n_gy + [red_shape]
            if last
            else [*state, (8, *plane), (8, *plane), red_shape],
            work + state if last else work,
        )
        if last:
            break
        base, z, oz, even, odd = outs
        past = (exchanged(red), base, z, oz)
    parts = deal(outs)
    (out,) = call(
        closing_kernel,
        "closing",
        (const, exchanged(red), *parts),
        [(1, 1 + PRONY, nx, ny_part, nz)],
    )
    return out


def solution(mesh):
    placed = (
        P("tm", None, "gx", "gy", None),
        P("gx", "gy", None),
        P(),
        P(),
        P("tm", None),
        P(),
        P(),
    )
    return jax.shard_map(
        on_device,
        mesh=mesh,
        in_specs=placed,
        out_specs=P("tm", None, "gx", "gy", None),
        check_vma=False,
    )
```

```python
import functools

import jax
import jax.numpy as jnp
from jax import lax
from jax.experimental import pallas as pl
from jax.experimental.pallas import tpu as pltpu
from jax.sharding import PartitionSpec as P

PACES = 2
SHARP = 3
LOOSE = 2
PRONY = 3
L = 3
LINE = ("gx", "gy")
LIMIT = 14 << 20


class Shifts:
    def __init__(self, ny, nz):
        self.ny, self.nz = ny, nz
        lane = lax.broadcasted_iota(jnp.int32, (ny, nz), 1)
        row = lax.broadcasted_iota(jnp.int32, (8, nz), 0)
        self.lane_first, self.lane_last = lane == 0, lane == nz - 1
        self.row_first, self.row_last = row == 0, row == 7

    def zup(self, v):
        return jnp.where(self.lane_last, 0.0, pltpu.roll(v, self.nz - 1, 1))

    def zdn(self, v):
        return jnp.where(self.lane_first, 0.0, pltpu.roll(v, 1, 1))

    def yup(self, v):
        v = pltpu.roll(v, self.ny - 1, 0)
        end = jnp.where(self.row_last, 0.0, v[self.ny - 8 :])
        return jnp.concatenate([v[: self.ny - 8], end], axis=0)

    def ydn(self, v):
        v = pltpu.roll(v, 1, 0)
        return jnp.concatenate([jnp.where(self.row_first, 0.0, v[:8]), v[8:]], axis=0)


def off_diagonal(sh, v, k, low, high, put):
    def spread(plane):
        up = sh.zup(plane)
        side, side_up = sh.yup(plane), sh.yup(up)
        return plane, up, side, side_up, plane + up, side + side_up

    near = spread(v(low - 1))
    carry = None
    for e in range(low - 1, high + 1):
        far = spread(v(e + 1))
        a, a_up, b, b_up, a_sum, b_sum = near
        c, c_up, d, d_up, c_sum, d_sum = far
        one_up, two_up = b_up + c_up, a_up + d_up
        one, two = b + c, a + d
        kk = k(e)
        if e >= low:
            e00, f00 = kk * (d_sum + one_up), kk * (d_sum + one)
            e01, f01 = kk * (c_sum + two_up), kk * (c_sum + two)
            e10, e11, f10, f11 = carry
            put(e, (e00 + e10) + sh.ydn(e01 + e11) + sh.zdn((f00 + f10) + sh.ydn(f01 + f11)))
        if e < high:
            carry = (
                kk * (b_sum + two_up),
                kk * (a_sum + one_up),
                kk * (b_sum + two),
                kk * (a_sum + one),
            )
        near = far


COARSE, HEAT, SLICE, SIDE, PART, CHIP, RIGID = 10, 20, 22, 23, 24, 25, 26


def fill_constants(heat_ref, coef_ref, time_ref, rigid_ref, dilate_ref, place_ref, const_ref):
    def put(at, value):
        const_ref[at : at + 1] = jnp.broadcast_to(value, (1, 128))

    def entry(ref, i):
        return jnp.broadcast_to(ref[0:1, i : i + 1], (1, 128))

    for first, dt in ((0, 1.0), (COARSE, 1.0 * PACES)):
        total = jnp.full((1, 128), 1.0 / dt, jnp.float32)
        for p in range(PRONY):
            decay = jnp.exp(-dt / entry(time_ref, p))
            f = entry(coef_ref, p) * decay
            put(first + p, decay)
            put(first + 3 + p, 1.0 - decay)
            put(first + 6 + p, f)
            total = total + f
        put(first + 9, total)
    put(HEAT, entry(heat_ref, 0))
    put(HEAT + 1, entry(heat_ref, PACES - 1))
    for i in range(4):
        put(SLICE + i, entry(place_ref, i))
    regions = rigid_ref.shape[1]
    for i in range(regions):
        put(RIGID + i, entry(rigid_ref, i))
        put(RIGID + regions + i, entry(dilate_ref, i))


def prony(const_ref, first):
    rows = [const_ref[first + i : first + i + 1] for i in range(10)]
    return rows[:3], rows[3:6], rows[6:9], rows[9]


def holds(const_ref, row, value, shape):
    return jnp.broadcast_to(const_ref[row : row + 1], shape) == float(value)


def moments_out(values, red_ref):
    lane = lax.broadcasted_iota(jnp.int32, (1, 128), 1)
    packed = jnp.zeros((1, 128), jnp.float32)
    for at, field in enumerate(values):
        total = jnp.sum(jnp.sum(field, axis=0, keepdims=True), axis=1, keepdims=True)
        packed = jnp.where(lane == at, total, packed)
    red_ref[...] = jnp.broadcast_to(packed[None], red_ref.shape)


def moments_in(red_ref, first, count):
    total = jnp.sum(red_ref[...], axis=0)
    lane = lax.broadcasted_iota(jnp.int32, (1, 128), 1)
    return [
        jnp.broadcast_to(
            jnp.sum(jnp.where(lane == first + i, total, 0.0), axis=1, keepdims=True), (1, 128)
        )
        for i in range(count)
    ]


def galerkin(nu):
    m = len(nu) // 2
    mu = [nu[i] + nu[i + 1] for i in range(2 * m - 1)]
    rows = [[mu[i + j] for j in range(m)] + [nu[i]] for i in range(m)]
    for i in range(m):
        for r in range(i + 1, m):
            factor = rows[r][i] / rows[i][i]
            for j in range(i + 1, m + 1):
                rows[r][j] = rows[r][j] - factor * rows[i][j]
    c = [None] * m
    for i in reversed(range(m)):
        acc = rows[i][m]
        for j in range(i + 1, m):
            acc = acc - rows[i][j] * c[j]
        c[i] = acc / rows[i][i]
    return c


def send(even_place, lo, hi, even_out, odd_out):
    for at, (low, high) in enumerate(zip(lo, hi)):
        even_out[at] = jnp.where(even_place, high, low)
        odd_out[at] = jnp.where(even_place, low, high)


def below(even_place, even_ref, odd_ref, at):
    return jnp.where(even_place, odd_ref[at], even_ref[at])


def above(even_place, even_ref, odd_ref, at):
    return jnp.where(even_place, even_ref[at], odd_ref[at])


def chosen(const_ref, row, values):
    value = values[-1]
    for v in range(len(values) - 1):
        value = jnp.where(holds(const_ref, row, v, value.shape), values[v], value)
    return value


def start_kernel(
    own_ref, even_ref, odd_ref, far_ref, const_ref,
    kel_ref, theta_ref, inv_f_ref, inv_c_ref, state_ref,
    zf_ref, ozf_ref, oozf_ref, zc_ref, ozc_ref,
    even_out, odd_out, far_out, red_ref,
    kal_ref, au_ref, w_ref,
):
    ny, nz = kel_ref.shape[1:]
    sh = Shifts(ny, nz)
    chunks = own_ref.shape[0]
    side = holds(const_ref, SIDE, 0, (ny, nz))
    side_part = holds(const_ref, SIDE, 0, (ny // chunks, nz))

    def raw(field, i):
        if i < 0:
            parts = [below(side_part, even_ref, odd_ref, (c, field, i + L)) for c in range(chunks)]
        elif i < L:
            parts = [own_ref[c, field, i] for c in range(chunks)]
        elif i < 2 * L:
            parts = [above(side_part, even_ref, odd_ref, (c, field, i - L)) for c in range(chunks)]
        else:
            parts = [far_ref[c, 0, 0] for c in range(chunks)]
        return jnp.concatenate(parts, axis=0)

    regions = (const_ref.shape[0] - RIGID) // 2
    table = [const_ref[RIGID + i : RIGID + i + 1] for i in range(2 * regions)]

    for e in range(-3, 6):
        label = raw(0, e)
        stiff = jnp.zeros((ny, nz), jnp.float32)
        load = jnp.zeros((ny, nz), jnp.float32)
        for region in range(regions):
            here = label == (region + 1.0)
            stiff = jnp.where(here, table[region], stiff)
            load = jnp.where(here, table[regions + region], load)
        kel_ref[e + 3] = stiff * (-1.0 / 12.0)
        kal_ref[e + 3] = 0.25 * (stiff * load)

    heat = [const_ref[HEAT + i : HEAT + i + 1] for i in range(2)]
    shift_f, shift_c = prony(const_ref, 0)[3], prony(const_ref, COARSE)[3]

    for i in range(-2, 6):
        ksum = kel_ref[i + 2] + kel_ref[i + 3]
        ksum = ksum + sh.ydn(ksum)
        ksum = ksum + sh.zdn(ksum)
        diag = -4.0 * ksum
        asum = kal_ref[i + 2] + kal_ref[i + 3]
        asum = asum + sh.ydn(asum)
        theta_ref[i + 2] = sh.zdn(asum) - asum
        inside = raw(0, i) > 0.5
        inv_f_ref[i + 2] = jnp.where(inside, 1.0 / (diag + shift_f), 0.0)
        inv_c_ref[i + 2] = jnp.where(inside, 1.0 / (diag + shift_c), 0.0)

    for i in range(-3, 7):
        state_ref[i + 3] = raw(1, i)

    def k(e):
        return kel_ref[e + 3]

    def put_au(i, plane):
        au_ref[i + 2] = plane

    off_diagonal(sh, lambda i: state_ref[i + 3], k, -2, 5, put_au)

    zeros = jnp.zeros((ny, nz), jnp.float32)
    acc = [zeros] * 10
    for i in range(-2, 6):
        later = raw(3, i)
        state_ref[10 + i + 2] = later
        ui = state_ref[i + 3]
        load = heat[0] * theta_ref[i + 2] + raw(2, i)
        s = load + ui - au_ref[i + 2]
        z = inv_f_ref[i + 2] * s - ui
        zf_ref[i + 2] = z
        if 0 <= i < L:
            acc[0] = acc[0] + z * (s - ui * (1.0 / inv_f_ref[i + 2]))
        if i < 5:
            load = heat[1] * theta_ref[i + 2] + later
            s = load + ui * (1.0 / PACES) - au_ref[i + 2]
            z = inv_c_ref[i + 2] * s - ui
            w_ref[i + 2] = z
            if 0 <= i < L:
                zc_ref[i] = z
                acc[6] = acc[6] + z * (s - ui * (1.0 / inv_c_ref[i + 2]))

    def put_oz(i, plane):
        oz = inv_f_ref[i + 2] * plane
        ozf_ref[i + 1] = oz
        if 0 <= i < L:
            acc[1] = acc[1] + zf_ref[i + 2] * plane
            acc[2] = acc[2] + oz * plane

    off_diagonal(sh, lambda i: zf_ref[i + 2], k, -1, 4, put_oz)

    def put_ooz(i, plane):
        ooz = inv_f_ref[i + 2] * plane
        oozf_ref[i] = ooz
        if i < L:
            acc[3] = acc[3] + ozf_ref[i + 1] * plane
            acc[4] = acc[4] + ooz * plane

    off_diagonal(sh, lambda i: ozf_ref[i + 1], k, 0, 3, put_ooz)

    def put_last(i, plane):
        acc[5] = acc[5] + oozf_ref[i] * plane

    by_elements(sh, lambda i: oozf_ref[i], k, put_last)

    def put_ozc(i, plane):
        oz = inv_c_ref[i + 2] * plane
        au_ref[i + 2] = oz
        if 0 <= i < L:
            ozc_ref[i] = oz
            acc[7] = acc[7] + w_ref[i + 2] * plane
            acc[8] = acc[8] + oz * plane

    off_diagonal(sh, lambda i: w_ref[i + 2], k, -1, 3, put_ozc)

    def put_lastc(i, plane):
        acc[9] = acc[9] + au_ref[i + 2] * plane

    off_diagonal(sh, lambda i: au_ref[i + 2], k, 0, 2, put_lastc)
    moments_out(acc, red_ref)

    hi = [zf_ref[2], ozf_ref[1], ozf_ref[2], oozf_ref[0], oozf_ref[1], oozf_ref[2]]
    lo = [ozf_ref[3], oozf_ref[1], oozf_ref[2]]
    send(side, lo + lo, hi, even_out, odd_out)
    far_out[0], far_out[1], far_out[2] = zf_ref[2], ozf_ref[1], oozf_ref[0]


def by_elements(sh, v, k, put):
    none = jnp.zeros((sh.ny, sh.nz), jnp.float32)

    def nodes(i):
        return v(i) if 0 <= i <= L else none

    def elements(e):
        return k(e) if 0 <= e < L else none

    off_diagonal(sh, nodes, elements, 0, L, put)


def second_kernel(
    const_ref, red_in, kel_ref, theta_ref, inv_f_ref, state_ref, own_ref,
    zf_ref, ozf_ref, oozf_ref, zc_ref, ozc_ref,
    even_ref, odd_ref, far_ref,
    base_ref, z_out, oz_out, ooz_out, red_ref,
    u_ref, z_ref, oz_ref, ooz_ref, au_ref,
):
    ny, nz = kel_ref.shape[1:]
    sh = Shifts(ny, nz)
    chunks = own_ref.shape[0]
    decay_f, rest_f, ff, shift_f = prony(const_ref, 0)
    decay_c, rest_c, fc, shift_c = prony(const_ref, COARSE)
    c = galerkin(moments_in(red_in, 0, 6))
    b = galerkin(moments_in(red_in, 6, 4))
    side = holds(const_ref, SIDE, 0, (ny, nz))
    heat = const_ref[HEAT + 1 : HEAT + 2]

    def basis(i, at, ref, low, high, up, down):
        if i == 6:
            return far_ref[at]
        if i < low:
            return below(side, even_ref, odd_ref, up + i + L)
        if i > high:
            return above(side, even_ref, odd_ref, down + i - high - 1)
        return ref[i - low]

    for i in range(-3, 7):
        z = basis(i, 0, zf_ref, -2, 5, 0, None)
        oz = basis(i, 1, ozf_ref, -1, 4, 1, 0)
        ooz = basis(i, 2, oozf_ref, 0, 3, 3, 1)
        u_ref[i + 3] = state_ref[i + 3] + c[0] * z + c[1] * oz + c[2] * ooz

    def k(e):
        return kel_ref[e + 3]

    def put_au(i, plane):
        au_ref[i + 2] = plane

    off_diagonal(sh, lambda i: u_ref[i + 3], k, -2, 5, put_au)

    grow = ff[0] * rest_f[0] + ff[1] * rest_f[1] + ff[2] * rest_f[2]
    zeros = jnp.zeros((ny, nz), jnp.float32)
    acc = [zeros] * 6
    weight = jnp.where(holds(const_ref, SLICE, 0, (1, nz)), 0.0, 1.0)
    for i in range(-2, 6):
        ui = u_ref[i + 3]
        s = heat * theta_ref[i + 2] + state_ref[10 + i + 2] + (grow + 1.0) * ui
        s = s - au_ref[i + 2]
        z = inv_f_ref[i + 2] * s - ui
        z_ref[i + 2] = z
        if 0 <= i < L:
            z_out[i] = z
            acc[0] = acc[0] + z * (s - ui * (1.0 / inv_f_ref[i + 2]))

    for i in range(L):
        u1 = u_ref[i + 3]
        g = state_ref[i + 3] + b[0] * zc_ref[i] + b[1] * ozc_ref[i]
        base_ref[i] = u1 - weight * g
        for p in range(PRONY):
            h = jnp.concatenate([own_ref[q, p, i] for q in range(chunks)], axis=0)
            h1 = decay_f[p] * h + rest_f[p] * u1
            gh = decay_c[p] * h + rest_c[p] * g
            base_ref[L * (1 + p) + i] = decay_f[p] * h1 + rest_f[p] * u1 - weight * gh

    def put_oz(i, plane):
        oz = inv_f_ref[i + 2] * plane
        oz_ref[i + 1] = oz
        if 0 <= i < L:
            oz_out[i] = oz
            acc[1] = acc[1] + z_ref[i + 2] * plane
            acc[2] = acc[2] + oz * plane

    off_diagonal(sh, lambda i: z_ref[i + 2], k, -1, 4, put_oz)

    def put_ooz(i, plane):
        ooz = inv_f_ref[i + 2] * plane
        ooz_ref[i] = ooz
        if i < L:
            ooz_out[i] = ooz
            acc[3] = acc[3] + oz_ref[i + 1] * plane
            acc[4] = acc[4] + ooz * plane

    off_diagonal(sh, lambda i: oz_ref[i + 1], k, 0, 3, put_ooz)

    def put_last(i, plane):
        acc[5] = acc[5] + ooz_ref[i] * plane

    by_elements(sh, lambda i: ooz_ref[i], k, put_last)
    moments_out(acc, red_ref)


def block_kernel(const_ref, red_in, base_ref, z_ref, oz_ref, ooz_ref, blk_ref):
    decay_f, rest_f, ff, shift_f = prony(const_ref, 0)
    c = galerkin(moments_in(red_in, 0, 6))
    ny = z_ref.shape[1]
    for i in range(L):
        delta = c[0] * z_ref[i] + c[1] * oz_ref[i] + c[2] * ooz_ref[i]
        blk_ref[i * ny : (i + 1) * ny] = base_ref[i] + delta
        for p in range(PRONY):
            at = L * (1 + p) + i
            blk_ref[at * ny : (at + 1) * ny] = base_ref[at] + rest_f[p] * delta
    blk_ref[4 * L * ny :] = jnp.broadcast_to(const_ref[HEAT + 1 : HEAT + 2], (8, blk_ref.shape[1]))


def halo_base(f, base_ref):
    sums = [
        f[0] * base_ref[L + i] + f[1] * base_ref[2 * L + i] + f[2] * base_ref[3 * L + i]
        for i in range(L)
    ]
    u = [base_ref[i] for i in range(L)]
    return u + [sums[0], sums[1]], [u[1], u[2], sums[2]]


def opening_kernel(const_ref, blk_ref, base_ref, even_out, odd_out):
    decay, rest, f, shift = prony(const_ref, COARSE)
    ny = even_out.shape[1]
    for at in range(4 * L):
        base_ref[at] = blk_ref[at * ny : (at + 1) * ny]
    lo, hi = halo_base(f, base_ref)
    hi = hi + hi[:2]
    send(holds(const_ref, SIDE, 0, even_out.shape[1:]), lo, hi, even_out, odd_out)


def chain_kernel(turn, count, opened, rounds, *refs):
    refs = list(refs)
    const_ref = refs.pop(0)
    if opened:
        base_in, even_ref, odd_ref = refs[:3]
        refs = refs[3:]
    else:
        red_in, base_in, z_in, oz_in, even_ref, odd_ref = refs[:6]
        refs = refs[6:]
    kel_ref, theta_ref, inv_ref, blk_ref = refs[:4]
    if rounds:
        outs, (red_ref, u_ref, au_ref, base_ref, z_ref, oz_ref) = refs[4 : 4 + rounds], refs[4 + rounds :]
    else:
        base_ref, z_ref, oz_ref, even_out, odd_out, red_ref, u_ref, au_ref = refs[4:]
    ny, nz = kel_ref.shape[1:]
    sh = Shifts(ny, nz)
    decay, rest, f, shift = prony(const_ref, COARSE)
    grow = f[0] * rest[0] + f[1] * rest[1] + f[2] * rest[2]
    heat = blk_ref[4 * L * ny : 4 * L * ny + 1]
    opening = holds(const_ref, SLICE, -turn % count, (ny, nz))
    fresh = holds(const_ref, SLICE, (1 - turn) % count, (ny, nz))
    side = holds(const_ref, SIDE, 0, (ny, nz))

    if not opened:
        c = galerkin(moments_in(red_in, 0, 4))

    def near(i, low_at, high_at):
        if i < 0:
            return below(side, even_ref, odd_ref, low_at)
        return above(side, even_ref, odd_ref, high_at)

    def delta(i):
        z = z_in[i + 1] if -1 <= i <= 4 else near(i, 3, 5)
        oz = oz_in[i] if 0 <= i <= 3 else near(i, i + 6, i + 2)
        return jnp.where(fresh, 0.0, c[0] * z + c[1] * oz)

    for i in range(-2, 6):
        base = base_in[i] if 0 <= i < L else near(i, i + 2, i - L)
        d = None if opened else delta(i)
        u_ref[i + 2] = base if opened else base + d
        if 0 <= i < L:
            h = [base_in[L * (1 + p) + i] for p in range(PRONY)]
            if not opened:
                h = [h[p] + rest[p] * d for p in range(PRONY)]
            total = f[0] * h[0] + f[1] * h[1] + f[2] * h[2]
            ui = u_ref[i + 2]
            base_ref[i] = jnp.where(opening, 0.0, ui) + blk_ref[i * ny : (i + 1) * ny]
            for p in range(PRONY):
                at = L * (1 + p) + i
                ahead = jnp.where(opening, 0.0, decay[p] * h[p] + rest[p] * ui)
                base_ref[at] = ahead + blk_ref[at * ny : (at + 1) * ny]
        elif -1 <= i < 5:
            total = near(i, 2, 3 + i - L)
            if not opened:
                total = total + grow * d
        if -1 <= i < 5:
            au_ref[i + 1] = heat * theta_ref[i + 2] + total

    zeros = jnp.zeros((ny, nz), jnp.float32)
    acc = [zeros] * 4

    def k(e):
        return kel_ref[e + 3]

    def put_z(i, plane):
        ui = u_ref[i + 2]
        s = au_ref[i + 1] + ui * (1.0 / PACES) - plane
        inv = inv_ref[i + 2]
        z = inv * s - ui
        z_ref[i + 1] = z
        if 0 <= i < L:
            acc[0] = acc[0] + z * (s - ui * (1.0 / inv))

    off_diagonal(sh, lambda i: u_ref[i + 2], k, -1, 4, put_z)

    def put_oz(i, plane):
        oz = inv_ref[i + 2] * plane
        oz_ref[i] = oz
        if 0 <= i < L:
            acc[1] = acc[1] + z_ref[i + 1] * plane
            acc[2] = acc[2] + oz * plane

    off_diagonal(sh, lambda i: z_ref[i + 1], k, 0, 3, put_oz)

    def put_last(i, plane):
        acc[3] = acc[3] + oz_ref[i] * plane

    by_elements(sh, lambda i: oz_ref[i], k, put_last)
    moments_out(acc, red_ref)

    if rounds:
        width = ny // rounds
        for i in range(L):
            fields = [base_ref[L * field + i] for field in range(1 + PRONY)]
            for at, field in enumerate(fields + [z_ref[i + 1], oz_ref[i]]):
                cuts = [field[q * width : (q + 1) * width] for q in range(rounds)]
                for r, out_ref in enumerate(outs):
                    ahead = [cuts[(v + r) % rounds] for v in range(rounds)]
                    out_ref[at, i] = chosen(const_ref, PART, ahead)
        return

    lo, hi = halo_base(f, base_ref)
    lo = lo + [z_ref[2 + 1], oz_ref[1], oz_ref[2]]
    hi = hi + [z_ref[1 + 1], oz_ref[1], oz_ref[2]]
    hi = hi + hi[:2]
    send(side, lo, hi, even_out, odd_out)


def closing_kernel(const_ref, red_in, *refs):
    parts, out_ref = refs[:-1], refs[-1]
    decay, rest, f, shift = prony(const_ref, COARSE)
    c = galerkin(moments_in(red_in, 0, 4))
    first = holds(const_ref, SLICE, 0, out_ref.shape[3:])
    count = len(parts)
    for k in range(count):
        for i in range(L):
            base_u, *base_h, z, oz = [
                chosen(const_ref, CHIP, [parts[(v - k) % count][at, i] for v in range(count)])
                for at in range(3 + PRONY)
            ]
            delta = jnp.where(first, 0.0, c[0] * z + c[1] * oz)
            out_ref[0, 0, k * L + i] = base_u + delta
            for p in range(PRONY):
                out_ref[0, 1 + p, k * L + i] = base_h[p] + rest[p] * delta


def spread_kernel(
    heat_ref, coef_ref, time_ref, rigid_ref, dilate_ref, place_ref, label_ref, values_ref,
    const_ref, *out_refs,
):
    fill_constants(heat_ref, coef_ref, time_ref, rigid_ref, dilate_ref, place_ref, const_ref)
    count = len(out_refs)
    for i in range(L):
        labels = [label_ref[k * L + i].astype(jnp.float32) + 1.0 for k in range(count)]
        fields = [labels]
        for field in range(1 + PRONY):
            fields.append([values_ref[0, field, k * L + i] for k in range(count)])
        for at, blocks in enumerate(fields):
            for r, out_ref in enumerate(out_refs):
                ahead = [blocks[(v - r) % count] for v in range(count)]
                out_ref[at, i] = chosen(const_ref, CHIP, ahead)


def join_kernel(const_ref, *refs):
    got_refs, (out_ref, past_ref) = refs[:-2], refs[-2:]
    decay, rest, f, shift = prony(const_ref, 0)
    count = len(got_refs)
    for q in range(count):
        for i in range(L):
            label, u, *h = [
                chosen(const_ref, PART, [got_refs[(q - v) % count][at, i] for v in range(count)])
                for at in range(2 + PRONY)
            ]
            fh = [f[p] * h[p] for p in range(PRONY)]
            out_ref[q, 0, i], out_ref[q, 1, i] = label, u
            out_ref[q, 2, i] = fh[0] + fh[1] + fh[2]
            out_ref[q, 3, i] = decay[0] * fh[0] + decay[1] * fh[1] + decay[2] * fh[2]
            for p in range(PRONY):
                past_ref[q, p, i] = h[p]


VMEM = pl.BlockSpec(memory_space=pltpu.VMEM)


def call(kernel, name, arrays, outs, scratch=()):
    f32 = jnp.float32
    return pl.pallas_call(
        kernel,
        name=name,
        out_shape=[jax.ShapeDtypeStruct(s, f32) for s in outs],
        in_specs=[VMEM] * len(arrays),
        out_specs=[VMEM] * len(outs),
        scratch_shapes=[pltpu.VMEM(s, f32) for s in scratch],
        compiler_params=pltpu.CompilerParams(vmem_limit_bytes=LIMIT),
    )(*arrays)


def on_device(
    segment_opening_values,
    cell_material_label,
    material_rigidity,
    dilation_mismatch,
    heat_swings_array,
    prony_coefficients,
    prony_decay_times,
):
    n_tm, n_gy = lax.axis_size("tm"), lax.axis_size("gy")
    line = lax.axis_size("gx") * n_gy
    nx, ny_part, nz = cell_material_label.shape
    ny = ny_part * n_gy
    assert nx == L * n_gy and n_gy == 4
    plane = (ny, nz)

    def device(position):
        row, rest = divmod(position, 2 * n_gy)
        x, core = divmod(rest, 2)
        return (2 * row + core) * n_gy + (x if row % 2 == 0 else n_gy - 1 - x)

    def deal(values, back=False):
        received = []
        for r, value in enumerate(values):
            perm = []
            for position in range(line):
                row, rest = divmod(position, 2 * n_gy)
                x, core = divmod(rest, 2)
                to = (2 * row + x // 2) * n_gy + (2 * (x % 2) + core + r) % n_gy
                perm.append((to, device(position)) if back else (device(position), to))
            received.append(lax.ppermute(value, LINE, sorted(perm)))
        return received

    def trade(even, odd):
        received = []
        for side, value in enumerate((even, odd)):
            pairs = [(device(p), device(p + 1)) for p in range(side, line - 1, 2)]
            both = pairs + [(b, a) for a, b in pairs]
            received.append(lax.ppermute(value, LINE, sorted(both)))
        return received

    def from_next_but_one(value):
        perm = [(device(p + 2), device(p)) for p in range(line - 2)]
        return lax.ppermute(value, LINE, sorted(perm))

    def exchanged(red):
        return lax.all_to_all(red, LINE, 0, 0, tiled=True)

    def ring(block):
        return lax.ppermute(block, "tm", [(s, (s - 1) % n_tm) for s in range(n_tm)])

    gx, gy = lax.axis_index("gx"), lax.axis_index("gy")
    core, flip = gx % 2, gx // 2 % 2
    x = jnp.where(flip == 0, gy, n_gy - 1 - gy)
    place = jnp.stack([lax.axis_index("tm"), core, 2 * (x % 2) + core, gy])
    place = place.astype(jnp.float32)[None]
    regions = material_rigidity.shape[0]
    tables = (prony_coefficients, prony_decay_times, material_rigidity, dilation_mismatch)

    const, *parts = call(
        spread_kernel,
        "spread",
        (
            heat_swings_array,
            *[table[None] for table in tables],
            place,
            cell_material_label,
            segment_opening_values,
        ),
        [(RIGID + 2 * regions, nz)] + [(2 + PRONY, L, ny_part, nz)] * n_gy,
    )
    own, past = call(
        join_kernel,
        "join",
        (const, *deal(parts, True)),
        [(n_gy, 4, L, ny_part, nz), (n_gy, PRONY, L, ny_part, nz)],
    )
    near, far = trade(own, own), from_next_but_one(own[:, 1:2, :1])

    red_shape = (line, 1, 128)
    (kel, theta, inv_f, inv_c, state, zf, ozf, oozf, zc, ozc, even, odd, far, red) = call(
        start_kernel,
        "start",
        (own, *near, far, const),
        [
            (9, *plane), (8, *plane), (8, *plane), (8, *plane), (18, *plane),
            (8, *plane), (6, *plane), (4, *plane), (L, *plane), (L, *plane),
            (6, *plane), (6, *plane), (3, *plane), red_shape,
        ],
        [(9, *plane), (8, *plane), (7, *plane)],
    )
    red = exchanged(red)
    near, far = trade(even, odd), from_next_but_one(far)
    base, z, oz, ooz, red = call(
        second_kernel,
        "second",
        (const, red, kel, theta, inv_f, state, past, zf, ozf, oozf, zc, ozc, *near, far),
        [(4 * L, *plane), (L, *plane), (L, *plane), (L, *plane), red_shape],
        [(10, *plane), (8, *plane), (6, *plane), (4, *plane), (8, *plane)],
    )
    red = exchanged(red)
    (block,) = call(
        block_kernel,
        "block",
        (const, red, base, z, oz, ooz),
        [(4 * L * ny + 8, nz)],
    )
    mine = block
    block = ring(block)
    base, even, odd = call(
        opening_kernel,
        "opening",
        (const, block),
        [(4 * L, *plane), (5, *plane), (5, *plane)],
    )
    past = (base,)
    for turn in range(2, n_tm + 1):
        if turn < n_tm:
            block, even = lax.optimization_barrier((block, even))
            block = ring(block)
        else:
            block = mine
        past = (*past, *trade(even, odd))
        last = turn == n_tm
        state = [(4 * L, *plane), (6, *plane), (4, *plane)]
        work = [(8, *plane), (6, *plane)]
        *outs, red = call(
            functools.partial(chain_kernel, turn, n_tm, turn == 2, n_gy if last else 0),
            f"chain{turn}",
            (const, *past, kel, theta, inv_c, block),
            [(3 + PRONY, L, ny_part, nz)] * n_gy + [red_shape]
            if last
            else [*state, (8, *plane), (8, *plane), red_shape],
            work + state if last else work,
        )
        if last:
            break
        base, z, oz, even, odd = outs
        past = (exchanged(red), base, z, oz)
    parts = deal(outs)
    (out,) = call(
        closing_kernel,
        "closing",
        (const, exchanged(red), *parts),
        [(1, 1 + PRONY, nx, ny_part, nz)],
    )
    return out


def solution(mesh):
    placed = (
        P("tm", None, "gx", "gy", None),
        P("gx", "gy", None),
        P(),
        P(),
        P("tm", None),
        P(),
        P(),
    )
    return jax.shard_map(
        on_device,
        mesh=mesh,
        in_specs=placed,
        out_specs=P("tm", None, "gx", "gy", None),
        check_vma=False,
    )
```

```python
import functools

import jax
import jax.numpy as jnp
from jax import lax
from jax.experimental import pallas as pl
from jax.experimental.pallas import tpu as pltpu
from jax.sharding import PartitionSpec as P

PACES = 2
SHARP = 3
LOOSE = 2
PRONY = 3
L = 3
LINE = ("gx", "gy")
LIMIT = 14 << 20


class Shifts:
    def __init__(self, ny, nz):
        self.ny, self.nz = ny, nz
        lane = lax.broadcasted_iota(jnp.int32, (ny, nz), 1)
        row = lax.broadcasted_iota(jnp.int32, (8, nz), 0)
        self.lane_first, self.lane_last = lane == 0, lane == nz - 1
        self.row_first, self.row_last = row == 0, row == 7

    def zup(self, v):
        return jnp.where(self.lane_last, 0.0, pltpu.roll(v, self.nz - 1, 1))

    def zdn(self, v):
        return jnp.where(self.lane_first, 0.0, pltpu.roll(v, 1, 1))

    def yup(self, v):
        v = pltpu.roll(v, self.ny - 1, 0)
        end = jnp.where(self.row_last, 0.0, v[self.ny - 8 :])
        return jnp.concatenate([v[: self.ny - 8], end], axis=0)

    def ydn(self, v):
        v = pltpu.roll(v, 1, 0)
        return jnp.concatenate([jnp.where(self.row_first, 0.0, v[:8]), v[8:]], axis=0)


def off_diagonal(sh, v, k, low, high, put):
    def spread(plane):
        up = sh.zup(plane)
        side, side_up = sh.yup(plane), sh.yup(up)
        return plane, up, side, side_up, plane + up, side + side_up

    near = spread(v(low - 1))
    carry = None
    for e in range(low - 1, high + 1):
        far = spread(v(e + 1))
        a, a_up, b, b_up, a_sum, b_sum = near
        c, c_up, d, d_up, c_sum, d_sum = far
        one_up, two_up = b_up + c_up, a_up + d_up
        one, two = b + c, a + d
        kk = k(e)
        if e >= low:
            e00, f00 = kk * (d_sum + one_up), kk * (d_sum + one)
            e01, f01 = kk * (c_sum + two_up), kk * (c_sum + two)
            e10, e11, f10, f11 = carry
            put(e, (e00 + e10) + sh.ydn(e01 + e11) + sh.zdn((f00 + f10) + sh.ydn(f01 + f11)))
        if e < high:
            carry = (
                kk * (b_sum + two_up),
                kk * (a_sum + one_up),
                kk * (b_sum + two),
                kk * (a_sum + one),
            )
        near = far


COARSE, HEAT, SLICE, SIDE, PART, CHIP, RIGID = 10, 20, 22, 23, 24, 25, 26


def fill_constants(heat_ref, coef_ref, time_ref, rigid_ref, dilate_ref, place_ref, const_ref):
    def put(at, value):
        const_ref[at : at + 1] = jnp.broadcast_to(value, (1, 128))

    def entry(ref, i):
        return jnp.broadcast_to(ref[0:1, i : i + 1], (1, 128))

    for first, dt in ((0, 1.0), (COARSE, 1.0 * PACES)):
        total = jnp.full((1, 128), 1.0 / dt, jnp.float32)
        for p in range(PRONY):
            decay = jnp.exp(-dt / entry(time_ref, p))
            f = entry(coef_ref, p) * decay
            put(first + p, decay)
            put(first + 3 + p, 1.0 - decay)
            put(first + 6 + p, f)
            total = total + f
        put(first + 9, total)
    put(HEAT, entry(heat_ref, 0))
    put(HEAT + 1, entry(heat_ref, PACES - 1))
    for i in range(4):
        put(SLICE + i, entry(place_ref, i))
    regions = rigid_ref.shape[1]
    for i in range(regions):
        put(RIGID + i, entry(rigid_ref, i))
        put(RIGID + regions + i, entry(dilate_ref, i))


def prony(const_ref, first):
    rows = [const_ref[first + i : first + i + 1] for i in range(10)]
    return rows[:3], rows[3:6], rows[6:9], rows[9]


def holds(const_ref, row, value, shape):
    return jnp.broadcast_to(const_ref[row : row + 1], shape) == float(value)


def moments_out(values, red_ref):
    lane = lax.broadcasted_iota(jnp.int32, (1, 128), 1)
    packed = jnp.zeros((1, 128), jnp.float32)
    for at, field in enumerate(values):
        total = jnp.sum(jnp.sum(field, axis=0, keepdims=True), axis=1, keepdims=True)
        packed = jnp.where(lane == at, total, packed)
    red_ref[...] = jnp.broadcast_to(packed[None], red_ref.shape)


def moments_in(red_ref, first, count):
    total = jnp.sum(red_ref[...], axis=0)
    lane = lax.broadcasted_iota(jnp.int32, (1, 128), 1)
    return [
        jnp.broadcast_to(
            jnp.sum(jnp.where(lane == first + i, total, 0.0), axis=1, keepdims=True), (1, 128)
        )
        for i in range(count)
    ]


def galerkin(nu):
    m = len(nu) // 2
    mu = [nu[i] + nu[i + 1] for i in range(2 * m - 1)]
    rows = [[mu[i + j] for j in range(m)] + [nu[i]] for i in range(m)]
    for i in range(m):
        for r in range(i + 1, m):
            factor = rows[r][i] / rows[i][i]
            for j in range(i + 1, m + 1):
                rows[r][j] = rows[r][j] - factor * rows[i][j]
    c = [None] * m
    for i in reversed(range(m)):
        acc = rows[i][m]
        for j in range(i + 1, m):
            acc = acc - rows[i][j] * c[j]
        c[i] = acc / rows[i][i]
    return c


def send(even_place, lo, hi, even_out, odd_out):
    for at, (low, high) in enumerate(zip(lo, hi)):
        even_out[at] = jnp.where(even_place, high, low)
        odd_out[at] = jnp.where(even_place, low, high)


def below(even_place, even_ref, odd_ref, at):
    return jnp.where(even_place, odd_ref[at], even_ref[at])


def above(even_place, even_ref, odd_ref, at):
    return jnp.where(even_place, even_ref[at], odd_ref[at])


def chosen(const_ref, row, values):
    value = values[-1]
    for v in range(len(values) - 1):
        value = jnp.where(holds(const_ref, row, v, value.shape), values[v], value)
    return value


def start_kernel(
    own_ref, even_ref, odd_ref, far_ref, const_ref,
    kel_ref, theta_ref, inv_f_ref, inv_c_ref, state_ref,
    zf_ref, ozf_ref, oozf_ref, zc_ref, ozc_ref,
    even_out, odd_out, far_out, red_ref,
    kal_ref, au_ref, w_ref,
):
    ny, nz = kel_ref.shape[1:]
    sh = Shifts(ny, nz)
    chunks = own_ref.shape[0]
    side = holds(const_ref, SIDE, 0, (ny, nz))
    side_part = holds(const_ref, SIDE, 0, (ny // chunks, nz))

    def raw(field, i):
        if i < 0:
            parts = [below(side_part, even_ref, odd_ref, (c, field, i + L)) for c in range(chunks)]
        elif i < L:
            parts = [own_ref[c, field, i] for c in range(chunks)]
        elif i < 2 * L:
            parts = [above(side_part, even_ref, odd_ref, (c, field, i - L)) for c in range(chunks)]
        else:
            parts = [far_ref[c, 0, 0] for c in range(chunks)]
        return jnp.concatenate(parts, axis=0)

    regions = (const_ref.shape[0] - RIGID) // 2
    table = [const_ref[RIGID + i : RIGID + i + 1] for i in range(2 * regions)]

    for e in range(-3, 6):
        label = raw(0, e)
        stiff = jnp.zeros((ny, nz), jnp.float32)
        load = jnp.zeros((ny, nz), jnp.float32)
        for region in range(regions):
            here = label == (region + 1.0)
            stiff = jnp.where(here, table[region], stiff)
            load = jnp.where(here, table[regions + region], load)
        kel_ref[e + 3] = stiff * (-1.0 / 12.0)
        kal_ref[e + 3] = 0.25 * (stiff * load)

    heat = [const_ref[HEAT + i : HEAT + i + 1] for i in range(2)]
    shift_f, shift_c = prony(const_ref, 0)[3], prony(const_ref, COARSE)[3]

    for i in range(-2, 6):
        ksum = kel_ref[i + 2] + kel_ref[i + 3]
        ksum = ksum + sh.ydn(ksum)
        ksum = ksum + sh.zdn(ksum)
        diag = -4.0 * ksum
        asum = kal_ref[i + 2] + kal_ref[i + 3]
        asum = asum + sh.ydn(asum)
        theta_ref[i + 2] = sh.zdn(asum) - asum
        inside = raw(0, i) > 0.5
        inv_f_ref[i + 2] = jnp.where(inside, 1.0 / (diag + shift_f), 0.0)
        inv_c_ref[i + 2] = jnp.where(inside, 1.0 / (diag + shift_c), 0.0)

    for i in range(-3, 7):
        state_ref[i + 3] = raw(1, i)

    def k(e):
        return kel_ref[e + 3]

    def put_au(i, plane):
        au_ref[i + 2] = plane

    off_diagonal(sh, lambda i: state_ref[i + 3], k, -2, 5, put_au)

    zeros = jnp.zeros((ny, nz), jnp.float32)
    acc = [zeros] * 10
    for i in range(-2, 6):
        later = raw(3, i)
        state_ref[10 + i + 2] = later
        ui = state_ref[i + 3]
        load = heat[0] * theta_ref[i + 2] + raw(2, i)
        s = load + ui - au_ref[i + 2]
        z = inv_f_ref[i + 2] * s - ui
        zf_ref[i + 2] = z
        if 0 <= i < L:
            acc[0] = acc[0] + z * (s - ui * (1.0 / inv_f_ref[i + 2]))
        if i < 5:
            load = heat[1] * theta_ref[i + 2] + later
            s = load + ui * (1.0 / PACES) - au_ref[i + 2]
            z = inv_c_ref[i + 2] * s - ui
            w_ref[i + 2] = z
            if 0 <= i < L:
                zc_ref[i] = z
                acc[6] = acc[6] + z * (s - ui * (1.0 / inv_c_ref[i + 2]))

    def put_oz(i, plane):
        oz = inv_f_ref[i + 2] * plane
        ozf_ref[i + 1] = oz
        if 0 <= i < L:
            acc[1] = acc[1] + zf_ref[i + 2] * plane
            acc[2] = acc[2] + oz * plane

    off_diagonal(sh, lambda i: zf_ref[i + 2], k, -1, 4, put_oz)

    def put_ooz(i, plane):
        ooz = inv_f_ref[i + 2] * plane
        oozf_ref[i] = ooz
        if i < L:
            acc[3] = acc[3] + ozf_ref[i + 1] * plane
            acc[4] = acc[4] + ooz * plane

    off_diagonal(sh, lambda i: ozf_ref[i + 1], k, 0, 3, put_ooz)

    def put_last(i, plane):
        acc[5] = acc[5] + oozf_ref[i] * plane

    by_elements(sh, lambda i: oozf_ref[i], k, put_last)

    def put_ozc(i, plane):
        oz = inv_c_ref[i + 2] * plane
        au_ref[i + 2] = oz
        if 0 <= i < L:
            ozc_ref[i] = oz
            acc[7] = acc[7] + w_ref[i + 2] * plane
            acc[8] = acc[8] + oz * plane

    off_diagonal(sh, lambda i: w_ref[i + 2], k, 0, 3, put_ozc)

    def put_lastc(i, plane):
        acc[9] = acc[9] + au_ref[i + 2] * plane

    by_elements(sh, lambda i: au_ref[i + 2], k, put_lastc)
    moments_out(acc, red_ref)

    hi = [zf_ref[2], ozf_ref[1], ozf_ref[2], oozf_ref[0], oozf_ref[1], oozf_ref[2]]
    lo = [ozf_ref[3], oozf_ref[1], oozf_ref[2]]
    send(side, lo + lo, hi, even_out, odd_out)
    far_out[0], far_out[1], far_out[2] = zf_ref[2], ozf_ref[1], oozf_ref[0]


def by_elements(sh, v, k, put):
    none = jnp.zeros((sh.ny, sh.nz), jnp.float32)

    def nodes(i):
        return v(i) if 0 <= i <= L else none

    def elements(e):
        return k(e) if 0 <= e < L else none

    off_diagonal(sh, nodes, elements, 0, L, put)


def second_kernel(
    const_ref, red_in, kel_ref, theta_ref, inv_f_ref, state_ref, own_ref,
    zf_ref, ozf_ref, oozf_ref, zc_ref, ozc_ref,
    even_ref, odd_ref, far_ref,
    base_ref, z_out, oz_out, ooz_out, red_ref,
    u_ref, z_ref, oz_ref, ooz_ref, au_ref,
):
    ny, nz = kel_ref.shape[1:]
    sh = Shifts(ny, nz)
    chunks = own_ref.shape[0]
    decay_f, rest_f, ff, shift_f = prony(const_ref, 0)
    decay_c, rest_c, fc, shift_c = prony(const_ref, COARSE)
    c = galerkin(moments_in(red_in, 0, 6))
    b = galerkin(moments_in(red_in, 6, 4))
    side = holds(const_ref, SIDE, 0, (ny, nz))
    heat = const_ref[HEAT + 1 : HEAT + 2]

    def basis(i, at, ref, low, high, up, down):
        if i == 6:
            return far_ref[at]
        if i < low:
            return below(side, even_ref, odd_ref, up + i + L)
        if i > high:
            return above(side, even_ref, odd_ref, down + i - high - 1)
        return ref[i - low]

    for i in range(-3, 7):
        z = basis(i, 0, zf_ref, -2, 5, 0, None)
        oz = basis(i, 1, ozf_ref, -1, 4, 1, 0)
        ooz = basis(i, 2, oozf_ref, 0, 3, 3, 1)
        u_ref[i + 3] = state_ref[i + 3] + c[0] * z + c[1] * oz + c[2] * ooz

    def k(e):
        return kel_ref[e + 3]

    def put_au(i, plane):
        au_ref[i + 2] = plane

    off_diagonal(sh, lambda i: u_ref[i + 3], k, -2, 5, put_au)

    grow = ff[0] * rest_f[0] + ff[1] * rest_f[1] + ff[2] * rest_f[2]
    zeros = jnp.zeros((ny, nz), jnp.float32)
    acc = [zeros] * 6
    weight = jnp.where(holds(const_ref, SLICE, 0, (1, nz)), 0.0, 1.0)
    for i in range(-2, 6):
        ui = u_ref[i + 3]
        s = heat * theta_ref[i + 2] + state_ref[10 + i + 2] + (grow + 1.0) * ui
        s = s - au_ref[i + 2]
        z = inv_f_ref[i + 2] * s - ui
        z_ref[i + 2] = z
        if 0 <= i < L:
            z_out[i] = z
            acc[0] = acc[0] + z * (s - ui * (1.0 / inv_f_ref[i + 2]))

    for i in range(L):
        u1 = u_ref[i + 3]
        g = state_ref[i + 3] + b[0] * zc_ref[i] + b[1] * ozc_ref[i]
        base_ref[i] = u1 - weight * g
        for p in range(PRONY):
            h = jnp.concatenate([own_ref[q, p, i] for q in range(chunks)], axis=0)
            h1 = decay_f[p] * h + rest_f[p] * u1
            gh = decay_c[p] * h + rest_c[p] * g
            base_ref[L * (1 + p) + i] = decay_f[p] * h1 + rest_f[p] * u1 - weight * gh

    def put_oz(i, plane):
        oz = inv_f_ref[i + 2] * plane
        oz_ref[i + 1] = oz
        if 0 <= i < L:
            oz_out[i] = oz
            acc[1] = acc[1] + z_ref[i + 2] * plane
            acc[2] = acc[2] + oz * plane

    off_diagonal(sh, lambda i: z_ref[i + 2], k, -1, 4, put_oz)

    def put_ooz(i, plane):
        ooz = inv_f_ref[i + 2] * plane
        ooz_ref[i] = ooz
        if i < L:
            ooz_out[i] = ooz
            acc[3] = acc[3] + oz_ref[i + 1] * plane
            acc[4] = acc[4] + ooz * plane

    off_diagonal(sh, lambda i: oz_ref[i + 1], k, 0, 3, put_ooz)

    def put_last(i, plane):
        acc[5] = acc[5] + ooz_ref[i] * plane

    by_elements(sh, lambda i: ooz_ref[i], k, put_last)
    moments_out(acc, red_ref)


def block_kernel(const_ref, red_in, base_ref, z_ref, oz_ref, ooz_ref, blk_ref):
    decay_f, rest_f, ff, shift_f = prony(const_ref, 0)
    c = galerkin(moments_in(red_in, 0, 6))
    ny = z_ref.shape[1]
    for i in range(L):
        delta = c[0] * z_ref[i] + c[1] * oz_ref[i] + c[2] * ooz_ref[i]
        blk_ref[i * ny : (i + 1) * ny] = base_ref[i] + delta
        for p in range(PRONY):
            at = L * (1 + p) + i
            blk_ref[at * ny : (at + 1) * ny] = base_ref[at] + rest_f[p] * delta
    blk_ref[4 * L * ny :] = jnp.broadcast_to(const_ref[HEAT + 1 : HEAT + 2], (8, blk_ref.shape[1]))


def halo_base(f, base_ref):
    sums = [
        f[0] * base_ref[L + i] + f[1] * base_ref[2 * L + i] + f[2] * base_ref[3 * L + i]
        for i in range(L)
    ]
    u = [base_ref[i] for i in range(L)]
    return u + [sums[0], sums[1]], [u[1], u[2], sums[2]]


def opening_kernel(const_ref, blk_ref, base_ref, even_out, odd_out):
    decay, rest, f, shift = prony(const_ref, COARSE)
    ny = even_out.shape[1]
    for at in range(4 * L):
        base_ref[at] = blk_ref[at * ny : (at + 1) * ny]
    lo, hi = halo_base(f, base_ref)
    hi = hi + hi[:2]
    send(holds(const_ref, SIDE, 0, even_out.shape[1:]), lo, hi, even_out, odd_out)


def chain_kernel(turn, count, opened, rounds, *refs):
    refs = list(refs)
    const_ref = refs.pop(0)
    if opened:
        base_in, even_ref, odd_ref = refs[:3]
        refs = refs[3:]
    else:
        red_in, base_in, z_in, oz_in, even_ref, odd_ref = refs[:6]
        refs = refs[6:]
    kel_ref, theta_ref, inv_ref, blk_ref = refs[:4]
    if rounds:
        outs, (red_ref, u_ref, au_ref, base_ref, z_ref, oz_ref) = refs[4 : 4 + rounds], refs[4 + rounds :]
    else:
        base_ref, z_ref, oz_ref, even_out, odd_out, red_ref, u_ref, au_ref = refs[4:]
    ny, nz = kel_ref.shape[1:]
    sh = Shifts(ny, nz)
    decay, rest, f, shift = prony(const_ref, COARSE)
    grow = f[0] * rest[0] + f[1] * rest[1] + f[2] * rest[2]
    heat = blk_ref[4 * L * ny : 4 * L * ny + 1]
    opening = holds(const_ref, SLICE, -turn % count, (ny, nz))
    fresh = holds(const_ref, SLICE, (1 - turn) % count, (ny, nz))
    side = holds(const_ref, SIDE, 0, (ny, nz))

    if not opened:
        c = galerkin(moments_in(red_in, 0, 4))

    def near(i, low_at, high_at):
        if i < 0:
            return below(side, even_ref, odd_ref, low_at)
        return above(side, even_ref, odd_ref, high_at)

    def delta(i):
        z = z_in[i + 1] if -1 <= i <= 4 else near(i, 3, 5)
        oz = oz_in[i] if 0 <= i <= 3 else near(i, i + 6, i + 2)
        return jnp.where(fresh, 0.0, c[0] * z + c[1] * oz)

    for i in range(-2, 6):
        base = base_in[i] if 0 <= i < L else near(i, i + 2, i - L)
        d = None if opened else delta(i)
        u_ref[i + 2] = base if opened else base + d
        if 0 <= i < L:
            h = [base_in[L * (1 + p) + i] for p in range(PRONY)]
            if not opened:
                h = [h[p] + rest[p] * d for p in range(PRONY)]
            total = f[0] * h[0] + f[1] * h[1] + f[2] * h[2]
            ui = u_ref[i + 2]
            base_ref[i] = jnp.where(opening, 0.0, ui) + blk_ref[i * ny : (i + 1) * ny]
            for p in range(PRONY):
                at = L * (1 + p) + i
                ahead = jnp.where(opening, 0.0, decay[p] * h[p] + rest[p] * ui)
                base_ref[at] = ahead + blk_ref[at * ny : (at + 1) * ny]
        elif -1 <= i < 5:
            total = near(i, 2, 3 + i - L)
            if not opened:
                total = total + grow * d
        if -1 <= i < 5:
            au_ref[i + 1] = heat * theta_ref[i + 2] + total

    zeros = jnp.zeros((ny, nz), jnp.float32)
    acc = [zeros] * 4

    def k(e):
        return kel_ref[e + 3]

    def put_z(i, plane):
        ui = u_ref[i + 2]
        s = au_ref[i + 1] + ui * (1.0 / PACES) - plane
        inv = inv_ref[i + 2]
        z = inv * s - ui
        z_ref[i + 1] = z
        if 0 <= i < L:
            acc[0] = acc[0] + z * (s - ui * (1.0 / inv))

    off_diagonal(sh, lambda i: u_ref[i + 2], k, -1, 4, put_z)

    def put_oz(i, plane):
        oz = inv_ref[i + 2] * plane
        oz_ref[i] = oz
        if 0 <= i < L:
            acc[1] = acc[1] + z_ref[i + 1] * plane
            acc[2] = acc[2] + oz * plane

    off_diagonal(sh, lambda i: z_ref[i + 1], k, 0, 3, put_oz)

    def put_last(i, plane):
        acc[3] = acc[3] + oz_ref[i] * plane

    by_elements(sh, lambda i: oz_ref[i], k, put_last)
    moments_out(acc, red_ref)

    if rounds:
        width = ny // rounds
        for i in range(L):
            fields = [base_ref[L * field + i] for field in range(1 + PRONY)]
            for at, field in enumerate(fields + [z_ref[i + 1], oz_ref[i]]):
                cuts = [field[q * width : (q + 1) * width] for q in range(rounds)]
                for r, out_ref in enumerate(outs):
                    ahead = [cuts[(v + r) % rounds] for v in range(rounds)]
                    out_ref[at, i] = chosen(const_ref, PART, ahead)
        return

    lo, hi = halo_base(f, base_ref)
    lo = lo + [z_ref[2 + 1], oz_ref[1], oz_ref[2]]
    hi = hi + [z_ref[1 + 1], oz_ref[1], oz_ref[2]]
    hi = hi + hi[:2]
    send(side, lo, hi, even_out, odd_out)


def closing_kernel(const_ref, red_in, *refs):
    parts, out_ref = refs[:-1], refs[-1]
    decay, rest, f, shift = prony(const_ref, COARSE)
    c = galerkin(moments_in(red_in, 0, 4))
    first = holds(const_ref, SLICE, 0, out_ref.shape[3:])
    count = len(parts)
    for k in range(count):
        for i in range(L):
            base_u, *base_h, z, oz = [
                chosen(const_ref, CHIP, [parts[(v - k) % count][at, i] for v in range(count)])
                for at in range(3 + PRONY)
            ]
            delta = jnp.where(first, 0.0, c[0] * z + c[1] * oz)
            out_ref[0, 0, k * L + i] = base_u + delta
            for p in range(PRONY):
                out_ref[0, 1 + p, k * L + i] = base_h[p] + rest[p] * delta


def spread_kernel(
    heat_ref, coef_ref, time_ref, rigid_ref, dilate_ref, place_ref, label_ref, values_ref,
    const_ref, *out_refs,
):
    fill_constants(heat_ref, coef_ref, time_ref, rigid_ref, dilate_ref, place_ref, const_ref)
    count = len(out_refs)
    for i in range(L):
        labels = [label_ref[k * L + i].astype(jnp.float32) + 1.0 for k in range(count)]
        fields = [labels]
        for field in range(1 + PRONY):
            fields.append([values_ref[0, field, k * L + i] for k in range(count)])
        for at, blocks in enumerate(fields):
            for r, out_ref in enumerate(out_refs):
                ahead = [blocks[(v - r) % count] for v in range(count)]
                out_ref[at, i] = chosen(const_ref, CHIP, ahead)


def join_kernel(const_ref, *refs):
    got_refs, (out_ref, past_ref) = refs[:-2], refs[-2:]
    decay, rest, f, shift = prony(const_ref, 0)
    count = len(got_refs)
    for q in range(count):
        for i in range(L):
            label, u, *h = [
                chosen(const_ref, PART, [got_refs[(q - v) % count][at, i] for v in range(count)])
                for at in range(2 + PRONY)
            ]
            fh = [f[p] * h[p] for p in range(PRONY)]
            out_ref[q, 0, i], out_ref[q, 1, i] = label, u
            out_ref[q, 2, i] = fh[0] + fh[1] + fh[2]
            out_ref[q, 3, i] = decay[0] * fh[0] + decay[1] * fh[1] + decay[2] * fh[2]
            for p in range(PRONY):
                past_ref[q, p, i] = h[p]


VMEM = pl.BlockSpec(memory_space=pltpu.VMEM)


def call(kernel, name, arrays, outs, scratch=()):
    f32 = jnp.float32
    return pl.pallas_call(
        kernel,
        name=name,
        out_shape=[jax.ShapeDtypeStruct(s, f32) for s in outs],
        in_specs=[VMEM] * len(arrays),
        out_specs=[VMEM] * len(outs),
        scratch_shapes=[pltpu.VMEM(s, f32) for s in scratch],
        compiler_params=pltpu.CompilerParams(vmem_limit_bytes=LIMIT),
    )(*arrays)


def on_device(
    segment_opening_values,
    cell_material_label,
    material_rigidity,
    dilation_mismatch,
    heat_swings_array,
    prony_coefficients,
    prony_decay_times,
):
    n_tm, n_gy = lax.axis_size("tm"), lax.axis_size("gy")
    line = lax.axis_size("gx") * n_gy
    nx, ny_part, nz = cell_material_label.shape
    ny = ny_part * n_gy
    assert nx == L * n_gy and n_gy == 4
    plane = (ny, nz)

    def device(position):
        row, rest = divmod(position, 2 * n_gy)
        x, core = divmod(rest, 2)
        return (2 * row + core) * n_gy + (x if row % 2 == 0 else n_gy - 1 - x)

    def deal(values, back=False):
        received = []
        for r, value in enumerate(values):
            perm = []
            for position in range(line):
                row, rest = divmod(position, 2 * n_gy)
                x, core = divmod(rest, 2)
                to = (2 * row + x // 2) * n_gy + (2 * (x % 2) + core + r) % n_gy
                perm.append((to, device(position)) if back else (device(position), to))
            received.append(lax.ppermute(value, LINE, sorted(perm)))
        return received

    def trade(even, odd):
        received = []
        for side, value in enumerate((even, odd)):
            pairs = [(device(p), device(p + 1)) for p in range(side, line - 1, 2)]
            both = pairs + [(b, a) for a, b in pairs]
            received.append(lax.ppermute(value, LINE, sorted(both)))
        return received

    def from_next_but_one(value):
        perm = [(device(p + 2), device(p)) for p in range(line - 2)]
        return lax.ppermute(value, LINE, sorted(perm))

    def exchanged(red):
        return lax.all_to_all(red, LINE, 0, 0, tiled=True)

    def ring(block):
        return lax.ppermute(block, "tm", [(s, (s - 1) % n_tm) for s in range(n_tm)])

    gx, gy = lax.axis_index("gx"), lax.axis_index("gy")
    core, flip = gx % 2, gx // 2 % 2
    x = jnp.where(flip == 0, gy, n_gy - 1 - gy)
    place = jnp.stack([lax.axis_index("tm"), core, 2 * (x % 2) + core, gy])
    place = place.astype(jnp.float32)[None]
    regions = material_rigidity.shape[0]
    tables = (prony_coefficients, prony_decay_times, material_rigidity, dilation_mismatch)

    const, *parts = call(
        spread_kernel,
        "spread",
        (
            heat_swings_array,
            *[table[None] for table in tables],
            place,
            cell_material_label,
            segment_opening_values,
        ),
        [(RIGID + 2 * regions, nz)] + [(2 + PRONY, L, ny_part, nz)] * n_gy,
    )
    own, past = call(
        join_kernel,
        "join",
        (const, *deal(parts, True)),
        [(n_gy, 4, L, ny_part, nz), (n_gy, PRONY, L, ny_part, nz)],
    )
    near, far = trade(own, own), from_next_but_one(own[:, 1:2, :1])

    red_shape = (line, 1, 128)
    (kel, theta, inv_f, inv_c, state, zf, ozf, oozf, zc, ozc, even, odd, far, red) = call(
        start_kernel,
        "start",
        (own, *near, far, const),
        [
            (9, *plane), (8, *plane), (8, *plane), (8, *plane), (18, *plane),
            (8, *plane), (6, *plane), (4, *plane), (L, *plane), (L, *plane),
            (6, *plane), (6, *plane), (3, *plane), red_shape,
        ],
        [(9, *plane), (8, *plane), (7, *plane)],
    )
    red = exchanged(red)
    near, far = trade(even, odd), from_next_but_one(far)
    base, z, oz, ooz, red = call(
        second_kernel,
        "second",
        (const, red, kel, theta, inv_f, state, past, zf, ozf, oozf, zc, ozc, *near, far),
        [(4 * L, *plane), (L, *plane), (L, *plane), (L, *plane), red_shape],
        [(10, *plane), (8, *plane), (6, *plane), (4, *plane), (8, *plane)],
    )
    red = exchanged(red)
    (block,) = call(
        block_kernel,
        "block",
        (const, red, base, z, oz, ooz),
        [(4 * L * ny + 8, nz)],
    )
    mine = block
    block = ring(block)
    base, even, odd = call(
        opening_kernel,
        "opening",
        (const, block),
        [(4 * L, *plane), (5, *plane), (5, *plane)],
    )
    past = (base,)
    for turn in range(2, n_tm + 1):
        if turn < n_tm:
            block, even = lax.optimization_barrier((block, even))
            block = ring(block)
        else:
            block = mine
        past = (*past, *trade(even, odd))
        last = turn == n_tm
        state = [(4 * L, *plane), (6, *plane), (4, *plane)]
        work = [(8, *plane), (6, *plane)]
        *outs, red = call(
            functools.partial(chain_kernel, turn, n_tm, turn == 2, n_gy if last else 0),
            f"chain{turn}",
            (const, *past, kel, theta, inv_c, block),
            [(3 + PRONY, L, ny_part, nz)] * n_gy + [red_shape]
            if last
            else [*state, (8, *plane), (8, *plane), red_shape],
            work + state if last else work,
        )
        if last:
            break
        base, z, oz, even, odd = outs
        past = (exchanged(red), base, z, oz)
    parts = deal(outs)
    (out,) = call(
        closing_kernel,
        "closing",
        (const, exchanged(red), *parts),
        [(1, 1 + PRONY, nx, ny_part, nz)],
    )
    return out


def solution(mesh):
    placed = (
        P("tm", None, "gx", "gy", None),
        P("gx", "gy", None),
        P(),
        P(),
        P("tm", None),
        P(),
        P(),
    )
    return jax.shard_map(
        on_device,
        mesh=mesh,
        in_specs=placed,
        out_specs=P("tm", None, "gx", "gy", None),
        check_vma=False,
    )
```
